32 devices in a mesh: dp: 16 (over z, y, core), tensor: 2 (over x).
Axes of the slice: x: 2, y: 2, z: 4, core: 2. Of those that a mesh axis runs over, the one named last changes fastest.
Arguments:
- tokens: bfloat16 [8192, 1024], P(('dp', 'tensor')), may hold values from -6 to 6
- cotangent: bfloat16 [8192, 1024], P(('dp', 'tensor')), may hold values from -6 to 6
- deal_slot: int32 [8192], P(('dp', 'tensor')), may hold values from 0 to 255, as said below
- back_slot: int32 [8192], P(('dp', 'tensor')), may hold values from 0 to 255, as said below
- lengths: int32 [16, 4], P('dp'), may hold values from 1 to 256, 512 in all within a row
- time_step: int32 [1], replicated, may hold values from 0 to 4999
- time_table: bfloat16 [5000, 1024], P(None, 'dp'), may hold values from -3 to 3
- w_qkv: bfloat16 [2, 3, 1024, 1024], P(None, None, 'dp', 'tensor'), may hold values from -0.1875 to 0.1875
- b_qv: float32 [2, 2, 1024], P(None, None, 'tensor'), may hold values from -2 to 2
- w_out: bfloat16 [2, 1024, 1024], P(None, 'tensor', 'dp'), may hold values from -1.5 to 1.5
- out_bias: float32 [2, 2, 1024], replicated, may hold values from -2 to 2
- ln_gain: float32 [2, 2, 1024], replicated, may hold values from 0.5 to 1.5
- ln_shift: float32 [2, 2, 1024], replicated, may hold values from -2 to 2
- w_ff1: bfloat16 [2, 1024, 4096], P(None, 'dp', 'tensor'), may hold values from -0.1875 to 0.1875
- b_ff1: float32 [2, 4096], P(None, 'tensor'), may hold values from -2 to 2
- w_ff2: bfloat16 [2, 4096, 1024], P(None, 'tensor', 'dp'), may hold values from -0.09375 to 0.09375
Outputs:
- encoded: bfloat16 [8192, 1024], P(('dp', 'tensor'))
- grad_tokens: bfloat16 [8192, 1024], P(('dp', 'tensor'))
- grad_time_row: float32 [1024], replicated
- grad_w_qkv: float32 [2, 3, 1024, 1024], P(None, None, 'dp', 'tensor')
- grad_b_qv: float32 [2, 2, 1024], P(None, None, 'tensor')
- grad_w_out: float32 [2, 1024, 1024], P(None, 'tensor', 'dp')
- grad_out_bias: float32 [2, 2, 1024], replicated
- grad_ln_gain: float32 [2, 2, 1024], replicated
- grad_ln_shift: float32 [2, 2, 1024], replicated
- grad_w_ff1: float32 [2, 1024, 4096], P(None, 'dp', 'tensor')
- grad_b_ff1: float32 [2, 4096], P(None, 'tensor')
- grad_w_ff2: float32 [2, 4096, 1024], P(None, 'tensor', 'dp')
The draws below stay inside these ranges and needn't reach their ends.
Inputs may be any that keep to these rules, and one draw needn't show every extreme that they name: `deal_slot`: the 256 entries of each device form a permutation of 0 to 255. `back_slot`: on each device's 256 entries, the inverse of deal_slot. Each group's 4 lengths sum to 512; the longest is exactly 256.
All inputs are finite; a program needn't handle non-finite values.
Results may differ from the reference program's by a relative error of at most 0.038.
Values may be sent and summed in bfloat16 or wider, within the bound.
No kernel may reach another device: no remote copies, remote signals or barrier semaphores. Data moves between devices by JAX's collectives and lax.ppermute only.
A program may use at most 192 MiB of HBM per device.

```python
import math
import jax
import jax.numpy as jnp
import numpy as np
from jax import lax

D = 1024
HEADS = 16
FF = 4096
LAYERS = 2
TOK_DEV = 256
SEQS = 4
TSTEPS = 5000
GROUPS = 16
TOK_GROUP = 512
TOKENS = 8192
BLK = 16
MAXLEN = 256
N_DP = 16
N_TENSOR = 2


def slot_order(key):
    devices = TOKENS // TOK_DEV
    ordered = jnp.broadcast_to(jnp.arange(TOK_DEV, dtype=jnp.int32)[None, :], (devices, TOK_DEV))
    return jax.random.permutation(jax.random.fold_in(key, 17), ordered, axis=1, independent=True)


def draw_deal_slot(key, part):
    return slot_order(key).reshape(TOKENS).astype(jnp.int32)


def draw_back_slot(key, part):
    return jnp.argsort(slot_order(key), axis=1, stable=True).astype(jnp.int32).reshape(TOKENS)


def block_scale(key, shape, cuts, smallest, top_value):
    def one(dim, blocks):
        heights = jax.random.uniform(jax.random.fold_in(jax.random.fold_in(key, 6), dim), (blocks,), jnp.float32, smallest / len(cuts), top_value / len(cuts))
        return jnp.repeat(jnp.exp(heights), shape[dim] // blocks).reshape((-1,) + (1,) * (len(shape) - dim - 1))

    gain = one(*cuts[0])
    for cut in cuts[1:]:
        gain = gain * one(*cut)
    return gain


def profile(number_of, total, most, skew):
    loads = [(1 << 20) // math.isqrt(standing ** skew) + 1 for standing in range(2, number_of + 1)]
    rest, counts = total - most - (number_of - 1), [1] * (number_of - 1)
    while rest > 0:
        free = [i for i in range(number_of - 1) if counts[i] < most]
        whole, budget = sum([loads[i] for i in free]), rest
        for i in free:
            extra = min(most - counts[i], max(1, budget * loads[i] // whole), rest)
            counts[i] = counts[i] + extra
            rest = rest - extra
    return np.array([most] + counts)


def ragged(key, amount, total, most, lean):
    if amount == 2:
        one = jax.random.randint(key, (), max(1, total - most), min(most, total - 1) + 1)
        return jnp.stack([one, total - one])
    tallies = jnp.asarray(profile(amount, total, most, lean), jnp.int32)
    pairs = (amount - 1) // 2
    donor, sink = tallies[1:1 + 2 * pairs:2], tallies[2:2 + 2 * pairs:2]
    slack = jnp.minimum(donor - 1, most - sink)
    moved = jax.random.randint(jax.random.fold_in(key, 1), (pairs,), 0, 1 << 20) % (slack + 1)
    tallies = tallies.at[1:1 + 2 * pairs:2].set(donor - moved).at[2:2 + 2 * pairs:2].set(sink + moved)
    return tallies[jax.random.permutation(jax.random.fold_in(key, 2), amount)]


def noise(key, extent, scale, bound, split=(), kind=jnp.bfloat16):
    array = scale * jax.random.normal(key, extent, jnp.float32)
    if split:
        array = array * block_scale(key, extent, split, -0.22, 0.18)
    return jnp.clip(array, -bound, bound).astype(kind)


def setup_inputs(seed: int = 0) -> dict:
    seeds = jax.random.split(jax.random.key(seed), 17)
    tokens = noise(seeds[0], (TOKENS, D), 1.0, 6.0, ((0, 32),))
    cotangent = noise(seeds[1], (TOKENS, D), 1.0, 6.0, ((0, 32),))
    deal_slot = draw_deal_slot(jax.random.fold_in(seeds[16], 71), 0)
    back_slot = draw_back_slot(jax.random.fold_in(seeds[16], 71), 0)
    lengths = jax.vmap(lambda own: ragged(own, SEQS, TOK_GROUP, MAXLEN, 2))(jax.random.split(seeds[4], GROUPS)).reshape((GROUPS, SEQS)).astype(jnp.int32)
    time_step = jax.random.randint(seeds[5], (1,), 0, TSTEPS).astype(jnp.int32)
    time_table = noise(seeds[6], (TSTEPS, D), 0.5, 3.0, ((1, 16),))
    w_qkv = noise(seeds[7], (LAYERS, 3, D, D), D ** -0.5, 0.1875, ((2, 16), (3, 2)))
    b_qv = noise(seeds[8], (LAYERS, 2, D), 0.3, 2.0, ((2, 2),), jnp.float32)
    w_out = noise(seeds[9], (LAYERS, D, D), (D // 64) ** -0.5, 1.5, ((1, 2), (2, 16)))
    out_bias = noise(seeds[10], (LAYERS, 2, D), 0.3, 2.0, (), jnp.float32)
    ln_gain = jnp.clip(1.0 + 0.1 * jax.random.normal(seeds[11], (LAYERS, 2, D), jnp.float32), 0.5, 1.5)
    ln_shift = noise(seeds[12], (LAYERS, 2, D), 0.3, 2.0, (), jnp.float32)
    w_ff1 = noise(seeds[13], (LAYERS, D, FF), D ** -0.5, 0.1875, ((1, 16), (2, 2)))
    b_ff1 = noise(seeds[14], (LAYERS, FF), 0.3, 2.0, ((1, 2),), jnp.float32)
    w_ff2 = noise(seeds[15], (LAYERS, FF, D), FF ** -0.5, 0.09375, ((1, 2), (2, 16)))
    return {"tokens": tokens, "cotangent": cotangent, "deal_slot": deal_slot, "back_slot": back_slot, "lengths": lengths, "time_step": time_step, "time_table": time_table, "w_qkv": w_qkv, "b_qv": b_qv, "w_out": w_out, "out_bias": out_bias, "ln_gain": ln_gain, "ln_shift": ln_shift, "w_ff1": w_ff1, "b_ff1": b_ff1, "w_ff2": w_ff2}


HIGHEST = lax.Precision.HIGHEST

@jax.custom_vjp
def low(v):
    return lax.optimization_barrier(v.astype(jnp.bfloat16)).astype(jnp.float32)

@jax.custom_vjp
def low_back(v):
    return v

def low_keep(v):
    return (low(v), None)

def low_pass(kept, grad):
    return (grad,)

def back_keep(v):
    return (v, None)

def back_low(kept, grad):
    return (low(grad),)
low.defvjp(low_keep, low_pass)
low_back.defvjp(back_keep, back_low)

def layer_norm(summed, scaling, offset_vec):
    centre = lax.optimization_barrier(jnp.mean(summed, axis=-1, keepdims=True))
    spread = summed - centre
    variance = lax.optimization_barrier(jnp.mean(spread * spread, axis=-1, keepdims=True))
    return spread * lax.rsqrt(variance + 1e-05) * scaling + offset_vec

def matmul_high(left, right):
    return jnp.dot(left, right, precision=HIGHEST)

def segment_ids(group_lengths):
    seq_ends = jnp.cumsum(group_lengths)
    positions = jnp.arange(TOK_GROUP, dtype=jnp.int32)
    return lax.optimization_barrier(jnp.sum((positions[:, None] >= seq_ends[None, :]).astype(jnp.int32), axis=1))

def attend_block(query_block, segment_block, key_rows, values, segment):
    score_scale = 1.0 / math.sqrt(D // HEADS)
    scores = jnp.einsum('qhe,khe->hqk', query_block, key_rows, precision=HIGHEST) * score_scale
    scores = low_back(scores)
    allowed = segment_block[:, None] == segment[None, :]
    scores = jnp.where(allowed[None], scores, -1e+30)
    probabilities = low(jax.nn.softmax(scores, axis=-1))
    return jnp.einsum('hqk,khe->qhe', probabilities, values, precision=HIGHEST)

def group_forward(stream, segment, params):
    w_qkv, b_qv, w_out, out_bias, ln_gain, ln_shift, w_ff1, b_ff1, w_ff2 = params
    head_size = D // HEADS
    group_rows = stream.shape[0]
    block_rows = min(512, group_rows)
    blocks = group_rows // block_rows
    checked = jax.checkpoint(attend_block)
    for layer_num in range(LAYERS):
        stream_low = low(stream)
        projected = jnp.einsum('rd,cde->rce', stream_low, w_qkv[layer_num], precision=HIGHEST)
        queries = low_back(low(projected[:, 0] + b_qv[layer_num, 0]))
        key_rows = low_back(low(projected[:, 1]))
        values = low_back(low(projected[:, 2] + b_qv[layer_num, 1]))
        key_heads = key_rows.reshape(group_rows, HEADS, head_size)
        value_heads = values.reshape(group_rows, HEADS, head_size)
        mixture = lax.map(lambda pair: checked(pair[0], pair[1], key_heads, value_heads, segment), (queries.reshape(blocks, block_rows, HEADS, head_size), segment.reshape(blocks, block_rows)))
        mixture = low_back(low(mixture.reshape(group_rows, D)))
        attended = low_back(matmul_high(mixture, w_out[layer_num]))
        middle = stream + attended + out_bias[layer_num, 0]
        normed = layer_norm(middle, ln_gain[layer_num, 0], ln_shift[layer_num, 0])
        hidden_pre = low_back(matmul_high(low(normed), w_ff1[layer_num]) + b_ff1[layer_num])
        activated = low(jax.nn.gelu(hidden_pre, approximate=False))
        branch_out = low_back(matmul_high(activated, w_ff2[layer_num]))
        stream = layer_norm(normed + branch_out + out_bias[layer_num, 1], ln_gain[layer_num, 1], ln_shift[layer_num, 1])
    return stream

def forward_all(owned, time_row, params, segments):
    checked = jax.checkpoint(group_forward)

    def per_group(pair):
        return checked(pair[0] + time_row, pair[1], params)
    return lax.map(per_group, (owned, segments))

def to_owner(natural, back_slot):
    arranged = natural.reshape(N_DP, N_TENSOR, TOK_DEV, D)
    index_rows = back_slot.reshape(N_DP, N_TENSOR, TOK_DEV, 1).astype(jnp.int32)
    slots = jnp.take_along_axis(arranged, index_rows, axis=2)
    slots = slots.reshape(N_DP, N_TENSOR, N_DP, BLK, D).transpose(2, 1, 0, 3, 4)
    return slots.reshape(N_DP, TOK_GROUP, D)

def from_owner(owned, deal_slot):
    slots = owned.reshape(N_DP, N_TENSOR, N_DP, BLK, D).transpose(2, 1, 0, 3, 4)
    slots = slots.reshape(N_DP, N_TENSOR, TOK_DEV, D)
    index_rows = deal_slot.reshape(N_DP, N_TENSOR, TOK_DEV, 1).astype(jnp.int32)
    return jnp.take_along_axis(slots, index_rows, axis=2).reshape(TOKENS, D)

def reference(tokens, cotangent, deal_slot, back_slot, lengths, time_step, time_table, w_qkv, b_qv, w_out, out_bias, ln_gain, ln_shift, w_ff1, b_ff1, w_ff2):
    owned = to_owner(tokens.astype(jnp.float32), back_slot)
    upstream = to_owner(cotangent.astype(jnp.float32), back_slot)
    segments = jax.vmap(segment_ids)(lengths)
    time_row = lax.dynamic_index_in_dim(time_table, time_step[0], 0, keepdims=False).astype(jnp.float32)
    params = (w_qkv.astype(jnp.float32), b_qv.astype(jnp.float32), w_out.astype(jnp.float32), out_bias.astype(jnp.float32), ln_gain.astype(jnp.float32), ln_shift.astype(jnp.float32), w_ff1.astype(jnp.float32), b_ff1.astype(jnp.float32), w_ff2.astype(jnp.float32))

    def whole(own, row, *plist):
        return forward_all(own, row, plist, segments)
    result, pullback = jax.vjp(whole, owned, time_row, *params)
    grads = pullback(upstream)
    encoded = from_owner(result.astype(jnp.bfloat16), deal_slot)
    grad_tokens = from_owner(grads[0].astype(jnp.bfloat16), deal_slot)
    return (encoded, grad_tokens, grads[1], grads[2], grads[3], grads[4], grads[5], grads[6], grads[7], grads[8], grads[9], grads[10])
```

```python
import math

import jax
import jax.numpy as jnp
import numpy as np
from jax import lax
from jax.sharding import PartitionSpec as P

D = 1024
HEADS = 16
FF = 4096
HEAD = D // HEADS
F32 = jnp.float32
BF16 = jnp.bfloat16


def layer_norm(summed, scaling, offset_vec):
    centre = jnp.mean(summed, axis=-1, keepdims=True)
    spread = summed - centre
    variance = jnp.mean(spread * spread, axis=-1, keepdims=True)
    return spread * lax.rsqrt(variance + 1e-05) * scaling + offset_vec


def gelu_slope(hidden_pre):
    normal_cdf = 0.5 * (1.0 + lax.erf(hidden_pre * 0.7071067811865476))
    return normal_cdf + hidden_pre * jnp.exp(-0.5 * hidden_pre * hidden_pre) * 0.3989422804014327


def dot(left, right):
    return jnp.dot(left, right, preferred_element_type=F32)


def contract_rows(left, right):
    return lax.dot_general(left, right, (((0,), (0,)), ((), ())), preferred_element_type=F32)


def times_transposed(left, right):
    return lax.dot_general(left, right, (((1,), (1,)), ((), ())), preferred_element_type=F32)


class Wires:
    def __init__(self, dp_size, tensor_size):
        self.dp_size, self.tensor_size = dp_size, tensor_size
        chips = dp_size // 2
        self.chips = chips
        order = list(range(0, chips, 2)) + list(range(chips - 1, 0, -2))
        place = {chip: spot for spot, chip in enumerate(order)}
        ring, sources = [], np.zeros((dp_size, chips), np.int32)
        for device in range(dp_size):
            chip, core = divmod(device, 2)
            way = 1 if core == 0 else -1
            ring.append((device, 2 * order[(place[chip] + way) % chips] + core))
            sources[device] = [order[(place[chip] - way * s) % chips] for s in range(chips)]
        self.ring = ring
        self.swap = [(d, d ^ 1) for d in range(dp_size)]
        dp_index = lax.axis_index("dp")
        self.core = dp_index % 2
        self.source = lax.dynamic_index_in_dim(jnp.asarray(sources), dp_index, 0, keepdims=False)

    def hop(self, array):
        return lax.ppermute(array, "dp", self.ring)

    def partner(self, array):
        return lax.ppermute(array, "dp", self.swap)

    def across(self, array):
        return lax.ppermute(array, "tensor", [(0, 1), (1, 0)])

    def half(self, array, axis, mine):
        width = array.shape[axis] // 2
        index = self.core if mine else 1 - self.core
        return lax.dynamic_slice_in_dim(array, index * width, width, axis)

    def ordered(self, mine, other, axis):
        return jnp.where(
            self.core == 0,
            jnp.concatenate([mine, other], axis),
            jnp.concatenate([other, mine], axis),
        )

    def gather_halves(self, shard, cuts, extra=None):
        mine, other = shard
        rows = mine.shape[0]
        got = self.partner(other)
        piece = self.ordered(mine, got, 0)
        chip_rows = 2 * rows
        if extra is not None:
            tail = jnp.zeros((8, piece.shape[1]), piece.dtype)
            pair = self.ordered(extra, self.partner(extra), 0)
            tail = lax.dynamic_update_slice(tail, pair[None, :], (0, 0))
            piece = jnp.concatenate([piece, tail], 0)
        wholes = [jnp.zeros((self.chips * chip_rows, b - a), piece.dtype) for a, b in cuts]
        vector = None if extra is None else jnp.zeros((self.chips, chip_rows), piece.dtype)
        for step in range(self.chips):
            if step:
                piece = self.hop(piece)
            chip = self.source[step]
            wholes = [
                lax.dynamic_update_slice(whole, piece[:chip_rows, a:b], (chip * chip_rows, 0))
                for whole, (a, b) in zip(wholes, cuts)
            ]
            if extra is not None:
                vector = lax.dynamic_update_slice(
                    vector, piece[chip_rows : chip_rows + 1, :chip_rows], (chip, 0)
                )
        halves = [(whole, self.partner(whole)) for whole in wholes]
        return halves if extra is None else (halves, vector.reshape(-1))

    def reduce_halves(self, sums):
        chip_rows = sums[0].shape[0] // self.chips
        widths = [part.shape[1] for part in sums]

        def portion(step):
            start = self.source[(step + 1) % self.chips] * chip_rows
            return [lax.dynamic_slice_in_dim(part, start, chip_rows, 0) for part in sums]

        total = jnp.concatenate(portion(0), 1)
        for step in range(1, self.chips):
            came = self.hop(total.astype(BF16)).astype(F32)
            total = came + jnp.concatenate(portion(step), 1).astype(F32)
        mine = self.half(total, 0, True)
        other = self.partner(self.half(total, 0, False).astype(BF16)).astype(F32)
        edges = np.cumsum([0] + widths)
        return [(mine[:, a:b], other[:, a:b]) for a, b in zip(edges[:-1], edges[1:])]

    def rows_in(self, local_rows):
        if self.tensor_size == 2:
            return [local_rows, self.across(local_rows)]
        return [lax.all_gather(local_rows, "tensor", axis=0, tiled=True)]

    def rows_out(self, term, count):
        if self.tensor_size == 2:
            came = self.across(term(1).astype(BF16))
            return term(0) + came.astype(F32)
        return lax.psum_scatter(
            term(0).astype(BF16), "tensor", scatter_dimension=0, tiled=True
        ).astype(F32)

    def butterfly(self, array, axis, size):
        bit = 1
        while bit < size:
            array = array + lax.ppermute(array, axis, [(i, i ^ bit) for i in range(size)])
            bit *= 2
        return array


def owner_swap(rows):
    return lax.all_to_all(rows, "dp", split_axis=0, concat_axis=0, tiled=True)


def masked_scores(query_block, key_rows, segment_block, segment, score_scale):
    scores = (
        jnp.einsum("qhe,khe->hqk", query_block, key_rows, preferred_element_type=F32) * score_scale
    )
    allowed = segment_block[:, None] == segment[None, :]
    return jnp.where(allowed[None], scores, -1e30)


def attend_forward(queries, key_rows, values, segment, score_scale):
    group_rows, head_count, head_size = queries.shape
    block_rows = min(512, group_rows)
    blocks = group_rows // block_rows

    def block_step(query_block, segment_block):
        scores = masked_scores(query_block, key_rows, segment_block, segment, score_scale)
        highest = jnp.max(scores, axis=-1, keepdims=True)
        weights = jnp.exp(scores - highest)
        summed = jnp.sum(weights, axis=-1, keepdims=True)
        probabilities = (weights / summed).astype(BF16)
        mixture = jnp.einsum("hqk,khe->qhe", probabilities, values, preferred_element_type=F32)
        return (mixture.astype(BF16), (highest + jnp.log(summed))[..., 0])

    if blocks == 1:
        mixture, log_total = block_step(queries, segment)
        log_total = log_total[None]
    else:
        _, (mixture, log_total) = lax.scan(
            lambda running, inputs: (running, block_step(*inputs)),
            None,
            (
                queries.reshape(blocks, block_rows, head_count, head_size),
                segment.reshape(blocks, block_rows),
            ),
        )
    return (mixture.reshape(group_rows, head_count * head_size), log_total)


def attend_backward(queries, key_rows, values, segment, log_total, grad_mixture, score_scale):
    group_rows, head_count, head_size = queries.shape
    block_rows = min(512, group_rows)
    blocks = group_rows // block_rows

    def block_step(query_block, segment_block, total_block, grad_block):
        scores = masked_scores(query_block, key_rows, segment_block, segment, score_scale)
        probabilities = jnp.exp(scores - total_block[..., None])
        grad_probs = jnp.einsum("qhe,khe->hqk", grad_block, values, preferred_element_type=F32)
        centre = jnp.sum(probabilities * grad_probs, axis=-1, keepdims=True)
        grad_scores = (probabilities * (grad_probs - centre)).astype(BF16)
        grad_query = (
            jnp.einsum("hqk,khe->qhe", grad_scores, key_rows, preferred_element_type=F32)
            * score_scale
        )
        grad_keys = (
            jnp.einsum("hqk,qhe->khe", grad_scores, query_block, preferred_element_type=F32)
            * score_scale
        )
        grad_values = jnp.einsum(
            "hqk,qhe->khe", probabilities.astype(BF16), grad_block, preferred_element_type=F32
        )
        return grad_query, grad_keys, grad_values

    if blocks == 1:
        grad_query, grad_keys, grad_values = block_step(
            queries, segment, log_total[0], grad_mixture
        )
    else:

        def step(running, inputs):
            grad_query, more_keys, more_values = block_step(*inputs)
            return (running[0] + more_keys, running[1] + more_values), grad_query

        zeros = jnp.zeros(key_rows.shape, F32)
        (grad_keys, grad_values), grad_query = lax.scan(
            step,
            (zeros, zeros),
            (
                queries.reshape(blocks, block_rows, head_count, head_size),
                segment.reshape(blocks, block_rows),
                log_total,
                grad_mixture.reshape(blocks, block_rows, head_count, head_size),
            ),
        )
    wide = (group_rows, head_count * head_size)
    return [
        part.astype(BF16).reshape(wide) for part in (grad_query, grad_keys, grad_values)
    ]


def join(blocks):
    return blocks[0] if len(blocks) == 1 else jnp.concatenate(blocks, 0)


def body(
    tokens,
    cotangent,
    deal_slot,
    back_slot,
    lengths,
    time_step,
    time_table,
    w_qkv,
    b_qv,
    w_out,
    out_bias,
    ln_gain,
    ln_shift,
    w_ff1,
    b_ff1,
    w_ff2,
):
    wires = Wires(lax.axis_size("dp"), lax.axis_size("tensor"))
    rows_dev = tokens.shape[0]
    group_rows = rows_dev * wires.tensor_size
    tensor_index = lax.axis_index("tensor")
    score_scale = 1.0 / math.sqrt(HEAD)
    layer_total = w_qkv.shape[0]
    inner = w_qkv.shape[3] // 2
    hidden = w_ff1.shape[2] // 2
    heads = inner // HEAD
    both = (True, False)

    time_piece = lax.dynamic_index_in_dim(time_table, time_step[0], 0, keepdims=False)
    weights = []
    for layer in range(layer_total):
        attn, feed = [], []
        for mine in both:
            qkv = wires.half(w_qkv[layer], 2, mine)
            attn.append(
                jnp.concatenate(
                    [qkv[0], qkv[1], qkv[2], wires.half(w_out[layer], 0, mine).T], axis=1
                )
            )
            feed.append(
                jnp.concatenate(
                    [wires.half(w_ff1[layer], 1, mine), wires.half(w_ff2[layer], 0, mine).T], axis=1
                )
            )
        attn_cuts = ((0, 3 * inner), (3 * inner, 4 * inner))
        feed_cuts = ((0, hidden), (hidden, 2 * hidden))
        if layer == 0:
            (qkv_w, out_w), time_row = wires.gather_halves(attn, attn_cuts, time_piece)
        else:
            qkv_w, out_w = wires.gather_halves(attn, attn_cuts)
        first_w, second_w = wires.gather_halves(feed, feed_cuts)
        weights.append((qkv_w, out_w, first_w, second_w))

    own_rows = owner_swap(jnp.take(tokens, back_slot, axis=0))
    upstream_rows = owner_swap(jnp.take(cotangent, back_slot, axis=0))
    seq_ends = jnp.cumsum(lengths[0])
    positions = jnp.arange(group_rows, dtype=jnp.int32)
    if wires.tensor_size == 2:
        positions = (positions + tensor_index * rows_dev) % group_rows
    segment = jnp.sum((positions[:, None] >= seq_ends[None, :]).astype(jnp.int32), axis=1)

    def split_heads(array):
        return array.reshape(group_rows, heads, HEAD)

    stream = own_rows.astype(F32) + time_row.astype(F32)
    saved = []
    for layer in range(layer_total):
        qkv_w, out_w, first_w, second_w = weights[layer]
        input_rows = join(wires.rows_in(stream.astype(BF16)))
        attention = []
        for half, mine in enumerate(both):
            bias_q = wires.half(b_qv[layer, 0], 0, mine)
            bias_v = wires.half(b_qv[layer, 1], 0, mine)
            projected = dot(input_rows, qkv_w[half])
            queries = split_heads((projected[:, :inner] + bias_q).astype(BF16))
            key_rows = split_heads(projected[:, inner : 2 * inner].astype(BF16))
            values = split_heads((projected[:, 2 * inner :] + bias_v).astype(BF16))
            head_out, log_total = attend_forward(queries, key_rows, values, segment, score_scale)
            attention.append((queries, key_rows, values, head_out, log_total))

        def attended_term(block):
            rows = group_rows if wires.tensor_size != 2 else rows_dev
            return sum(
                times_transposed(part[3][block * rows : (block + 1) * rows], out_w[half])
                for half, part in enumerate(attention)
            )

        middle = stream + wires.rows_out(attended_term, rows_dev) + out_bias[layer, 0]
        normed = layer_norm(middle, ln_gain[layer, 0], ln_shift[layer, 0])
        normed_blocks = wires.rows_in(normed.astype(BF16))
        hidden_blocks, act_blocks = [], []
        for block in normed_blocks:
            pre = [
                dot(block, first_w[half]) + wires.half(b_ff1[layer], 0, mine)
                for half, mine in enumerate(both)
            ]
            hidden_blocks.append(pre)
            act_blocks.append([jax.nn.gelu(f, approximate=False).astype(BF16) for f in pre])

        def feed_term(block):
            return sum(times_transposed(act_blocks[block][half], second_w[half]) for half in (0, 1))

        second_sum = normed + wires.rows_out(feed_term, rows_dev) + out_bias[layer, 1]
        saved.append(
            (input_rows, attention, middle, normed_blocks, hidden_blocks, act_blocks, second_sum)
        )
        stream = layer_norm(second_sum, ln_gain[layer, 1], ln_shift[layer, 1])
    returned_out = owner_swap(stream.astype(BF16))
    encoded = jnp.take(returned_out, deal_slot, axis=0)

    def both_cores(term):
        came = wires.partner(term(1).astype(BF16))
        return (term(0) + came.astype(F32)).astype(BF16)

    gradient = upstream_rows.astype(F32)
    matrix_grads = [None] * layer_total
    vector_grads = [None] * layer_total
    for layer in reversed(range(layer_total)):
        qkv_w, out_w, first_w, second_w = weights[layer]
        input_rows, attention, middle, normed_blocks, hidden_blocks, act_blocks, second_sum = saved[
            layer
        ]
        _, pull_second = jax.vjp(layer_norm, second_sum, ln_gain[layer, 1], ln_shift[layer, 1])
        grad_second, gain_second, shift_second = pull_second(gradient)
        branch_blocks = wires.rows_in(grad_second.astype(BF16))
        grad_pre = [
            [
                (dot(branch, second_w[half]) * gelu_slope(pre[half])).astype(BF16)
                for half in (0, 1)
            ]
            for branch, pre in zip(branch_blocks, hidden_blocks)
        ]

        def hidden_term(block):
            return sum(times_transposed(grad_pre[block][half], first_w[half]) for half in (0, 1))

        grad_normed = grad_second + wires.rows_out(hidden_term, rows_dev)
        grad_first_w = both_cores(
            lambda half: contract_rows(join(normed_blocks), join([b[half] for b in grad_pre]))
        )
        grad_second_w = both_cores(
            lambda half: contract_rows(join(branch_blocks), join([b[half] for b in act_blocks]))
        )
        feed_grads = wires.reduce_halves([grad_first_w, grad_second_w])
        grad_hidden_bias = [
            sum(jnp.sum(b[half].astype(F32), axis=0) for b in grad_pre) for half in (0, 1)
        ]
        _, pull_first = jax.vjp(layer_norm, middle, ln_gain[layer, 0], ln_shift[layer, 0])
        grad_middle, gain_first, shift_first = pull_first(grad_normed)
        attend_all = join(wires.rows_in(grad_middle.astype(BF16)))
        grad_qkv = []
        for half in (0, 1):
            queries, key_rows, values, head_out, log_total = attention[half]
            grad_heads = dot(attend_all, out_w[half]).astype(BF16)
            grad_qkv.append(
                attend_backward(
                    queries,
                    key_rows,
                    values,
                    segment,
                    log_total,
                    split_heads(grad_heads),
                    score_scale,
                )
            )
        grad_wide = [jnp.concatenate(parts, axis=1) for parts in grad_qkv]

        def proj_term(block):
            rows = group_rows if wires.tensor_size != 2 else rows_dev
            return sum(
                times_transposed(grad_wide[half][block * rows : (block + 1) * rows], qkv_w[half])
                for half in (0, 1)
            )

        gradient = grad_middle + wires.rows_out(proj_term, rows_dev)
        grad_proj = both_cores(lambda half: contract_rows(attend_all, attention[half][3]))
        grad_query_w = both_cores(lambda half: contract_rows(input_rows, grad_wide[half]))
        attn_grads = wires.reduce_halves([grad_query_w, grad_proj])
        qkv_pair, out_pair = attn_grads
        first_pair, second_pair = feed_grads
        rows = qkv_pair[0].shape[0]
        matrix_grads[layer] = (
            wires.ordered(
                *(part.reshape(rows, 3, inner).transpose(1, 0, 2) for part in qkv_pair), 2
            ),
            wires.ordered(out_pair[0].T, out_pair[1].T, 0),
            wires.ordered(first_pair[0], first_pair[1], 1),
            wires.ordered(second_pair[0].T, second_pair[1].T, 0),
        )
        qkv_sums = [jnp.sum(part.astype(F32), axis=0).reshape(3, inner) for part in grad_wide]
        vector_grads[layer] = (
            wires.ordered(qkv_sums[0], qkv_sums[1], 1)[jnp.array([0, 2])],
            wires.ordered(grad_hidden_bias[0], grad_hidden_bias[1], 0),
            jnp.stack([jnp.sum(grad_middle, axis=0), jnp.sum(grad_second, axis=0)]),
            jnp.stack([gain_first, gain_second]),
            jnp.stack([shift_first, shift_second]),
        )
    returned_grad = owner_swap(gradient.astype(BF16))
    grad_tokens = jnp.take(returned_grad, deal_slot, axis=0)
    time_grad = jnp.sum(gradient, axis=0)
    local = [jnp.stack([part[i] for part in vector_grads]) for i in range(5)]
    flat = jnp.concatenate([part.reshape(-1) for part in local[:2] + [time_grad] + local[2:]])
    flat = wires.butterfly(flat, "dp", wires.dp_size)
    border = local[0].size + local[1].size
    shared = wires.butterfly(flat[border:], "tensor", wires.tensor_size)
    grad_b_qv = flat[: local[0].size].reshape(local[0].shape)
    grad_b_ff1 = flat[local[0].size : border].reshape(local[1].shape)
    time_grad = shared[:D]
    rest = shared[D:].reshape(3, layer_total, 2, D)
    return (
        encoded,
        grad_tokens,
        time_grad,
        jnp.stack([part[0] for part in matrix_grads]),
        grad_b_qv,
        jnp.stack([part[1] for part in matrix_grads]),
        rest[0],
        rest[1],
        rest[2],
        jnp.stack([part[2] for part in matrix_grads]),
        grad_b_ff1,
        jnp.stack([part[3] for part in matrix_grads]),
    )


def solution(mesh):
    return jax.shard_map(
        body,
        mesh=mesh,
        in_specs=(
            P(("dp", "tensor"), None),
            P(("dp", "tensor"), None),
            P(("dp", "tensor")),
            P(("dp", "tensor")),
            P("dp", None),
            P(),
            P(None, "dp"),
            P(None, None, "dp", "tensor"),
            P(None, None, "tensor"),
            P(None, "tensor", "dp"),
            P(),
            P(),
            P(),
            P(None, "dp", "tensor"),
            P(None, "tensor"),
            P(None, "tensor", "dp"),
        ),
        out_specs=(
            P(("dp", "tensor"), None),
            P(("dp", "tensor"), None),
            P(),
            P(None, None, "dp", "tensor"),
            P(None, None, "tensor"),
            P(None, "tensor", "dp"),
            P(),
            P(),
            P(),
            P(None, "dp", "tensor"),
            P(None, "tensor"),
            P(None, "tensor", "dp"),
        ),
        check_vma=False,
    )
```

```python
import math

import jax
import jax.numpy as jnp
import numpy as np
from jax import lax
from jax.experimental import pallas as pl
from jax.experimental.pallas import tpu as pltpu
from jax.sharding import PartitionSpec as P

D = 1024
HEADS = 16
FF = 4096
HEAD = D // HEADS
F32 = jnp.float32
BF16 = jnp.bfloat16


def layer_norm(summed, scaling, offset_vec):
    centre = jnp.mean(summed, axis=-1, keepdims=True)
    spread = summed - centre
    variance = jnp.mean(spread * spread, axis=-1, keepdims=True)
    return spread * lax.rsqrt(variance + 1e-05) * scaling + offset_vec


def dot(left, right):
    return jnp.dot(left, right, preferred_element_type=F32)


def contract_rows(left, right):
    return lax.dot_general(left, right, (((0,), (0,)), ((), ())), preferred_element_type=F32)


def times_transposed(left, right):
    return lax.dot_general(left, right, (((1,), (1,)), ((), ())), preferred_element_type=F32)


class Wires:
    def __init__(self, dp_size, tensor_size):
        self.dp_size, self.tensor_size = dp_size, tensor_size
        chips = dp_size // 2
        self.chips = chips
        order = list(range(0, chips, 2)) + list(range(chips - 1, 0, -2))
        place = {chip: spot for spot, chip in enumerate(order)}
        ring, sources = [], np.zeros((dp_size, chips), np.int32)
        for device in range(dp_size):
            chip, core = divmod(device, 2)
            way = 1 if core == 0 else -1
            ring.append((device, 2 * order[(place[chip] + way) % chips] + core))
            sources[device] = [order[(place[chip] - way * s) % chips] for s in range(chips)]
        self.ring = ring
        self.swap = [(d, d ^ 1) for d in range(dp_size)]
        dp_index = lax.axis_index("dp")
        self.core = dp_index % 2
        self.source = lax.dynamic_index_in_dim(jnp.asarray(sources), dp_index, 0, keepdims=False)

    def hop(self, array):
        return lax.ppermute(array, "dp", self.ring)

    def partner(self, array):
        return lax.ppermute(array, "dp", self.swap)

    def across(self, array):
        return lax.ppermute(array, "tensor", [(0, 1), (1, 0)])

    def half(self, array, axis, mine):
        width = array.shape[axis] // 2
        index = self.core if mine else 1 - self.core
        return lax.dynamic_slice_in_dim(array, index * width, width, axis)

    def ordered(self, mine, other, axis):
        return jnp.where(
            self.core == 0,
            jnp.concatenate([mine, other], axis),
            jnp.concatenate([other, mine], axis),
        )

    def gather_halves(self, shard, cuts, extra=None):
        mine, other = shard
        got = self.partner(other)
        piece = self.ordered(mine, got, 0)
        chip_rows = piece.shape[0]
        if extra is not None:
            tail = jnp.zeros((8, piece.shape[1]), piece.dtype)
            pair = self.ordered(extra, self.partner(extra), 0)
            tail = lax.dynamic_update_slice(tail, pair[None, :], (0, 0))
            piece = jnp.concatenate([piece, tail], 0)
        piece = yield piece
        pieces = [piece]
        for _ in range(1, self.chips):
            piece = yield self.hop(piece)
            pieces.append(piece)
        wholes, vector = place_pieces(self.source, pieces, chip_rows, cuts)
        halves = [(whole, self.partner(whole)) for whole in wholes]
        if extra is None:
            return halves
        return halves, vector[:, 0, :chip_rows].reshape(-1)

    def reduce_halves(self, terms):
        came = [self.partner(term(1).astype(BF16)) for term in terms]
        came = yield came
        sums = [(term(0) + part.astype(F32)).astype(BF16) for term, part in zip(terms, came)]
        chip_rows = sums[0].shape[0] // self.chips
        widths = [part.shape[1] for part in sums]

        def portion(step):
            start = self.source[(step + 1) % self.chips] * chip_rows
            return [lax.dynamic_slice_in_dim(part, start, chip_rows, 0) for part in sums]

        total = jnp.concatenate(portion(0), 1)
        for step in range(1, self.chips):
            came = yield self.hop(total.astype(BF16))
            total = came.astype(F32) + jnp.concatenate(portion(step), 1).astype(F32)
        mine = self.half(total, 0, True)
        other = self.partner(self.half(total, 0, False).astype(BF16)).astype(F32)
        edges = np.cumsum([0] + widths)
        return [(mine[:, a:b], other[:, a:b]) for a, b in zip(edges[:-1], edges[1:])]

    def rows_in(self, local_rows, beside):
        beside = beside or Beside(0.0)
        local_rows = beside.tick(local_rows)
        if self.tensor_size == 2:
            return [local_rows, beside.tick(self.across(local_rows))]
        return [beside.tick(lax.all_gather(local_rows, "tensor", axis=0, tiled=True))]

    def rows_out(self, term, beside):
        if self.tensor_size == 2:
            came = self.across(beside.tick(term(1).astype(BF16)))
            return term(0) + beside.tick(came).astype(F32)
        whole = beside.tick(term(0).astype(BF16))
        return beside.tick(
            lax.psum_scatter(whole, "tensor", scatter_dimension=0, tiled=True)
        ).astype(F32)

    def butterfly(self, array, axis, size):
        bit = 1
        while bit < size:
            array = array + lax.ppermute(array, axis, [(i, i ^ bit) for i in range(size)])
            bit *= 2
        return array


class Task:
    def __init__(self, steps, load):
        self.steps, self.load, self.done, self.result = steps, load, False, None
        self.pending = None
        self.advance(None, first=True)

    def advance(self, arrived, first=False):
        try:
            self.pending = next(self.steps) if first else self.steps.send(arrived)
        except StopIteration as stop:
            self.done, self.result = True, stop.value

    def finish(self):
        while not self.done:
            self.advance(self.pending)
        return self.result


class Beside:
    def __init__(self, most):
        self.most, self.tasks = most, []

    def add(self, task):
        self.tasks.append(task)
        return task

    def lead(self, first, second):
        step = 0
        while not first.done:
            chosen = [first, second] if step % 2 else [first]
            arrived = lax.optimization_barrier([task.pending for task in chosen])
            for task, part in zip(chosen, arrived):
                task.advance(part)
            step += 1
        return first.result

    def tick(self, value):
        self.tasks = [task for task in self.tasks if not task.done]
        chosen, load = [], 0.0
        for task in self.tasks:
            if not chosen or load + task.load <= self.most:
                chosen.append(task)
                load += task.load
        if not chosen:
            return value
        value, arrived = lax.optimization_barrier((value, [task.pending for task in chosen]))
        for task, part in zip(chosen, arrived):
            task.advance(part)
        return value


def place_pieces(source, pieces, chip_rows, cuts):
    count, width = len(pieces), pieces[0].shape[1]
    aligned = all(a % 128 == 0 and b % 128 == 0 for a, b in cuts)
    ranges = cuts if aligned else ((0, width),)
    spare = pieces[0].shape[0] - chip_rows

    def kernel(source_ref, *refs):
        ins, outs, sems = refs[:count], refs[count:-1], refs[-1]
        copies = []
        for i, piece in enumerate(ins):
            rows = pl.ds(pl.multiple_of(source_ref[i] * chip_rows, chip_rows), chip_rows)
            for j, (a, b) in enumerate(ranges):
                copies.append(
                    pltpu.make_async_copy(
                        piece.at[0:chip_rows, a:b], outs[j].at[rows, :], sems.at[i, j]
                    )
                )
            if spare:
                copies.append(
                    pltpu.make_async_copy(
                        piece.at[chip_rows : chip_rows + spare, 0:128],
                        outs[-1].at[source_ref[i]],
                        sems.at[i, len(ranges)],
                    )
                )
        for copy in copies:
            copy.start()
        for copy in copies:
            copy.wait()

    shapes = [jax.ShapeDtypeStruct((count * chip_rows, b - a), BF16) for a, b in ranges]
    if spare:
        shapes.append(jax.ShapeDtypeStruct((count, spare, 128), BF16))
    size = count * pieces[0].size * 2
    outs = pl.pallas_call(
        kernel,
        out_shape=shapes,
        in_specs=[pl.BlockSpec(memory_space=pltpu.SMEM)]
        + [pl.BlockSpec(memory_space=pl.ANY)] * count,
        out_specs=[pl.BlockSpec(memory_space=pltpu.VMEM)] * len(shapes),
        scratch_shapes=[pltpu.SemaphoreType.DMA((count, len(shapes)))],
        compiler_params=pltpu.CompilerParams(vmem_limit_bytes=16 << 20),
        cost_estimate=pl.CostEstimate(flops=0, bytes_accessed=2 * size, transcendentals=0),
        name="place_pieces",
    )(source, *pieces)
    vector = outs[-1] if spare else None
    wholes = outs[: len(ranges)]
    if not aligned:
        wholes = [wholes[0][:, a:b] for a, b in cuts]
    return wholes, vector


def owner_swap(rows):
    return lax.all_to_all(rows, "dp", split_axis=0, concat_axis=0, tiled=True)


def erf(x):
    x = jnp.clip(x, -3.7439211627767994, 3.7439211627767994)
    s = x * x
    top = jnp.full_like(s, 0.00022905065861350646)
    for c in (0.0034082910107109506, 0.050955695062380861, 0.18520832239976145, 1.128379143519084):
        top = top * s + c
    low = jnp.full_like(s, -1.1791602954361697e-7)
    for c in (
        0.000023547966471313185,
        0.0010179625278914885,
        0.014070470171167667,
        0.11098505178285362,
        0.49746925110067538,
        1.0,
    ):
        low = low * s + c
    return x * top / low


def whole_spec(shape):
    return pl.BlockSpec(shape, lambda *_: (0,) * len(shape))


def attend_forward(blocks, weight, bias, segment):
    rows = sum(block.shape[0] for block in blocks)
    inner = weight.shape[1] // 3
    heads = inner // HEAD
    step = min(512, rows)
    scale = 1.0 / math.sqrt(HEAD)

    def kernel(*refs):
        xs = refs[: len(blocks)]
        w_ref, bias_ref, col_ref, row_ref, qkv_ref, out_ref, log_ref = refs[len(blocks) :]
        start = 0
        for x in xs:
            size = x.shape[0]
            projected = dot(x[...], w_ref[...]) + bias_ref[...]
            qkv_ref[start : start + size, :] = projected.astype(BF16)
            start += size
        for first in range(0, rows, step):
            part = slice(first, first + step)
            far = jnp.where(col_ref[...] == row_ref[:, part], 0.0, -1e30)
            mixed = []
            for h in range(heads):
                lanes = [slice(i * inner + h * HEAD, i * inner + (h + 1) * HEAD) for i in range(3)]
                scores = times_transposed(qkv_ref[:, lanes[1]], qkv_ref[part, lanes[0]])
                scores = scores * scale + far
                highest = jnp.max(scores, axis=0, keepdims=True)
                powers = jnp.exp(scores - highest)
                summed = jnp.sum(powers, axis=0, keepdims=True)
                mixture = contract_rows(qkv_ref[:, lanes[2]], powers.astype(BF16))
                mixed.append(mixture * (1.0 / summed))
                log_ref[h : h + 1, part] = highest + jnp.log(summed)
            out_ref[part, :] = jnp.concatenate(mixed, 0).T.astype(BF16)

    flops = 2 * rows * (D * 3 * inner + 2 * rows * inner)
    return pl.pallas_call(
        kernel,
        out_shape=[
            jax.ShapeDtypeStruct((rows, 3 * inner), BF16),
            jax.ShapeDtypeStruct((rows, inner), BF16),
            jax.ShapeDtypeStruct((heads, rows), F32),
        ],
        compiler_params=pltpu.CompilerParams(vmem_limit_bytes=56 << 20),
        cost_estimate=pl.CostEstimate(
            flops=flops, bytes_accessed=2 * (rows + 3 * inner) * D, transcendentals=heads * rows**2
        ),
        name="attend_forward",
    )(*blocks, weight, bias[None], segment[:, None], segment[None])


def attend_backward(blocks, weight, qkv, mixture, log_total, segment):
    rows = sum(block.shape[0] for block in blocks)
    inner = weight.shape[1]
    heads = inner // HEAD
    step = min(512, rows)
    scale = 1.0 / math.sqrt(HEAD)

    def kernel(*refs):
        xs = refs[: len(blocks)]
        (w_ref, qkv_ref, mix_ref, log_ref, col_ref, row_ref) = refs[len(blocks) : len(blocks) + 6]
        grad_ref, sum_ref, dout_ref = refs[len(blocks) + 6 :]
        start = 0
        for x in xs:
            size = x.shape[0]
            dout_ref[start : start + size, :] = dot(x[...], w_ref[...]).astype(BF16)
            start += size
        ones = jnp.ones((8, HEAD), F32)
        keys = [jnp.zeros((rows, HEAD), F32)] * heads
        values = [jnp.zeros((rows, HEAD), F32)] * heads
        for first in range(0, rows, step):
            part = slice(first, first + step)
            far = jnp.where(col_ref[...] == row_ref[:, part], 0.0, -1e30)
            queries = []
            for h in range(heads):
                lanes = [slice(i * inner + h * HEAD, i * inner + (h + 1) * HEAD) for i in range(3)]
                query, key = qkv_ref[part, lanes[0]], qkv_ref[:, lanes[1]]
                dout = dout_ref[part, lanes[0]]
                scores = times_transposed(key, query) * scale + far
                weights = jnp.exp(scores - log_ref[h : h + 1, part])
                product = dout.astype(F32) * mix_ref[part, lanes[0]].astype(F32)
                centre = lax.dot_general(
                    ones,
                    product,
                    (((1,), (1,)), ((), ())),
                    precision=lax.Precision.HIGHEST,
                    preferred_element_type=F32,
                )[0:1]
                grad_weights = times_transposed(qkv_ref[:, lanes[2]], dout)
                grad_scores = (weights * (grad_weights - centre)).astype(BF16)
                queries.append(contract_rows(key, grad_scores))
                keys[h] = keys[h] + dot(grad_scores, query)
                values[h] = values[h] + dot(weights.astype(BF16), dout)
            grad_ref[part, 0:inner] = (jnp.concatenate(queries, 0).T * scale).astype(BF16)
        for h in range(heads):
            grad_ref[:, inner + h * HEAD : inner + (h + 1) * HEAD] = (keys[h] * scale).astype(BF16)
            grad_ref[:, 2 * inner + h * HEAD : 2 * inner + (h + 1) * HEAD] = values[h].astype(BF16)
        sum_ref[...] = jnp.sum(grad_ref[...].astype(F32), axis=0, keepdims=True)

    flops = 2 * rows * (D * inner + 5 * rows * inner)
    return pl.pallas_call(
        kernel,
        out_shape=[
            jax.ShapeDtypeStruct((rows, 3 * inner), BF16),
            jax.ShapeDtypeStruct((1, 3 * inner), F32),
        ],
        scratch_shapes=[pltpu.VMEM((rows, inner), BF16)],
        compiler_params=pltpu.CompilerParams(vmem_limit_bytes=56 << 20),
        cost_estimate=pl.CostEstimate(
            flops=flops, bytes_accessed=2 * (rows + inner) * D, transcendentals=heads * rows**2
        ),
        name="attend_backward",
    )(*blocks, weight, qkv, mixture, log_total, segment[:, None], segment[None])


def feed(source, first, second, side, block, rows_all, filled, out_type, forward):
    rows = source.shape[0]
    hidden = first[0].shape[1]
    tile = min(512, hidden)
    tiles = hidden // tile
    row_tile = min(256, rows)
    inner_count = 2 if forward else 1
    given = 0 if filled is None else inner_count

    def kernel(x_ref, a_own, a_part, b_own, b_part, side_ref, *refs):
        refs = refs[given:]
        out_ref, inner_refs, refs = refs[0], refs[1 : 1 + inner_count], refs[1 + inner_count :]
        total_ref = refs[-1]
        index = pl.program_id(1)

        def run(a_ref, b_ref):
            pre = dot(x_ref[...], a_ref[...])
            if forward:
                pre = pre + side_ref[...]
                cdf = 0.5 + 0.5 * erf(pre * 0.7071067811865476)
                bell = jnp.exp(-0.5 * pre * pre) * 0.3989422804014327
                kept = (pre * cdf).astype(BF16)
                inner_refs[0][...] = kept
                inner_refs[1][...] = (cdf + pre * bell).astype(BF16)
            else:
                kept = (pre * side_ref[...].astype(F32)).astype(BF16)
                inner_refs[0][...] = kept
                refs[0][...] = jnp.sum(kept.astype(F32), axis=0, keepdims=True)[None]
            term = times_transposed(kept, b_ref[...])

            @pl.when(index == 0)
            def _():
                total_ref[...] = term

            @pl.when(index > 0)
            def _():
                total_ref[...] += term

        @pl.when(index < tiles)
        def _():
            run(a_own, b_own)

        @pl.when(index >= tiles)
        def _():
            run(a_part, b_part)

        @pl.when(index == 2 * tiles - 1)
        def _():
            out_ref[...] = total_ref[...].astype(out_type)

    shift = block * (rows // row_tile)
    own = pl.BlockSpec((D, tile), lambda r, i: (0, jnp.minimum(i, tiles - 1)))
    part = pl.BlockSpec((D, tile), lambda r, i: (0, jnp.maximum(i - tiles, 0)))
    over = pl.BlockSpec((row_tile, tile), lambda r, i: (r + shift, i))
    source_spec = pl.BlockSpec((row_tile, D), lambda r, i: (r, 0))
    side_spec = pl.BlockSpec((1, tile), lambda r, i: (0, i)) if forward else over
    out_shape = [jax.ShapeDtypeStruct((rows, D), out_type)]
    out_shape += [jax.ShapeDtypeStruct((rows_all, 2 * hidden), BF16)] * inner_count
    out_specs = [source_spec] + [over] * inner_count
    if not forward:
        out_shape.append(jax.ShapeDtypeStruct((rows // row_tile, 1, 2 * hidden), F32))
        out_specs.append(pl.BlockSpec((1, 1, tile), lambda r, i: (r, 0, i)))
    outs = pl.pallas_call(
        kernel,
        grid=(rows // row_tile, 2 * tiles),
        out_shape=out_shape,
        in_specs=[source_spec, own, part, own, part, side_spec]
        + [pl.BlockSpec(memory_space=pl.ANY)] * given,
        out_specs=out_specs,
        scratch_shapes=[pltpu.VMEM((row_tile, D), F32)],
        input_output_aliases={6 + i: 1 + i for i in range(given)},
        compiler_params=pltpu.CompilerParams(vmem_limit_bytes=40 << 20),
        cost_estimate=pl.CostEstimate(
            flops=8 * rows * D * hidden,
            bytes_accessed=8 * D * hidden,
            transcendentals=2 * rows * hidden if forward else 0,
        ),
        name="feed_forward" if forward else "feed_backward",
    )(source, *first, *second, side, *(filled or ()))
    return outs


def join(blocks):
    return blocks[0] if len(blocks) == 1 else jnp.concatenate(blocks, 0)


def body(
    tokens,
    cotangent,
    deal_slot,
    back_slot,
    lengths,
    time_step,
    time_table,
    w_qkv,
    b_qv,
    w_out,
    out_bias,
    ln_gain,
    ln_shift,
    w_ff1,
    b_ff1,
    w_ff2,
):
    wires = Wires(lax.axis_size("dp"), lax.axis_size("tensor"))
    rows_dev = tokens.shape[0]
    group_rows = rows_dev * wires.tensor_size
    tensor_index = lax.axis_index("tensor")
    layer_total = w_qkv.shape[0]
    inner = w_qkv.shape[3] // 2
    hidden = w_ff1.shape[2] // 2
    both = (True, False)

    time_piece = lax.dynamic_index_in_dim(time_table, time_step[0], 0, keepdims=False)
    own_rows = owner_swap(jnp.take(tokens, back_slot, axis=0))
    attn_cuts = ((0, 3 * inner), (3 * inner, 4 * inner))
    feed_cuts = ((0, hidden), (hidden, 2 * hidden))
    beside = Beside(3.0)
    tasks = []
    for layer in range(layer_total):
        attn_shards, feed_shards = [], []
        for mine in both:
            qkv = wires.half(w_qkv[layer], 2, mine)
            attn_shards.append(
                jnp.concatenate(
                    [qkv[0], qkv[1], qkv[2], wires.half(w_out[layer], 0, mine).T], axis=1
                )
            )
            feed_shards.append(
                jnp.concatenate(
                    [wires.half(w_ff1[layer], 1, mine), wires.half(w_ff2[layer], 0, mine).T], axis=1
                )
            )
        extra = time_piece if layer == 0 else None
        tasks.append(
            (
                Task(wires.gather_halves(attn_shards, attn_cuts, extra), 1.0),
                Task(wires.gather_halves(feed_shards, feed_cuts), 2.0),
            )
        )
    first_attn, time_row = beside.lead(*tasks[0])
    for task in [tasks[0][1]] + [task for pair in tasks[1:] for task in pair]:
        beside.add(task)


    def upstream_steps():
        picked = yield jnp.take(cotangent, back_slot, axis=0)
        arrived = yield owner_swap(picked)
        return arrived

    upstream = beside.add(Task(upstream_steps(), 1.0))
    seq_ends = jnp.cumsum(lengths[0])
    positions = jnp.arange(group_rows, dtype=jnp.int32)
    if wires.tensor_size == 2:
        positions = (positions + tensor_index * rows_dev) % group_rows
    segment = jnp.sum((positions[:, None] >= seq_ends[None, :]).astype(jnp.int32), axis=1)

    def relative(vector):
        return jnp.concatenate([wires.half(vector, 0, mine) for mine in both])

    weights = []
    stream = own_rows.astype(F32) + time_row.astype(F32)
    saved = []
    for layer in range(layer_total):
        input_blocks = wires.rows_in(stream.astype(BF16), beside if layer else None)
        qkv_w, out_w = first_attn if layer == 0 else tasks[layer][0].finish()
        attention = []
        for half, mine in enumerate(both):
            bias_q = wires.half(b_qv[layer, 0], 0, mine)
            bias_v = wires.half(b_qv[layer, 1], 0, mine)
            bias = jnp.concatenate([bias_q, jnp.zeros_like(bias_q), bias_v])
            attention.append(attend_forward(input_blocks, qkv_w[half], bias, segment))

        def attended_term(block):
            rows = input_blocks[0].shape[0]
            return sum(
                times_transposed(part[1][block * rows : (block + 1) * rows], out_w[half])
                for half, part in enumerate(attention)
            )

        middle = stream + wires.rows_out(attended_term, beside) + out_bias[layer, 0]
        normed = layer_norm(middle, ln_gain[layer, 0], ln_shift[layer, 0])
        normed_blocks = wires.rows_in(normed.astype(BF16), beside)
        first_w, second_w = tasks[layer][1].finish()
        weights.append((qkv_w, out_w, first_w, second_w))
        bias = relative(b_ff1[layer])[None]
        feed_sums, filled = [], None
        for block, rows in enumerate(normed_blocks):
            out_type = F32 if block == 0 else BF16
            total, *filled = feed(
                rows, first_w, second_w, bias, block, group_rows, filled, out_type, True
            )
            feed_sums.append(total)
        second_sum = normed + wires.rows_out(lambda i: feed_sums[i], beside) + out_bias[layer, 1]
        saved.append((input_blocks, attention, middle, normed_blocks, filled, second_sum))
        stream = layer_norm(second_sum, ln_gain[layer, 1], ln_shift[layer, 1])

    def returned_steps(rows):
        rows = yield rows
        rows = yield owner_swap(rows)
        return rows

    returned_out = beside.add(Task(returned_steps(stream.astype(BF16)), 1.0))
    gradient = upstream.finish().astype(F32)
    gradient_tasks = [None] * layer_total
    vector_grads = [None] * layer_total
    for layer in reversed(range(layer_total)):
        qkv_w, out_w, first_w, second_w = weights[layer]
        input_blocks, attention, middle, normed_blocks, (act, slope), second_sum = saved[layer]
        _, pull_second = jax.vjp(layer_norm, second_sum, ln_gain[layer, 1], ln_shift[layer, 1])
        grad_second, gain_second, shift_second = pull_second(gradient)
        branch_blocks = wires.rows_in(grad_second.astype(BF16), beside)
        feed_sums, hidden_sums, filled = [], [], None
        for block, rows in enumerate(branch_blocks):
            out_type = F32 if block == 0 else BF16
            total, grad_pre, sums = feed(
                rows, second_w, first_w, slope, block, group_rows, filled, out_type, False
            )
            filled = (grad_pre,)
            feed_sums.append(total)
            hidden_sums.append(sums)
        hidden_sums = sum(jnp.sum(sums, axis=(0, 1)) for sums in hidden_sums)
        width = act.shape[1] // 2
        feed_task = beside.add(
            Task(
                wires.reduce_halves(
                    [
                        lambda half, n=join(normed_blocks), g=grad_pre: contract_rows(
                            n, g[:, half * width : (half + 1) * width]
                        ),
                        lambda half, n=join(branch_blocks), g=act: contract_rows(
                            n, g[:, half * width : (half + 1) * width]
                        ),
                    ]
                ),
                2.0,
            )
        )
        grad_normed = grad_second + wires.rows_out(lambda i: feed_sums[i], beside)
        _, pull_first = jax.vjp(layer_norm, middle, ln_gain[layer, 0], ln_shift[layer, 0])
        grad_middle, gain_first, shift_first = pull_first(grad_normed)
        attend_blocks = wires.rows_in(grad_middle.astype(BF16), beside)
        grad_wide, qkv_sums = [], []
        for half in (0, 1):
            qkv, mixture, log_total = attention[half]
            wide, sums = attend_backward(
                attend_blocks, out_w[half], qkv, mixture, log_total, segment
            )
            grad_wide.append(wide)
            qkv_sums.append(sums.reshape(3, inner))

        def proj_term(block):
            rows = input_blocks[0].shape[0]
            return sum(
                times_transposed(grad_wide[half][block * rows : (block + 1) * rows], qkv_w[half])
                for half in (0, 1)
            )

        attn_task = beside.add(
            Task(
                wires.reduce_halves(
                    [
                        lambda half, n=join(input_blocks), g=grad_wide: contract_rows(n, g[half]),
                        lambda half, n=join(attend_blocks), g=attention: contract_rows(n, g[half][1]),
                    ]
                ),
                1.0,
            )
        )
        gradient = grad_middle + wires.rows_out(proj_term, beside)
        gradient_tasks[layer] = (attn_task, feed_task)
        vector_grads[layer] = (
            wires.ordered(qkv_sums[0][::2], qkv_sums[1][::2], 1),
            wires.ordered(hidden_sums[:width], hidden_sums[width:], 0),
            jnp.stack([jnp.sum(grad_middle, axis=0), jnp.sum(grad_second, axis=0)]),
            jnp.stack([gain_first, gain_second]),
            jnp.stack([shift_first, shift_second]),
        )
    returned_grad = owner_swap(gradient.astype(BF16))
    grad_tokens = jnp.take(returned_grad, deal_slot, axis=0)
    encoded = jnp.take(returned_out.finish(), deal_slot, axis=0)
    matrix_grads = []
    for attn_task, feed_task in gradient_tasks:
        first_pair, second_pair = feed_task.finish()
        qkv_pair, out_pair = attn_task.finish()
        rows = qkv_pair[0].shape[0]
        matrix_grads.append((
            wires.ordered(
                *(part.reshape(rows, 3, inner).transpose(1, 0, 2) for part in qkv_pair), 2
            ),
            wires.ordered(out_pair[0].T, out_pair[1].T, 0),
            wires.ordered(first_pair[0], first_pair[1], 1),
            wires.ordered(second_pair[0].T, second_pair[1].T, 0),
        ))
    time_grad = jnp.sum(gradient, axis=0)
    local = [jnp.stack([part[i] for part in vector_grads]) for i in range(5)]
    flat = jnp.concatenate([part.reshape(-1) for part in local[:2] + [time_grad] + local[2:]])
    flat = wires.butterfly(flat, "dp", wires.dp_size)
    border = local[0].size + local[1].size
    shared = wires.butterfly(flat[border:], "tensor", wires.tensor_size)
    grad_b_qv = flat[: local[0].size].reshape(local[0].shape)
    grad_b_ff1 = flat[local[0].size : border].reshape(local[1].shape)
    time_grad = shared[:D]
    rest = shared[D:].reshape(3, layer_total, 2, D)
    return (
        encoded,
        grad_tokens,
        time_grad,
        jnp.stack([part[0] for part in matrix_grads]),
        grad_b_qv,
        jnp.stack([part[1] for part in matrix_grads]),
        rest[0],
        rest[1],
        rest[2],
        jnp.stack([part[2] for part in matrix_grads]),
        grad_b_ff1,
        jnp.stack([part[3] for part in matrix_grads]),
    )


def solution(mesh):
    return jax.shard_map(
        body,
        mesh=mesh,
        in_specs=(
            P(("dp", "tensor"), None),
            P(("dp", "tensor"), None),
            P(("dp", "tensor")),
            P(("dp", "tensor")),
            P("dp", None),
            P(),
            P(None, "dp"),
            P(None, None, "dp", "tensor"),
            P(None, None, "tensor"),
            P(None, "tensor", "dp"),
            P(),
            P(),
            P(),
            P(None, "dp", "tensor"),
            P(None, "tensor"),
            P(None, "tensor", "dp"),
        ),
        out_specs=(
            P(("dp", "tensor"), None),
            P(("dp", "tensor"), None),
            P(),
            P(None, None, "dp", "tensor"),
            P(None, None, "tensor"),
            P(None, "tensor", "dp"),
            P(),
            P(),
            P(),
            P(None, "dp", "tensor"),
            P(None, "tensor"),
            P(None, "tensor", "dp"),
        ),
        check_vma=False,
    )
```

```python
import math

import jax
import jax.numpy as jnp
import numpy as np
from jax import lax
from jax.experimental import pallas as pl
from jax.experimental.pallas import tpu as pltpu
from jax.sharding import PartitionSpec as P

D = 1024
HEADS = 16
FF = 4096
HEAD = D // HEADS
F32 = jnp.float32
BF16 = jnp.bfloat16


def layer_norm(summed, scaling, offset_vec):
    centre = jnp.mean(summed, axis=-1, keepdims=True)
    spread = summed - centre
    variance = jnp.mean(spread * spread, axis=-1, keepdims=True)
    return spread * lax.rsqrt(variance + 1e-05) * scaling + offset_vec


def dot(left, right):
    return jnp.dot(left, right, preferred_element_type=F32)


def contract_rows(left, right):
    return lax.dot_general(left, right, (((0,), (0,)), ((), ())), preferred_element_type=F32)


def times_transposed(left, right):
    return lax.dot_general(left, right, (((1,), (1,)), ((), ())), preferred_element_type=F32)


class Wires:
    def __init__(self, dp_size, tensor_size):
        self.dp_size, self.tensor_size = dp_size, tensor_size
        chips = dp_size // 2
        self.chips = chips
        order = list(range(0, chips, 2)) + list(range(chips - 1, 0, -2))
        place = {chip: spot for spot, chip in enumerate(order)}
        ring, sources = [], np.zeros((dp_size, chips), np.int32)
        for device in range(dp_size):
            chip, core = divmod(device, 2)
            way = 1 if core == 0 else -1
            ring.append((device, 2 * order[(place[chip] + way) % chips] + core))
            sources[device] = [order[(place[chip] - way * s) % chips] for s in range(chips)]
        self.ring = ring
        self.cores = [list(range(core, dp_size, 2)) for core in (0, 1)]
        self.swap = [(d, d ^ 1) for d in range(dp_size)]
        dp_index = lax.axis_index("dp")
        self.core = dp_index % 2
        self.source = lax.dynamic_index_in_dim(jnp.asarray(sources), dp_index, 0, keepdims=False)

    def hop(self, array):
        return lax.ppermute(array, "dp", self.ring)

    def partner(self, array):
        return lax.ppermute(array, "dp", self.swap)

    def across(self, array):
        return lax.ppermute(array, "tensor", [(0, 1), (1, 0)])

    def half(self, array, axis, mine):
        width = array.shape[axis] // 2
        index = self.core if mine else 1 - self.core
        return lax.dynamic_slice_in_dim(array, index * width, width, axis)

    def ordered(self, mine, other, axis):
        return jnp.where(
            self.core == 0,
            jnp.concatenate([mine, other], axis),
            jnp.concatenate([other, mine], axis),
        )

    def chip_piece(self, shard):
        mine, other = shard
        return self.ordered(mine, self.partner(other), 0)

    def gather_ring(self, piece, extra=None):
        chip_rows = piece.shape[0]
        if extra is not None:
            tail = jnp.zeros((8, piece.shape[1]), piece.dtype)
            pair = self.ordered(extra, self.partner(extra), 0)
            tail = lax.dynamic_update_slice(tail, pair[None, :], (0, 0))
            piece = jnp.concatenate([piece, tail], 0)
        piece = yield piece
        pieces = [piece]
        for _ in range(1, self.chips):
            piece = yield self.hop(piece)
            pieces.append(piece)
        whole, vector = place_pieces(self.source, pieces, chip_rows)
        halves = (whole, self.partner(whole))
        return halves if extra is None else (halves, vector[:, 0, :chip_rows].reshape(-1))

    def gather_queue(self, piece):
        whole = lax.all_gather(piece, "dp", axis=0, tiled=True, axis_index_groups=self.cores)
        return whole, self.partner(whole)

    def own_half(self, terms, came):
        return [(term + part.astype(F32)).astype(BF16) for term, part in zip(terms, came)]

    def reduce_ring(self, sums):
        chip_rows = sums[0].shape[0] // self.chips

        def portion(step):
            start = self.source[(step + 1) % self.chips] * chip_rows
            return jnp.concatenate(
                [lax.dynamic_slice_in_dim(part, start, chip_rows, 0) for part in sums], 1
            )

        total = portion(0)
        for step in range(1, self.chips):
            arrived = yield self.hop(total.astype(BF16))
            total = arrived.astype(F32) + portion(step).astype(F32)
        return self.share_rows(total)

    def reduce_queue(self, sums):
        total = lax.psum_scatter(
            jnp.concatenate(sums, 1),
            "dp",
            scatter_dimension=0,
            tiled=True,
            axis_index_groups=self.cores,
        )
        return self.share_rows(total.astype(F32))

    def share_rows(self, total):
        mine = self.half(total, 0, True)
        other = self.partner(self.half(total, 0, False).astype(BF16)).astype(F32)
        return mine, other

    def rows_in(self, local_rows):
        if self.tensor_size == 2:
            return [local_rows, self.across(local_rows)]
        return [lax.all_gather(local_rows, "tensor", axis=0, tiled=True)]

    def rows_out(self, sums):
        if self.tensor_size == 2:
            return sums[0] + self.across(sums[1]).astype(F32)
        return lax.psum_scatter(sums[0], "tensor", scatter_dimension=0, tiled=True).astype(F32)

    def butterfly(self, array, border):
        for axis, size in (("dp", self.dp_size), ("tensor", self.tensor_size)):
            if axis == "tensor":
                array, kept = array[border:], array
            bit = 1
            while bit < size:
                pairs = [(i, i ^ bit) for i in range(size)]
                array = array + (yield lax.ppermute(array, axis, pairs))
                bit *= 2
        return kept, array


def owner_swap(rows):
    return lax.all_to_all(rows, "dp", split_axis=0, concat_axis=0, tiled=True)


class Task:
    def __init__(self, steps):
        self.steps, self.done, self.result = steps, False, None
        self.advance(None, first=True)

    def advance(self, arrived, first=False):
        try:
            self.pending = next(self.steps) if first else self.steps.send(arrived)
        except StopIteration as stop:
            self.done, self.result = True, stop.value

    def finish(self):
        while not self.done:
            self.advance(self.pending)
        return self.result


def tick(value, *tasks):
    tasks = [task for task in tasks if task is not None and not task.done]
    if not tasks:
        return value
    value, arrived = lax.optimization_barrier((value, [task.pending for task in tasks]))
    for task, part in zip(tasks, arrived):
        task.advance(part)
    return value


def tie(*values):
    return lax.optimization_barrier(values)


def place_pieces(source, pieces, chip_rows):
    count, width = len(pieces), pieces[0].shape[1]
    spare = pieces[0].shape[0] - chip_rows

    def kernel(source_ref, *refs):
        ins, outs, sems = refs[:count], refs[count:-1], refs[-1]
        copies = []
        for i, piece in enumerate(ins):
            rows = pl.ds(pl.multiple_of(source_ref[i] * chip_rows, chip_rows), chip_rows)
            copies.append(
                pltpu.make_async_copy(piece.at[0:chip_rows], outs[0].at[rows], sems.at[i, 0])
            )
            if spare:
                copies.append(
                    pltpu.make_async_copy(
                        piece.at[chip_rows : chip_rows + spare, 0:128],
                        outs[1].at[source_ref[i]],
                        sems.at[i, 1],
                    )
                )
        for copy in copies:
            copy.start()
        for copy in copies:
            copy.wait()

    shapes = [jax.ShapeDtypeStruct((count * chip_rows, width), BF16)]
    if spare:
        shapes.append(jax.ShapeDtypeStruct((count, spare, 128), BF16))
    outs = pl.pallas_call(
        kernel,
        out_shape=shapes,
        in_specs=[pl.BlockSpec(memory_space=pltpu.SMEM)]
        + [pl.BlockSpec(memory_space=pl.ANY)] * count,
        out_specs=[pl.BlockSpec(memory_space=pltpu.VMEM)] * len(shapes),
        scratch_shapes=[pltpu.SemaphoreType.DMA((count, 2))],
        compiler_params=pltpu.CompilerParams(vmem_limit_bytes=16 << 20),
        cost_estimate=pl.CostEstimate(
            flops=0, bytes_accessed=4 * count * pieces[0].size, transcendentals=0
        ),
        name="place_pieces",
    )(source, *pieces)
    return outs[0], (outs[1] if spare else None)


def erf(x):
    x = jnp.clip(x, -3.7439211627767994, 3.7439211627767994)
    s = x * x
    top = jnp.full_like(s, 0.00022905065861350646)
    for c in (0.0034082910107109506, 0.050955695062380861, 0.18520832239976145, 1.128379143519084):
        top = top * s + c
    low = jnp.full_like(s, -1.1791602954361697e-7)
    for c in (
        0.000023547966471313185,
        0.0010179625278914885,
        0.014070470171167667,
        0.11098505178285362,
        0.49746925110067538,
        1.0,
    ):
        low = low * s + c
    return x * top / low


def whole_spec(shape):
    return pl.BlockSpec(shape, lambda *_: (0,) * len(shape))


def attend_forward(blocks, weight, bias, segment, earlier=None):
    rows = sum(block.shape[0] for block in blocks)
    inner = weight.shape[1] // 4
    heads = inner // HEAD
    step = min(512, rows)
    scale = 1.0 / math.sqrt(HEAD)
    extra = 0 if earlier is None else 2

    def kernel(*refs):
        xs, refs = refs[: len(blocks)], refs[len(blocks) :]
        w_ref, bias_ref, col_ref, row_ref = refs[:4]
        before, refs = refs[4 : 4 + extra], refs[4 + extra :]
        qkv_ref, out_ref, log_ref = refs[:3]
        start = 0
        for x in xs:
            size = x.shape[0]
            projected = dot(x[...], w_ref[:, : 3 * inner]) + bias_ref[...]
            qkv_ref[start : start + size, :] = projected.astype(BF16)
            start += size
        for first in range(0, rows, step):
            part = slice(first, first + step)
            far = jnp.where(col_ref[...] == row_ref[:, part], 0.0, -1e30)
            mixed = []
            for h in range(heads):
                lanes = [slice(i * inner + h * HEAD, i * inner + (h + 1) * HEAD) for i in range(3)]
                scores = times_transposed(qkv_ref[:, lanes[1]], qkv_ref[part, lanes[0]])
                scores = scores * scale + far
                highest = jnp.max(scores, axis=0, keepdims=True)
                powers = jnp.exp(scores - highest)
                summed = jnp.sum(powers, axis=0, keepdims=True)
                mixture = contract_rows(qkv_ref[:, lanes[2]], powers.astype(BF16))
                mixed.append(mixture * (1.0 / summed))
                log_ref[h : h + 1, part] = highest + jnp.log(summed)
            out_ref[part, :] = jnp.concatenate(mixed, 0).T.astype(BF16)
        start = 0
        for sum_ref in refs[3:]:
            part = slice(start, start + sum_ref.shape[0])
            start += sum_ref.shape[0]
            total = times_transposed(before[0][part, :], before[1][:, 3 * inner :])
            total += times_transposed(out_ref[part, :], w_ref[:, 3 * inner :])
            sum_ref[...] = total.astype(sum_ref.dtype)

    shapes = [
        jax.ShapeDtypeStruct((rows, 3 * inner), BF16),
        jax.ShapeDtypeStruct((rows, inner), BF16),
        jax.ShapeDtypeStruct((heads, rows), F32),
    ]
    if earlier is not None:
        shapes += sum_shapes(blocks)
    outs = pl.pallas_call(
        kernel,
        out_shape=shapes,
        compiler_params=pltpu.CompilerParams(vmem_limit_bytes=56 << 20),
        cost_estimate=pl.CostEstimate(
            flops=2 * rows * (D * 3 * inner + 2 * rows * inner) + extra * rows * D * 2 * inner,
            bytes_accessed=2 * (rows + 4 * inner) * D,
            transcendentals=heads * rows**2,
        ),
        name="attend_forward",
    )(*blocks, weight, bias[None], segment[:, None], segment[None], *(earlier or ()))
    return tuple(outs[:3]), list(outs[3:])


def sum_shapes(blocks):
    kinds = (F32, BF16) if len(blocks) == 2 else (BF16,)
    return [jax.ShapeDtypeStruct(block.shape, kind) for block, kind in zip(blocks, kinds)]


def attend_backward(blocks, weight, qkv, mixture, log_total, segment, earlier=None):
    rows = sum(block.shape[0] for block in blocks)
    inner = weight.shape[1] // 4
    extra = 0 if earlier is None else 2
    heads = inner // HEAD
    step = min(512, rows)
    scale = 1.0 / math.sqrt(HEAD)

    def kernel(*refs):
        xs = refs[: len(blocks)]
        (w_ref, qkv_ref, mix_ref, log_ref, col_ref, row_ref) = refs[len(blocks) : len(blocks) + 6]
        refs = refs[len(blocks) + 6 :]
        before, refs = refs[:extra], refs[extra:]
        grad_ref, sum_ref, dout_ref = refs[0], refs[1], refs[-1]
        start = 0
        for x in xs:
            size = x.shape[0]
            dout_ref[start : start + size, :] = dot(x[...], w_ref[:, 3 * inner :]).astype(BF16)
            start += size
        ones = jnp.ones((8, HEAD), F32)
        keys = [jnp.zeros((rows, HEAD), F32)] * heads
        values = [jnp.zeros((rows, HEAD), F32)] * heads
        for first in range(0, rows, step):
            part = slice(first, first + step)
            far = jnp.where(col_ref[...] == row_ref[:, part], 0.0, -1e30)
            queries = []
            for h in range(heads):
                lanes = [slice(i * inner + h * HEAD, i * inner + (h + 1) * HEAD) for i in range(3)]
                query, key = qkv_ref[part, lanes[0]], qkv_ref[:, lanes[1]]
                dout = dout_ref[part, lanes[0]]
                scores = times_transposed(key, query) * scale + far
                weights = jnp.exp(scores - log_ref[h : h + 1, part])
                product = dout.astype(F32) * mix_ref[part, lanes[0]].astype(F32)
                centre = lax.dot_general(
                    ones,
                    product,
                    (((1,), (1,)), ((), ())),
                    precision=lax.Precision.HIGHEST,
                    preferred_element_type=F32,
                )[0:1]
                grad_weights = times_transposed(qkv_ref[:, lanes[2]], dout)
                grad_scores = (weights * (grad_weights - centre)).astype(BF16)
                queries.append(contract_rows(key, grad_scores))
                keys[h] = keys[h] + dot(grad_scores, query)
                values[h] = values[h] + dot(weights.astype(BF16), dout)
            grad_ref[part, 0:inner] = (jnp.concatenate(queries, 0).T * scale).astype(BF16)
        for h in range(heads):
            grad_ref[:, inner + h * HEAD : inner + (h + 1) * HEAD] = (keys[h] * scale).astype(BF16)
            grad_ref[:, 2 * inner + h * HEAD : 2 * inner + (h + 1) * HEAD] = values[h].astype(BF16)
        sum_ref[...] = jnp.sum(grad_ref[...].astype(F32), axis=0, keepdims=True)
        start = 0
        for out_ref in refs[2:-1]:
            part = slice(start, start + out_ref.shape[0])
            start += out_ref.shape[0]
            total = times_transposed(before[0][part, :], before[1][:, : 3 * inner])
            total += times_transposed(grad_ref[part, :], w_ref[:, : 3 * inner])
            out_ref[...] = total.astype(out_ref.dtype)

    flops = 2 * rows * (D * inner + 5 * rows * inner) + extra * rows * D * 6 * inner
    shapes = [
        jax.ShapeDtypeStruct((rows, 3 * inner), BF16),
        jax.ShapeDtypeStruct((1, 3 * inner), F32),
    ]
    if earlier is not None:
        shapes += sum_shapes(blocks)
    outs = pl.pallas_call(
        kernel,
        out_shape=shapes,
        scratch_shapes=[pltpu.VMEM((rows, inner), BF16)],
        compiler_params=pltpu.CompilerParams(vmem_limit_bytes=56 << 20),
        cost_estimate=pl.CostEstimate(
            flops=flops, bytes_accessed=2 * (rows + inner) * D, transcendentals=heads * rows**2
        ),
        name="attend_backward",
    )(*blocks, weight, qkv, mixture, log_total, segment[:, None], segment[None], *(earlier or ()))
    return outs[0], outs[1], list(outs[2:])


def feed(source, weights, side, block, rows_all, filled, out_type, forward):
    rows = source.shape[0]
    hidden = weights[0].shape[1] // 2
    tile = min(512, hidden)
    tiles = hidden // tile
    row_tile = min(256, rows)
    inner_count = 2 if forward else 1
    given = 0 if filled is None else inner_count

    def kernel(x_ref, a_own, a_part, b_own, b_part, side_ref, *refs):
        refs = refs[given:]
        out_ref, inner_refs, refs = refs[0], refs[1 : 1 + inner_count], refs[1 + inner_count :]
        total_ref = refs[-1]
        index = pl.program_id(1)

        def run(a_ref, b_ref):
            pre = dot(x_ref[...], a_ref[...])
            if forward:
                pre = pre + side_ref[...]
                cdf = 0.5 + 0.5 * erf(pre * 0.7071067811865476)
                bell = jnp.exp(-0.5 * pre * pre) * 0.3989422804014327
                kept = (pre * cdf).astype(BF16)
                inner_refs[0][...] = kept
                inner_refs[1][...] = (cdf + pre * bell).astype(BF16)
            else:
                kept = (pre * side_ref[...].astype(F32)).astype(BF16)
                inner_refs[0][...] = kept
                refs[0][...] = jnp.sum(kept.astype(F32), axis=0, keepdims=True)[None]
            term = times_transposed(kept, b_ref[...])

            @pl.when(index == 0)
            def _():
                total_ref[...] = term

            @pl.when(index > 0)
            def _():
                total_ref[...] += term

        @pl.when(index < tiles)
        def _():
            run(a_own, b_own)

        @pl.when(index >= tiles)
        def _():
            run(a_part, b_part)

        @pl.when(index == 2 * tiles - 1)
        def _():
            out_ref[...] = total_ref[...].astype(out_type)

    shift = block * (rows // row_tile)
    shifts = (0, tiles) if forward else (tiles, 0)
    owns = [
        pl.BlockSpec((D, tile), lambda r, i, k=k: (0, jnp.minimum(i, tiles - 1) + k)) for k in shifts
    ]
    parts = [
        pl.BlockSpec((D, tile), lambda r, i, k=k: (0, jnp.maximum(i - tiles, 0) + k)) for k in shifts
    ]
    over = pl.BlockSpec((row_tile, tile), lambda r, i: (r + shift, i))
    source_spec = pl.BlockSpec((row_tile, D), lambda r, i: (r, 0))
    side_spec = pl.BlockSpec((1, tile), lambda r, i: (0, i)) if forward else over
    out_shape = [jax.ShapeDtypeStruct((rows, D), out_type)]
    out_shape += [jax.ShapeDtypeStruct((rows_all, 2 * hidden), BF16)] * inner_count
    out_specs = [source_spec] + [over] * inner_count
    if not forward:
        out_shape.append(jax.ShapeDtypeStruct((rows // row_tile, 1, 2 * hidden), F32))
        out_specs.append(pl.BlockSpec((1, 1, tile), lambda r, i: (r, 0, i)))
    outs = pl.pallas_call(
        kernel,
        grid=(rows // row_tile, 2 * tiles),
        out_shape=out_shape,
        in_specs=[source_spec, owns[0], parts[0], owns[1], parts[1], side_spec]
        + [pl.BlockSpec(memory_space=pl.ANY)] * given,
        out_specs=out_specs,
        scratch_shapes=[pltpu.VMEM((row_tile, D), F32)],
        input_output_aliases={6 + i: 1 + i for i in range(given)},
        compiler_params=pltpu.CompilerParams(vmem_limit_bytes=60 << 20),
        cost_estimate=pl.CostEstimate(
            flops=8 * rows * D * hidden,
            bytes_accessed=8 * D * hidden,
            transcendentals=2 * rows * hidden if forward else 0,
        ),
        name="feed_forward" if forward else "feed_backward",
    )(source, *weights, *weights, side, *(filled or ()))
    return outs


def join(blocks):
    return blocks[0] if len(blocks) == 1 else jnp.concatenate(blocks, 0)


def body(
    tokens,
    cotangent,
    deal_slot,
    back_slot,
    lengths,
    time_step,
    time_table,
    w_qkv,
    b_qv,
    w_out,
    out_bias,
    ln_gain,
    ln_shift,
    w_ff1,
    b_ff1,
    w_ff2,
):
    wires = Wires(lax.axis_size("dp"), lax.axis_size("tensor"))
    rows_dev = tokens.shape[0]
    group_rows = rows_dev * wires.tensor_size
    tensor_index = lax.axis_index("tensor")
    layer_total = w_qkv.shape[0]
    inner = w_qkv.shape[3] // 2
    hidden = w_ff1.shape[2] // 2
    both = (True, False)

    own_tokens = owner_swap(jnp.take(tokens, back_slot, axis=0))
    time_piece = lax.dynamic_index_in_dim(time_table, time_step[0], 0, keepdims=False)
    pieces = []
    for layer in range(layer_total):
        attn_shard, feed_shard = [], []
        for mine in both:
            qkv = wires.half(w_qkv[layer], 2, mine)
            out = wires.half(w_out[layer], 0, mine).T
            attn_shard.append(jnp.concatenate([qkv[0], qkv[1], qkv[2], out], axis=1))
            first = wires.half(w_ff1[layer], 1, mine)
            second = wires.half(w_ff2[layer], 0, mine).T
            feed_shard.append(jnp.concatenate([first, second], axis=1))
        pieces.append((wires.chip_piece(attn_shard), wires.chip_piece(feed_shard)))
    attn_ring = Task(wires.gather_ring(pieces[0][0], time_piece))
    feed_ring = Task(wires.gather_ring(pieces[0][1]))
    step = 0
    while not attn_ring.done:
        if step == 3:
            own_tokens = tick(own_tokens, attn_ring, feed_ring)
            token_blocks = wires.rows_in(own_tokens)
        else:
            tick((), attn_ring, feed_ring if step % 2 else None)
        step += 1
    attn_w, time_row = attn_ring.result
    time_row, *queued = tie(time_row, *[part for pair in pieces[1:] for part in pair])
    weights = [[attn_w, None]]
    for i in range(0, len(queued), 2):
        weights.append([wires.gather_queue(queued[i]), wires.gather_queue(queued[i + 1])])
    time_row = time_row.astype(F32)

    seq_ends = jnp.cumsum(lengths[0])
    positions = jnp.arange(group_rows, dtype=jnp.int32)
    if wires.tensor_size == 2:
        positions = (positions + tensor_index * rows_dev) % group_rows
    segment = jnp.sum((positions[:, None] >= seq_ends[None, :]).astype(jnp.int32), axis=1)

    stream = own_tokens.astype(F32) + time_row
    saved = []
    for layer in range(layer_total):
        if layer == 0:
            input_blocks = [(rows.astype(F32) + time_row).astype(BF16) for rows in token_blocks]
        else:
            input_blocks = wires.rows_in(stream.astype(BF16))
        beside = feed_ring if layer == 0 else None
        attn_w = weights[layer][0]
        biases = []
        for mine in both:
            bias_q, bias_v = [wires.half(b_qv[layer, i], 0, mine) for i in (0, 1)]
            biases.append(jnp.concatenate([bias_q, jnp.zeros_like(bias_q), bias_v]))
        (qkv, mixture, log_total), _ = attend_forward(input_blocks, attn_w[0], biases[0], segment)
        mixture = tick(mixture, beside)
        attention = [(qkv, mixture, log_total)]
        part, sums = attend_forward(
            input_blocks, attn_w[1], biases[1], segment, (mixture, attn_w[0])
        )
        attention.append(part)
        sums[-1] = tick(sums[-1], beside)
        middle = stream + wires.rows_out(sums) + out_bias[layer, 0]
        normed = layer_norm(middle, ln_gain[layer, 0], ln_shift[layer, 0])
        normed_blocks = wires.rows_in(tick(normed.astype(BF16), beside))
        if layer == 0:
            weights[0][1] = feed_ring.finish()
        feed_w = weights[layer][1]
        bias = jnp.concatenate([wires.half(b_ff1[layer], 0, mine) for mine in both])[None]
        sums, filled = [], None
        for block, rows in enumerate(normed_blocks):
            kind = F32 if block == 0 and wires.tensor_size == 2 else BF16
            total, *filled = feed(rows, feed_w, bias, block, group_rows, filled, kind, True)
            sums.append(total)
        second_sum = normed + wires.rows_out(sums) + out_bias[layer, 1]
        saved.append((input_blocks, attention, middle, normed_blocks, filled, second_sum))
        stream = layer_norm(second_sum, ln_gain[layer, 1], ln_shift[layer, 1])
        if layer == 0:
            stream, cotangent = tie(stream, cotangent)
            upstream = owner_swap(jnp.take(cotangent, back_slot, axis=0))

    encoded_own = stream.astype(BF16)
    gradient = upstream.astype(F32)
    reduced = [None] * layer_total
    vector_grads = [None] * layer_total
    for layer in reversed(range(layer_total)):
        attn_w, feed_w = weights[layer]
        input_blocks, attention, middle, normed_blocks, (act, slope), second_sum = saved[layer]
        _, pull_second = jax.vjp(layer_norm, second_sum, ln_gain[layer, 1], ln_shift[layer, 1])
        grad_second, gain_second, shift_second = pull_second(gradient)
        branch_blocks = wires.rows_in(grad_second.astype(BF16))
        sums, hidden_sums, filled = [], [], None
        for block, rows in enumerate(branch_blocks):
            kind = F32 if block == 0 and wires.tensor_size == 2 else BF16
            total, grad_pre, more = feed(rows, feed_w, slope, block, group_rows, filled, kind, False)
            filled = (grad_pre,)
            sums.append(total)
            hidden_sums.append(more)
        hidden_sums = sum(jnp.sum(part, axis=(0, 1)) for part in hidden_sums)
        if layer == layer_total - 1:
            sums[-1], encoded_own = tie(sums[-1], encoded_own)
            returned_out = owner_swap(encoded_own)
        normed_all, branch_all = join(normed_blocks), join(branch_blocks)

        def feed_terms(half):
            columns = slice(half * hidden, (half + 1) * hidden)
            return [
                contract_rows(normed_all, grad_pre[:, columns]),
                contract_rows(branch_all, act[:, columns]),
            ]

        came = [wires.partner(term.astype(BF16)) for term in feed_terms(1)]
        grad_normed = grad_second + wires.rows_out(sums)
        grad_normed, came = tie(grad_normed, came)
        _, pull_first = jax.vjp(layer_norm, middle, ln_gain[layer, 0], ln_shift[layer, 0])
        grad_middle, gain_first, shift_first = pull_first(grad_normed)
        attend_blocks = wires.rows_in(grad_middle.astype(BF16))
        feed_sums = wires.own_half(feed_terms(0), came)
        attend_blocks[-1], feed_sums = tie(attend_blocks[-1], feed_sums)
        feed_task = None
        if layer == 0:
            feed_task = Task(wires.reduce_ring(feed_sums))
        else:
            feed_total = wires.reduce_queue(feed_sums)
        input_all, attend_all = join(input_blocks), join(attend_blocks)

        def attn_terms(half, wide):
            return [
                contract_rows(input_all, wide),
                contract_rows(attend_all, attention[half][1]),
            ]

        wide, part_sums, _ = attend_backward(attend_blocks, attn_w[1], *attention[1], segment)
        sends = [term.astype(BF16) for term in attn_terms(1, wide)]
        wide = tick(wide, feed_task)
        if layer == 0:
            wide, sends = tie(wide, sends)
        came = [wires.partner(term) for term in sends]
        own_wide, own_sums, sums = attend_backward(
            attend_blocks, attn_w[0], *attention[0], segment, (wide, attn_w[1])
        )
        sums[-1] = tick(sums[-1], feed_task)
        gradient = grad_middle + wires.rows_out(sums)
        attn_sums = wires.own_half(attn_terms(0, own_wide), came)
        if layer == 0:
            attn_task = Task(wires.reduce_ring(attn_sums))
        else:
            gradient, attn_sums = tie(gradient, attn_sums)
            reduced[layer] = (wires.reduce_queue(attn_sums), feed_total)
        qkv_sums = [part.reshape(3, inner)[::2] for part in (own_sums, part_sums)]
        vector_grads[layer] = (
            wires.ordered(qkv_sums[0], qkv_sums[1], 1),
            wires.ordered(hidden_sums[:hidden], hidden_sums[hidden:], 0),
            jnp.stack([jnp.sum(grad_middle, axis=0), jnp.sum(grad_second, axis=0)]),
            jnp.stack([gain_first, gain_second]),
            jnp.stack([shift_first, shift_second]),
        )

    returned_grad = owner_swap(gradient.astype(BF16))
    time_grad = jnp.sum(gradient, axis=0)
    local = [jnp.stack([part[i] for part in vector_grads]) for i in range(5)]
    flat = jnp.concatenate([part.reshape(-1) for part in local[:2] + [time_grad] + local[2:]])
    border = local[0].size + local[1].size
    vector_task = Task(wires.butterfly(flat, border))
    while not (attn_task.done and feed_task.done and vector_task.done):
        tick((), attn_task, feed_task, vector_task)
    reduced[0] = (attn_task.result, feed_task.result)
    flat, shared = vector_task.result
    grad_tokens = jnp.take(returned_grad, deal_slot, axis=0)
    encoded = jnp.take(returned_out, deal_slot, axis=0)
    matrix_grads = []
    for attn_pair, feed_pair in reduced:
        rows = attn_pair[0].shape[0]
        matrix_grads.append(
            (
                wires.ordered(
                    *(
                        part[:, : 3 * inner].reshape(rows, 3, inner).transpose(1, 0, 2)
                        for part in attn_pair
                    ),
                    2,
                ),
                wires.ordered(*(part[:, 3 * inner :].T for part in attn_pair), 0),
                wires.ordered(*(part[:, :hidden] for part in feed_pair), 1),
                wires.ordered(*(part[:, hidden:].T for part in feed_pair), 0),
            )
        )
    grad_b_qv = flat[: local[0].size].reshape(local[0].shape)
    grad_b_ff1 = flat[local[0].size : border].reshape(local[1].shape)
    time_grad = shared[:D]
    rest = shared[D:].reshape(3, layer_total, 2, D)
    return (
        encoded,
        grad_tokens,
        time_grad,
        jnp.stack([part[0] for part in matrix_grads]),
        grad_b_qv,
        jnp.stack([part[1] for part in matrix_grads]),
        rest[0],
        rest[1],
        rest[2],
        jnp.stack([part[2] for part in matrix_grads]),
        grad_b_ff1,
        jnp.stack([part[3] for part in matrix_grads]),
    )


def solution(mesh):
    return jax.shard_map(
        body,
        mesh=mesh,
        in_specs=(
            P(("dp", "tensor"), None),
            P(("dp", "tensor"), None),
            P(("dp", "tensor")),
            P(("dp", "tensor")),
            P("dp", None),
            P(),
            P(None, "dp"),
            P(None, None, "dp", "tensor"),
            P(None, None, "tensor"),
            P(None, "tensor", "dp"),
            P(),
            P(),
            P(),
            P(None, "dp", "tensor"),
            P(None, "tensor"),
            P(None, "tensor", "dp"),
        ),
        out_specs=(
            P(("dp", "tensor"), None),
            P(("dp", "tensor"), None),
            P(),
            P(None, None, "dp", "tensor"),
            P(None, None, "tensor"),
            P(None, "tensor", "dp"),
            P(),
            P(),
            P(),
            P(None, "dp", "tensor"),
            P(None, "tensor"),
            P(None, "tensor", "dp"),
        ),
        check_vma=False,
    )
```

```python
import math

import jax
import jax.numpy as jnp
import numpy as np
from jax import lax
from jax.experimental import pallas as pl
from jax.experimental.pallas import tpu as pltpu
from jax.sharding import PartitionSpec as P

D = 1024
HEADS = 16
FF = 4096
HEAD = D // HEADS
F32 = jnp.float32
BF16 = jnp.bfloat16


def layer_norm(summed, scaling, offset_vec):
    centre = jnp.mean(summed, axis=-1, keepdims=True)
    spread = summed - centre
    variance = jnp.mean(spread * spread, axis=-1, keepdims=True)
    return spread * lax.rsqrt(variance + 1e-05) * scaling + offset_vec


def dot(left, right):
    return jnp.dot(left, right, preferred_element_type=F32)


def contract_rows(left, right):
    return lax.dot_general(left, right, (((0,), (0,)), ((), ())), preferred_element_type=F32)


def times_transposed(left, right):
    return lax.dot_general(left, right, (((1,), (1,)), ((), ())), preferred_element_type=F32)


class Wires:
    def __init__(self, dp_size, tensor_size):
        self.dp_size, self.tensor_size = dp_size, tensor_size
        chips = dp_size // 2
        self.chips = chips
        order = list(range(0, chips, 2)) + list(range(chips - 1, 0, -2))
        place = {chip: spot for spot, chip in enumerate(order)}
        self.rounds = chips // 2
        ahead, spots = [], np.zeros((dp_size, chips), np.int32)
        for device in range(dp_size):
            chip, core = divmod(device, 2)
            way = 1 if core == 0 else -1
            ahead.append((device, 2 * order[(place[chip] + way) % chips] + core))
            spots[device] = [order[(place[chip] + way * s) % chips] for s in range(chips)]
        self.ahead = ahead
        self.back = [(there, here) for here, there in ahead]
        self.swap = [(d, d ^ 1) for d in range(dp_size)]
        dp_index = lax.axis_index("dp")
        self.core = dp_index % 2
        self.spot = lax.dynamic_index_in_dim(jnp.asarray(spots), dp_index, 0, keepdims=False)

    def round(self, forth, back):
        if back is None:
            return [lax.ppermute(forth, "dp", self.ahead)]
        return [lax.ppermute(forth, "dp", self.ahead), lax.ppermute(back, "dp", self.back)]

    def partner(self, array):
        return lax.ppermute(array, "dp", self.swap)

    def across(self, array):
        return lax.ppermute(array, "tensor", [(0, 1), (1, 0)])

    def half(self, array, axis, mine):
        width = array.shape[axis] // 2
        index = self.core if mine else 1 - self.core
        return lax.dynamic_slice_in_dim(array, index * width, width, axis)

    def ordered(self, mine, other, axis):
        return jnp.where(
            self.core == 0,
            jnp.concatenate([mine, other], axis),
            jnp.concatenate([other, mine], axis),
        )

    def chip_piece(self, shard):
        mine, other = shard
        return self.ordered(mine, self.partner(other), 0)

    def gather_ring(self, piece, extra=None):
        chip_rows = piece.shape[0]
        if extra is not None:
            tail = jnp.zeros((8, piece.shape[1]), piece.dtype)
            pair = self.ordered(extra, self.partner(extra), 0)
            tail = lax.dynamic_update_slice(tail, pair[None, :], (0, 0))
            piece = jnp.concatenate([piece, tail], 0)
        piece = yield piece
        forth, back = [piece], [piece]
        for step in range(1, self.rounds + 1):
            both_ways = step < self.chips - self.rounds
            came = yield self.round(forth[-1], back[-1] if both_ways else None)
            forth.append(came[0])
            back += came[1:]
        blocks = [0] + [self.chips - s for s in range(1, len(forth))] + list(range(1, len(back)))
        whole, vector = place_pieces(self.spot[np.array(blocks)], forth + back[1:], chip_rows)
        halves = (whole, self.partner(whole))
        return halves if extra is None else (halves, vector[:, 0, :chip_rows].reshape(-1))

    def own_half(self, terms, came):
        return [(term + part.astype(F32)).astype(BF16) for term, part in zip(terms, came)]

    def reduce_ring(self, sums):
        chip_rows = sums[0].shape[0] // self.chips

        def portion(ahead):
            start = self.spot[ahead % self.chips] * chip_rows
            return jnp.concatenate(
                [lax.dynamic_slice_in_dim(part, start, chip_rows, 0) for part in sums], 1
            )

        forth, back = portion(self.rounds), portion(1 + self.rounds)
        for step in range(1, self.rounds + 1):
            both_ways = step < self.chips - self.rounds
            came = yield self.round(forth, back if both_ways else None)
            if step < self.rounds:
                forth = (came[0].astype(F32) + portion(self.rounds - step).astype(F32)).astype(BF16)
            else:
                forth = came[0]
            if both_ways:
                back = came[1]
                if step + 1 < self.chips - self.rounds:
                    more = portion(1 + self.rounds + step)
                    back = (back.astype(F32) + more.astype(F32)).astype(BF16)
        return self.share_rows(portion(0).astype(F32) + forth.astype(F32) + back.astype(F32))

    def share_rows(self, total):
        mine = self.half(total, 0, True)
        other = self.partner(self.half(total, 0, False).astype(BF16)).astype(F32)
        return mine, other

    def rows_in(self, local_rows):
        if self.tensor_size == 2:
            return [local_rows, self.across(local_rows)]
        return [lax.all_gather(local_rows, "tensor", axis=0, tiled=True)]

    def rows_out(self, sums):
        if self.tensor_size == 2:
            return sums[0] + self.across(sums[1]).astype(F32)
        return lax.psum_scatter(sums[0], "tensor", scatter_dimension=0, tiled=True).astype(F32)

    def butterfly(self, array, border):
        for axis, size in (("dp", self.dp_size), ("tensor", self.tensor_size)):
            if axis == "tensor":
                array, kept = array[border:], array
            bit = 1
            while bit < size:
                pairs = [(i, i ^ bit) for i in range(size)]
                array = array + (yield lax.ppermute(array, axis, pairs))
                bit *= 2
        return kept, array


def owner_swap(rows):
    return lax.all_to_all(rows, "dp", split_axis=0, concat_axis=0, tiled=True)


class Task:
    def __init__(self, steps):
        self.steps, self.done, self.result = steps, False, None
        self.advance(None, first=True)

    def advance(self, arrived, first=False):
        try:
            self.pending = next(self.steps) if first else self.steps.send(arrived)
        except StopIteration as stop:
            self.done, self.result = True, stop.value

    def finish(self):
        while not self.done:
            self.advance(self.pending)
        return self.result


def tick(value, *tasks):
    tasks = [task for task in tasks if task is not None and not task.done]
    if not tasks:
        return value
    value, arrived = lax.optimization_barrier((value, [task.pending for task in tasks]))
    for task, part in zip(tasks, arrived):
        task.advance(part)
    return value


def tie(*values):
    return lax.optimization_barrier(values)


def place_pieces(source, pieces, chip_rows):
    count, width = len(pieces), pieces[0].shape[1]
    spare = pieces[0].shape[0] - chip_rows

    def kernel(source_ref, *refs):
        ins, outs, sems = refs[:count], refs[count:-1], refs[-1]
        copies = []
        for i, piece in enumerate(ins):
            rows = pl.ds(pl.multiple_of(source_ref[i] * chip_rows, chip_rows), chip_rows)
            copies.append(
                pltpu.make_async_copy(piece.at[0:chip_rows], outs[0].at[rows], sems.at[i, 0])
            )
            if spare:
                copies.append(
                    pltpu.make_async_copy(
                        piece.at[chip_rows : chip_rows + spare, 0:128],
                        outs[1].at[source_ref[i]],
                        sems.at[i, 1],
                    )
                )
        for copy in copies:
            copy.start()
        for copy in copies:
            copy.wait()

    shapes = [jax.ShapeDtypeStruct((count * chip_rows, width), BF16)]
    if spare:
        shapes.append(jax.ShapeDtypeStruct((count, spare, 128), BF16))
    outs = pl.pallas_call(
        kernel,
        out_shape=shapes,
        in_specs=[pl.BlockSpec(memory_space=pltpu.SMEM)]
        + [pl.BlockSpec(memory_space=pl.ANY)] * count,
        out_specs=[pl.BlockSpec(memory_space=pltpu.VMEM)] * len(shapes),
        scratch_shapes=[pltpu.SemaphoreType.DMA((count, 2))],
        compiler_params=pltpu.CompilerParams(vmem_limit_bytes=16 << 20),
        cost_estimate=pl.CostEstimate(
            flops=0, bytes_accessed=4 * count * pieces[0].size, transcendentals=0
        ),
        name="place_pieces",
    )(source, *pieces)
    return outs[0], (outs[1] if spare else None)


def erf(x):
    x = jnp.clip(x, -3.7439211627767994, 3.7439211627767994)
    s = x * x
    top = jnp.full_like(s, 0.00022905065861350646)
    for c in (0.0034082910107109506, 0.050955695062380861, 0.18520832239976145, 1.128379143519084):
        top = top * s + c
    low = jnp.full_like(s, -1.1791602954361697e-7)
    for c in (
        0.000023547966471313185,
        0.0010179625278914885,
        0.014070470171167667,
        0.11098505178285362,
        0.49746925110067538,
        1.0,
    ):
        low = low * s + c
    return x * top / low


def whole_spec(shape):
    return pl.BlockSpec(shape, lambda *_: (0,) * len(shape))


def attend_forward(blocks, weight, bias, segment, earlier=None):
    rows = sum(block.shape[0] for block in blocks)
    inner = weight.shape[1] // 4
    heads = inner // HEAD
    step = min(512, rows)
    scale = 1.0 / math.sqrt(HEAD)
    extra = 0 if earlier is None else 2

    def kernel(*refs):
        xs, refs = refs[: len(blocks)], refs[len(blocks) :]
        w_ref, bias_ref, col_ref, row_ref = refs[:4]
        before, refs = refs[4 : 4 + extra], refs[4 + extra :]
        qkv_ref, out_ref, log_ref = refs[:3]
        start = 0
        for x in xs:
            size = x.shape[0]
            projected = dot(x[...], w_ref[:, : 3 * inner]) + bias_ref[...]
            qkv_ref[start : start + size, :] = projected.astype(BF16)
            start += size
        for first in range(0, rows, step):
            part = slice(first, first + step)
            far = jnp.where(col_ref[...] == row_ref[:, part], 0.0, -1e30)
            mixed = []
            for h in range(heads):
                lanes = [slice(i * inner + h * HEAD, i * inner + (h + 1) * HEAD) for i in range(3)]
                scores = times_transposed(qkv_ref[:, lanes[1]], qkv_ref[part, lanes[0]])
                scores = scores * scale + far
                highest = jnp.max(scores, axis=0, keepdims=True)
                powers = jnp.exp(scores - highest)
                summed = jnp.sum(powers, axis=0, keepdims=True)
                mixture = contract_rows(qkv_ref[:, lanes[2]], powers.astype(BF16))
                mixed.append(mixture * (1.0 / summed))
                log_ref[h : h + 1, part] = highest + jnp.log(summed)
            out_ref[part, :] = jnp.concatenate(mixed, 0).T.astype(BF16)
        start = 0
        for sum_ref in refs[3:]:
            part = slice(start, start + sum_ref.shape[0])
            start += sum_ref.shape[0]
            total = times_transposed(before[0][part, :], before[1][:, 3 * inner :])
            total += times_transposed(out_ref[part, :], w_ref[:, 3 * inner :])
            sum_ref[...] = total.astype(sum_ref.dtype)

    shapes = [
        jax.ShapeDtypeStruct((rows, 3 * inner), BF16),
        jax.ShapeDtypeStruct((rows, inner), BF16),
        jax.ShapeDtypeStruct((heads, rows), F32),
    ]
    if earlier is not None:
        shapes += sum_shapes(blocks)
    outs = pl.pallas_call(
        kernel,
        out_shape=shapes,
        compiler_params=pltpu.CompilerParams(vmem_limit_bytes=56 << 20),
        cost_estimate=pl.CostEstimate(
            flops=2 * rows * (D * 3 * inner + 2 * rows * inner) + extra * rows * D * 2 * inner,
            bytes_accessed=2 * (rows + 4 * inner) * D,
            transcendentals=heads * rows**2,
        ),
        name="attend_forward",
    )(*blocks, weight, bias[None], segment[:, None], segment[None], *(earlier or ()))
    return tuple(outs[:3]), list(outs[3:])


def sum_shapes(blocks):
    kinds = (F32, BF16) if len(blocks) == 2 else (BF16,)
    return [jax.ShapeDtypeStruct(block.shape, kind) for block, kind in zip(blocks, kinds)]


def attend_backward(blocks, weight, qkv, mixture, log_total, segment, earlier=None):
    rows = sum(block.shape[0] for block in blocks)
    inner = weight.shape[1] // 4
    extra = 0 if earlier is None else 2
    heads = inner // HEAD
    step = min(512, rows)
    scale = 1.0 / math.sqrt(HEAD)

    def kernel(*refs):
        xs = refs[: len(blocks)]
        (w_ref, qkv_ref, mix_ref, log_ref, col_ref, row_ref) = refs[len(blocks) : len(blocks) + 6]
        refs = refs[len(blocks) + 6 :]
        before, refs = refs[:extra], refs[extra:]
        grad_ref, sum_ref, dout_ref = refs[0], refs[1], refs[-1]
        start = 0
        for x in xs:
            size = x.shape[0]
            dout_ref[start : start + size, :] = dot(x[...], w_ref[:, 3 * inner :]).astype(BF16)
            start += size
        ones = jnp.ones((8, HEAD), F32)
        keys = [jnp.zeros((rows, HEAD), F32)] * heads
        values = [jnp.zeros((rows, HEAD), F32)] * heads
        for first in range(0, rows, step):
            part = slice(first, first + step)
            far = jnp.where(col_ref[...] == row_ref[:, part], 0.0, -1e30)
            queries = []
            for h in range(heads):
                lanes = [slice(i * inner + h * HEAD, i * inner + (h + 1) * HEAD) for i in range(3)]
                query, key = qkv_ref[part, lanes[0]], qkv_ref[:, lanes[1]]
                dout = dout_ref[part, lanes[0]]
                scores = times_transposed(key, query) * scale + far
                weights = jnp.exp(scores - log_ref[h : h + 1, part])
                product = dout.astype(F32) * mix_ref[part, lanes[0]].astype(F32)
                centre = lax.dot_general(
                    ones,
                    product,
                    (((1,), (1,)), ((), ())),
                    precision=lax.Precision.HIGHEST,
                    preferred_element_type=F32,
                )[0:1]
                grad_weights = times_transposed(qkv_ref[:, lanes[2]], dout)
                grad_scores = (weights * (grad_weights - centre)).astype(BF16)
                queries.append(contract_rows(key, grad_scores))
                keys[h] = keys[h] + dot(grad_scores, query)
                values[h] = values[h] + dot(weights.astype(BF16), dout)
            grad_ref[part, 0:inner] = (jnp.concatenate(queries, 0).T * scale).astype(BF16)
        for h in range(heads):
            grad_ref[:, inner + h * HEAD : inner + (h + 1) * HEAD] = (keys[h] * scale).astype(BF16)
            grad_ref[:, 2 * inner + h * HEAD : 2 * inner + (h + 1) * HEAD] = values[h].astype(BF16)
        sum_ref[...] = jnp.sum(grad_ref[...].astype(F32), axis=0, keepdims=True)
        start = 0
        for out_ref in refs[2:-1]:
            part = slice(start, start + out_ref.shape[0])
            start += out_ref.shape[0]
            total = times_transposed(before[0][part, :], before[1][:, : 3 * inner])
            total += times_transposed(grad_ref[part, :], w_ref[:, : 3 * inner])
            out_ref[...] = total.astype(out_ref.dtype)

    flops = 2 * rows * (D * inner + 5 * rows * inner) + extra * rows * D * 6 * inner
    shapes = [
        jax.ShapeDtypeStruct((rows, 3 * inner), BF16),
        jax.ShapeDtypeStruct((1, 3 * inner), F32),
    ]
    if earlier is not None:
        shapes += sum_shapes(blocks)
    outs = pl.pallas_call(
        kernel,
        out_shape=shapes,
        scratch_shapes=[pltpu.VMEM((rows, inner), BF16)],
        compiler_params=pltpu.CompilerParams(vmem_limit_bytes=56 << 20),
        cost_estimate=pl.CostEstimate(
            flops=flops, bytes_accessed=2 * (rows + inner) * D, transcendentals=heads * rows**2
        ),
        name="attend_backward",
    )(*blocks, weight, qkv, mixture, log_total, segment[:, None], segment[None], *(earlier or ()))
    return outs[0], outs[1], list(outs[2:])


def feed(source, weights, side, block, rows_all, filled, out_type, forward):
    rows = source.shape[0]
    hidden = weights[0].shape[1] // 2
    tile = min(512, hidden)
    tiles = hidden // tile
    row_tile = min(256, rows)
    inner_count = 2 if forward else 1
    given = 0 if filled is None else inner_count

    def kernel(x_ref, a_own, a_part, b_own, b_part, side_ref, *refs):
        refs = refs[given:]
        out_ref, inner_refs, refs = refs[0], refs[1 : 1 + inner_count], refs[1 + inner_count :]
        total_ref = refs[-1]
        index = pl.program_id(1)

        def run(a_ref, b_ref):
            pre = dot(x_ref[...], a_ref[...])
            if forward:
                pre = pre + side_ref[...]
                cdf = 0.5 + 0.5 * erf(pre * 0.7071067811865476)
                bell = jnp.exp(-0.5 * pre * pre) * 0.3989422804014327
                kept = (pre * cdf).astype(BF16)
                inner_refs[0][...] = kept
                inner_refs[1][...] = (cdf + pre * bell).astype(BF16)
            else:
                kept = (pre * side_ref[...].astype(F32)).astype(BF16)
                inner_refs[0][...] = kept
                refs[0][...] = jnp.sum(kept.astype(F32), axis=0, keepdims=True)[None]
            term = times_transposed(kept, b_ref[...])

            @pl.when(index == 0)
            def _():
                total_ref[...] = term

            @pl.when(index > 0)
            def _():
                total_ref[...] += term

        @pl.when(index < tiles)
        def _():
            run(a_own, b_own)

        @pl.when(index >= tiles)
        def _():
            run(a_part, b_part)

        @pl.when(index == 2 * tiles - 1)
        def _():
            out_ref[...] = total_ref[...].astype(out_type)

    shift = block * (rows // row_tile)
    shifts = (0, tiles) if forward else (tiles, 0)
    owns = [
        pl.BlockSpec((D, tile), lambda r, i, k=k: (0, jnp.minimum(i, tiles - 1) + k)) for k in shifts
    ]
    parts = [
        pl.BlockSpec((D, tile), lambda r, i, k=k: (0, jnp.maximum(i - tiles, 0) + k)) for k in shifts
    ]
    over = pl.BlockSpec((row_tile, tile), lambda r, i: (r + shift, i))
    source_spec = pl.BlockSpec((row_tile, D), lambda r, i: (r, 0))
    side_spec = pl.BlockSpec((1, tile), lambda r, i: (0, i)) if forward else over
    out_shape = [jax.ShapeDtypeStruct((rows, D), out_type)]
    out_shape += [jax.ShapeDtypeStruct((rows_all, 2 * hidden), BF16)] * inner_count
    out_specs = [source_spec] + [over] * inner_count
    if not forward:
        out_shape.append(jax.ShapeDtypeStruct((rows // row_tile, 1, 2 * hidden), F32))
        out_specs.append(pl.BlockSpec((1, 1, tile), lambda r, i: (r, 0, i)))
    outs = pl.pallas_call(
        kernel,
        grid=(rows // row_tile, 2 * tiles),
        out_shape=out_shape,
        in_specs=[source_spec, owns[0], parts[0], owns[1], parts[1], side_spec]
        + [pl.BlockSpec(memory_space=pl.ANY)] * given,
        out_specs=out_specs,
        scratch_shapes=[pltpu.VMEM((row_tile, D), F32)],
        input_output_aliases={6 + i: 1 + i for i in range(given)},
        compiler_params=pltpu.CompilerParams(vmem_limit_bytes=60 << 20),
        cost_estimate=pl.CostEstimate(
            flops=8 * rows * D * hidden,
            bytes_accessed=8 * D * hidden,
            transcendentals=2 * rows * hidden if forward else 0,
        ),
        name="feed_forward" if forward else "feed_backward",
    )(source, *weights, *weights, side, *(filled or ()))
    return outs


def join(blocks):
    return blocks[0] if len(blocks) == 1 else jnp.concatenate(blocks, 0)


def body(
    tokens,
    cotangent,
    deal_slot,
    back_slot,
    lengths,
    time_step,
    time_table,
    w_qkv,
    b_qv,
    w_out,
    out_bias,
    ln_gain,
    ln_shift,
    w_ff1,
    b_ff1,
    w_ff2,
):
    wires = Wires(lax.axis_size("dp"), lax.axis_size("tensor"))
    rows_dev = tokens.shape[0]
    group_rows = rows_dev * wires.tensor_size
    tensor_index = lax.axis_index("tensor")
    layer_total = w_qkv.shape[0]
    inner = w_qkv.shape[3] // 2
    hidden = w_ff1.shape[2] // 2
    both = (True, False)

    time_piece = lax.dynamic_index_in_dim(time_table, time_step[0], 0, keepdims=False)

    def rings(layer, arrays, extra):
        w_qkv, w_out, w_ff1, w_ff2 = arrays
        attn_shard, feed_shard = [], []
        for mine in both:
            qkv = wires.half(w_qkv[layer], 2, mine)
            out = wires.half(w_out[layer], 0, mine).T
            attn_shard.append(jnp.concatenate([qkv[0], qkv[1], qkv[2], out], axis=1))
            first = wires.half(w_ff1[layer], 1, mine)
            second = wires.half(w_ff2[layer], 0, mine).T
            feed_shard.append(jnp.concatenate([first, second], axis=1))
        return (
            Task(wires.gather_ring(wires.chip_piece(attn_shard), extra)),
            Task(wires.gather_ring(wires.chip_piece(feed_shard))),
        )

    arrays = (w_qkv, w_out, w_ff1, w_ff2)
    attn_rings, feed_rings = [None] * (layer_total + 1), [None] * (layer_total + 1)
    attn_rings[0], feed_rings[0] = rings(0, arrays, time_piece)
    step = 0
    while not attn_rings[0].done:
        beside = (attn_rings[0], feed_rings[0] if step % 2 else None)
        if step == 0:
            tokens, back_slot = tick((tokens, back_slot), *beside)
            own_tokens = owner_swap(jnp.take(tokens, back_slot, axis=0))
        elif step == 2:
            own_tokens = tick(own_tokens, *beside)
            token_blocks = wires.rows_in(own_tokens)
        else:
            tick((), *beside)
        step += 1
    attn_w, time_row = attn_rings[0].result
    time_row, *arrays = tie(time_row, *arrays)
    for layer in range(1, layer_total):
        attn_rings[layer], feed_rings[layer] = rings(layer, arrays, None)
    time_row = time_row.astype(F32)

    seq_ends = jnp.cumsum(lengths[0])
    positions = jnp.arange(group_rows, dtype=jnp.int32)
    if wires.tensor_size == 2:
        positions = (positions + tensor_index * rows_dev) % group_rows
    segment = jnp.sum((positions[:, None] >= seq_ends[None, :]).astype(jnp.int32), axis=1)

    stream = own_tokens.astype(F32) + time_row
    weights, saved = [], []
    for layer in range(layer_total):
        if layer == 0:
            input_blocks = [(rows.astype(F32) + time_row).astype(BF16) for rows in token_blocks]
        else:
            now = (attn_rings[layer], feed_rings[layer])
            input_blocks = wires.rows_in(tick(stream.astype(BF16), *now))
            input_blocks[-1] = tick(input_blocks[-1], *now)
            attn_w = attn_rings[layer].finish()
        ahead = (attn_rings[layer + 1], feed_rings[layer + 1])
        biases = []
        for mine in both:
            bias_q, bias_v = [wires.half(b_qv[layer, i], 0, mine) for i in (0, 1)]
            biases.append(jnp.concatenate([bias_q, jnp.zeros_like(bias_q), bias_v]))
        (qkv, mixture, log_total), _ = attend_forward(input_blocks, attn_w[0], biases[0], segment)
        if layer == 0:
            mixture = tick(mixture, feed_rings[0])
        attention = [(qkv, mixture, log_total)]
        part, sums = attend_forward(
            input_blocks, attn_w[1], biases[1], segment, (mixture, attn_w[0])
        )
        attention.append(part)
        sums[-1] = tick(sums[-1], feed_rings[layer])
        middle = stream + wires.rows_out(sums) + out_bias[layer, 0]
        normed = layer_norm(middle, ln_gain[layer, 0], ln_shift[layer, 0])
        normed_low = tick(normed.astype(BF16), feed_rings[layer], ahead[0])
        normed_blocks = wires.rows_in(normed_low)
        normed_blocks[-1] = tick(normed_blocks[-1], ahead[0])
        feed_w = feed_rings[layer].finish()
        weights.append((attn_w, feed_w))
        bias = jnp.concatenate([wires.half(b_ff1[layer], 0, mine) for mine in both])[None]
        sums, filled = [], None
        for block, rows in enumerate(normed_blocks):
            kind = F32 if block == 0 and wires.tensor_size == 2 else BF16
            total, *filled = feed(rows, feed_w, bias, block, group_rows, filled, kind, True)
            sums.append(total)
        sums[-1] = tick(sums[-1], *ahead)
        second_sum = normed + wires.rows_out(sums) + out_bias[layer, 1]
        saved.append((input_blocks, attention, middle, normed_blocks, filled, second_sum))
        stream = layer_norm(second_sum, ln_gain[layer, 1], ln_shift[layer, 1])
        if layer == 0:
            stream, cotangent = tie(stream, cotangent)
            upstream = owner_swap(jnp.take(cotangent, back_slot, axis=0))

    encoded_own = stream.astype(BF16)
    gradient = upstream.astype(F32)
    feed_tasks, attn_tasks = [None] * (layer_total + 1), [None] * (layer_total + 1)
    attn_sums = None
    vector_grads = [None] * layer_total
    for layer in reversed(range(layer_total)):
        attn_w, feed_w = weights[layer]
        input_blocks, attention, middle, normed_blocks, (act, slope), second_sum = saved[layer]
        _, pull_second = jax.vjp(layer_norm, second_sum, ln_gain[layer, 1], ln_shift[layer, 1])
        grad_second, gain_second, shift_second = pull_second(gradient)
        later = (feed_tasks[layer + 1], attn_tasks[layer + 1])
        branch_blocks = wires.rows_in(tick(grad_second.astype(BF16), later[0]))
        if attn_sums is not None:
            branch_blocks[-1], attn_sums = tie(branch_blocks[-1], attn_sums)
            branch_blocks[-1] = tick(branch_blocks[-1], later[0])
            attn_tasks[layer + 1] = Task(wires.reduce_ring(attn_sums))
            later = (later[0], attn_tasks[layer + 1])
        sums, hidden_sums, filled = [], [], None
        for block, rows in enumerate(branch_blocks):
            kind = F32 if block == 0 and wires.tensor_size == 2 else BF16
            total, grad_pre, more = feed(rows, feed_w, slope, block, group_rows, filled, kind, False)
            filled = (grad_pre,)
            sums.append(total)
            hidden_sums.append(more)
        hidden_sums = sum(jnp.sum(part, axis=(0, 1)) for part in hidden_sums)
        if layer == layer_total - 1:
            sums[-1], encoded_own = tie(sums[-1], encoded_own)
            returned_out = owner_swap(encoded_own)
        sums[-1] = tick(sums[-1], *later)
        normed_all, branch_all = join(normed_blocks), join(branch_blocks)

        def feed_terms(half):
            columns = slice(half * hidden, (half + 1) * hidden)
            return [
                contract_rows(normed_all, grad_pre[:, columns]),
                contract_rows(branch_all, act[:, columns]),
            ]

        came = [wires.partner(term.astype(BF16)) for term in feed_terms(1)]
        grad_normed = grad_second + wires.rows_out(sums)
        grad_normed, came = tie(grad_normed, came)
        _, pull_first = jax.vjp(layer_norm, middle, ln_gain[layer, 0], ln_shift[layer, 0])
        grad_middle, gain_first, shift_first = pull_first(grad_normed)
        attend_blocks = wires.rows_in(tick(grad_middle.astype(BF16), later[1]))
        feed_sums = wires.own_half(feed_terms(0), came)
        attend_blocks[-1], feed_sums = tie(attend_blocks[-1], feed_sums)
        attend_blocks[-1] = tick(attend_blocks[-1], later[1])
        feed_tasks[layer] = Task(wires.reduce_ring(feed_sums))
        input_all, attend_all = join(input_blocks), join(attend_blocks)

        def attn_terms(half, wide):
            return [
                contract_rows(input_all, wide),
                contract_rows(attend_all, attention[half][1]),
            ]

        wide, part_sums, _ = attend_backward(attend_blocks, attn_w[1], *attention[1], segment)
        sends = [term.astype(BF16) for term in attn_terms(1, wide)]
        if layer == 0:
            wide, sends = tie(wide, sends)
        came = [wires.partner(term) for term in sends]
        own_wide, own_sums, sums = attend_backward(
            attend_blocks, attn_w[0], *attention[0], segment, (wide, attn_w[1])
        )
        sums[-1] = tick(sums[-1], feed_tasks[layer], later[1])
        gradient = grad_middle + wires.rows_out(sums)
        attn_sums = wires.own_half(attn_terms(0, own_wide), came)
        qkv_sums = [part.reshape(3, inner)[::2] for part in (own_sums, part_sums)]
        vector_grads[layer] = (
            wires.ordered(qkv_sums[0], qkv_sums[1], 1),
            wires.ordered(hidden_sums[:hidden], hidden_sums[hidden:], 0),
            jnp.stack([jnp.sum(grad_middle, axis=0), jnp.sum(grad_second, axis=0)]),
            jnp.stack([gain_first, gain_second]),
            jnp.stack([shift_first, shift_second]),
        )

    attn_tasks[0] = Task(wires.reduce_ring(attn_sums))
    returned_grad = owner_swap(gradient.astype(BF16))
    time_grad = jnp.sum(gradient, axis=0)
    local = [jnp.stack([part[i] for part in vector_grads]) for i in range(5)]
    flat = jnp.concatenate([part.reshape(-1) for part in local[:2] + [time_grad] + local[2:]])
    border = local[0].size + local[1].size
    vector_task = Task(wires.butterfly(flat, border))
    final = (attn_tasks[0], feed_tasks[0], vector_task)
    while not all(task.done for task in final):
        tick((), *final)
    reduced = [
        (attn_tasks[layer].finish(), feed_tasks[layer].finish()) for layer in range(layer_total)
    ]
    flat, shared = vector_task.result
    grad_tokens = jnp.take(returned_grad, deal_slot, axis=0)
    encoded = jnp.take(returned_out, deal_slot, axis=0)
    matrix_grads = []
    for attn_pair, feed_pair in reduced:
        rows = attn_pair[0].shape[0]
        matrix_grads.append(
            (
                wires.ordered(
                    *(
                        part[:, : 3 * inner].reshape(rows, 3, inner).transpose(1, 0, 2)
                        for part in attn_pair
                    ),
                    2,
                ),
                wires.ordered(*(part[:, 3 * inner :].T for part in attn_pair), 0),
                wires.ordered(*(part[:, :hidden] for part in feed_pair), 1),
                wires.ordered(*(part[:, hidden:].T for part in feed_pair), 0),
            )
        )
    grad_b_qv = flat[: local[0].size].reshape(local[0].shape)
    grad_b_ff1 = flat[local[0].size : border].reshape(local[1].shape)
    time_grad = shared[:D]
    rest = shared[D:].reshape(3, layer_total, 2, D)
    return (
        encoded,
        grad_tokens,
        time_grad,
        jnp.stack([part[0] for part in matrix_grads]),
        grad_b_qv,
        jnp.stack([part[1] for part in matrix_grads]),
        rest[0],
        rest[1],
        rest[2],
        jnp.stack([part[2] for part in matrix_grads]),
        grad_b_ff1,
        jnp.stack([part[3] for part in matrix_grads]),
    )


def solution(mesh):
    return jax.shard_map(
        body,
        mesh=mesh,
        in_specs=(
            P(("dp", "tensor"), None),
            P(("dp", "tensor"), None),
            P(("dp", "tensor")),
            P(("dp", "tensor")),
            P("dp", None),
            P(),
            P(None, "dp"),
            P(None, None, "dp", "tensor"),
            P(None, None, "tensor"),
            P(None, "tensor", "dp"),
            P(),
            P(),
            P(),
            P(None, "dp", "tensor"),
            P(None, "tensor"),
            P(None, "tensor", "dp"),
        ),
        out_specs=(
            P(("dp", "tensor"), None),
            P(("dp", "tensor"), None),
            P(),
            P(None, None, "dp", "tensor"),
            P(None, None, "tensor"),
            P(None, "tensor", "dp"),
            P(),
            P(),
            P(),
            P(None, "dp", "tensor"),
            P(None, "tensor"),
            P(None, "tensor", "dp"),
        ),
        check_vma=False,
    )
```

```python
import math

import jax
import jax.numpy as jnp
import numpy as np
from jax import lax
from jax.experimental import pallas as pl
from jax.experimental.pallas import tpu as pltpu
from jax.sharding import PartitionSpec as P

D = 1024
HEADS = 16
FF = 4096
HEAD = D // HEADS
F32 = jnp.float32
BF16 = jnp.bfloat16


def layer_norm(summed, scaling, offset_vec):
    centre = jnp.mean(summed, axis=-1, keepdims=True)
    spread = summed - centre
    variance = jnp.mean(spread * spread, axis=-1, keepdims=True)
    return spread * lax.rsqrt(variance + 1e-05) * scaling + offset_vec


def dot(left, right):
    return jnp.dot(left, right, preferred_element_type=F32)


def contract_rows(left, right):
    return lax.dot_general(left, right, (((0,), (0,)), ((), ())), preferred_element_type=F32)


def times_transposed(left, right):
    return lax.dot_general(left, right, (((1,), (1,)), ((), ())), preferred_element_type=F32)


class Wires:
    def __init__(self, dp_size, tensor_size):
        self.dp_size, self.tensor_size = dp_size, tensor_size
        chips = dp_size // 2
        self.chips = chips
        order = list(range(0, chips, 2)) + list(range(chips - 1, 0, -2))
        place = {chip: spot for spot, chip in enumerate(order)}
        self.rounds = chips // 2
        ahead, spots = [], np.zeros((dp_size, chips), np.int32)
        for device in range(dp_size):
            chip, core = divmod(device, 2)
            way = 1 if core == 0 else -1
            ahead.append((device, 2 * order[(place[chip] + way) % chips] + core))
            spots[device] = [order[(place[chip] + way * s) % chips] for s in range(chips)]
        self.ahead = ahead
        self.back = [(there, here) for here, there in ahead]
        self.swap = [(d, d ^ 1) for d in range(dp_size)]
        dp_index = lax.axis_index("dp")
        self.core = dp_index % 2
        self.spot = lax.dynamic_index_in_dim(jnp.asarray(spots), dp_index, 0, keepdims=False)

    def round(self, forth, back):
        if back is None:
            return [lax.ppermute(forth, "dp", self.ahead)]
        return [lax.ppermute(forth, "dp", self.ahead), lax.ppermute(back, "dp", self.back)]

    def partner(self, array):
        return lax.ppermute(array, "dp", self.swap)

    def across(self, array):
        return lax.ppermute(array, "tensor", [(0, 1), (1, 0)])

    def half(self, array, axis, mine):
        width = array.shape[axis] // 2
        index = self.core if mine else 1 - self.core
        return lax.dynamic_slice_in_dim(array, index * width, width, axis)

    def ordered(self, mine, other, axis):
        return jnp.where(
            self.core == 0,
            jnp.concatenate([mine, other], axis),
            jnp.concatenate([other, mine], axis),
        )

    def chip_piece(self, shard):
        mine, other = shard
        return self.ordered(mine, self.partner(other), 0)

    def gather_ring(self, piece, extra=None):
        chip_rows = piece.shape[0]
        if extra is not None:
            tail = jnp.zeros((8, piece.shape[1]), piece.dtype)
            pair = self.ordered(extra, self.partner(extra), 0)
            tail = lax.dynamic_update_slice(tail, pair[None, :], (0, 0))
            piece = jnp.concatenate([piece, tail], 0)
        piece = yield piece
        forth, back = [piece], [piece]
        for step in range(1, self.rounds + 1):
            both_ways = step < self.chips - self.rounds
            came = yield self.round(forth[-1], back[-1] if both_ways else None)
            forth.append(came[0])
            back += came[1:]
        blocks = [0] + [self.chips - s for s in range(1, len(forth))] + list(range(1, len(back)))
        whole, vector = place_pieces(self.spot, blocks, forth + back[1:], chip_rows)
        halves = (whole, self.partner(whole))
        return halves if extra is None else (halves, vector[:, 0, :chip_rows].reshape(-1))

    def reduce_ring(self, sums):
        chip_rows = sums.shape[0] // self.chips

        def portion(ahead):
            start = self.spot[ahead % self.chips] * chip_rows
            return lax.dynamic_slice_in_dim(sums, start, chip_rows, 0)

        forth, back = portion(self.rounds), portion(1 + self.rounds)
        for step in range(1, self.rounds + 1):
            both_ways = step < self.chips - self.rounds
            came = yield self.round(forth, back if both_ways else None)
            places = [self.rounds - step] if step < self.rounds else []
            if step + 1 < self.chips - self.rounds:
                places.append(1 + self.rounds + step)
            added = add_portions(self.spot, places, came, sums) if places else []
            forth = added[0] if step < self.rounds else came[0]
            if both_ways:
                back = added[1] if len(places) == 2 else came[1]
        return self.share_rows(portion(0).astype(F32) + forth.astype(F32) + back.astype(F32))

    def share_rows(self, total):
        mine = self.half(total, 0, True)
        other = self.partner(self.half(total, 0, False).astype(BF16)).astype(F32)
        return mine, other

    def rows_in(self, local_rows):
        if self.tensor_size == 2:
            return [local_rows, self.across(local_rows)]
        return [lax.all_gather(local_rows, "tensor", axis=0, tiled=True)]

    def rows_out(self, sums):
        if self.tensor_size == 2:
            return sums[0] + self.across(sums[1]).astype(F32)
        return lax.psum_scatter(sums[0], "tensor", scatter_dimension=0, tiled=True).astype(F32)

    def butterfly(self, array, border):
        for axis, size in (("dp", self.dp_size), ("tensor", self.tensor_size)):
            if axis == "tensor":
                array, kept = array[border:], array
            bit = 1
            while bit < size:
                pairs = [(i, i ^ bit) for i in range(size)]
                array = array + (yield lax.ppermute(array, axis, pairs))
                bit *= 2
        return kept, array


def owner_swap(rows):
    return lax.all_to_all(rows, "dp", split_axis=0, concat_axis=0, tiled=True)


class Task:
    def __init__(self, steps):
        self.steps, self.done, self.result = steps, False, None
        self.advance(None, first=True)

    def advance(self, arrived, first=False):
        try:
            self.pending = next(self.steps) if first else self.steps.send(arrived)
        except StopIteration as stop:
            self.done, self.result = True, stop.value

    def finish(self):
        while not self.done:
            self.advance(self.pending)
        return self.result


def tick(value, *tasks):
    tasks = [task for task in tasks if task is not None and not task.done]
    if not tasks:
        return value
    value, arrived = lax.optimization_barrier((value, [task.pending for task in tasks]))
    for task, part in zip(tasks, arrived):
        task.advance(part)
    return value


def tie(*values):
    return lax.optimization_barrier(values)


def place_pieces(spot, places, pieces, chip_rows):
    count, width = len(pieces), pieces[0].shape[1]
    spare = pieces[0].shape[0] - chip_rows

    def kernel(spot_ref, *refs):
        ins, outs, sems = refs[:count], refs[count:-1], refs[-1]
        copies = []
        for i, piece in enumerate(ins):
            chip = spot_ref[places[i]]
            rows = pl.ds(pl.multiple_of(chip * chip_rows, chip_rows), chip_rows)
            copies.append(
                pltpu.make_async_copy(piece.at[0:chip_rows], outs[0].at[rows], sems.at[i, 0])
            )
            if spare:
                copies.append(
                    pltpu.make_async_copy(
                        piece.at[chip_rows : chip_rows + spare, 0:128],
                        outs[1].at[chip],
                        sems.at[i, 1],
                    )
                )
        for copy in copies:
            copy.start()
        for copy in copies:
            copy.wait()

    shapes = [jax.ShapeDtypeStruct((count * chip_rows, width), BF16)]
    if spare:
        shapes.append(jax.ShapeDtypeStruct((count, spare, 128), BF16))
    outs = pl.pallas_call(
        kernel,
        out_shape=shapes,
        in_specs=[pl.BlockSpec(memory_space=pltpu.SMEM)]
        + [pl.BlockSpec(memory_space=pl.ANY)] * count,
        out_specs=[pl.BlockSpec(memory_space=pltpu.VMEM)] * len(shapes),
        scratch_shapes=[pltpu.SemaphoreType.DMA((count, 2))],
        compiler_params=pltpu.CompilerParams(vmem_limit_bytes=16 << 20),
        cost_estimate=pl.CostEstimate(
            flops=0, bytes_accessed=4 * count * pieces[0].size, transcendentals=0
        ),
        name="place_pieces",
    )(spot, *pieces)
    return outs[0], (outs[1] if spare else None)


def attend_forward(blocks, weight, bias, segment, earlier=None):
    rows = sum(block.shape[0] for block in blocks)
    inner = weight.shape[1] // 4
    heads = inner // HEAD
    step = min(512, rows)
    scale = 1.0 / math.sqrt(HEAD)
    extra = 0 if earlier is None else 2

    def kernel(*refs):
        xs, refs = refs[: len(blocks)], refs[len(blocks) :]
        w_ref, bias_ref, col_ref, row_ref = refs[:4]
        before, refs = refs[4 : 4 + extra], refs[4 + extra :]
        qkv_ref, out_ref, log_ref = refs[:3]
        start = 0
        for x in xs:
            size = x.shape[0]
            projected = dot(x[...], w_ref[:, : 3 * inner]) + bias_ref[...]
            qkv_ref[start : start + size, :] = projected.astype(BF16)
            start += size
        for first in range(0, rows, step):
            part = slice(first, first + step)
            far = jnp.where(col_ref[...] == row_ref[:, part], 0.0, -1e30)
            mixed = []
            for h in range(heads):
                lanes = [slice(i * inner + h * HEAD, i * inner + (h + 1) * HEAD) for i in range(3)]
                scores = times_transposed(qkv_ref[:, lanes[1]], qkv_ref[part, lanes[0]])
                scores = scores * scale + far
                highest = jnp.max(scores, axis=0, keepdims=True)
                powers = jnp.exp(scores - highest)
                summed = jnp.sum(powers, axis=0, keepdims=True)
                mixture = contract_rows(qkv_ref[:, lanes[2]], powers.astype(BF16))
                mixed.append(mixture * (1.0 / summed))
                log_ref[h : h + 1, part] = highest + jnp.log(summed)
            out_ref[part, :] = jnp.concatenate(mixed, 0).T.astype(BF16)
        start = 0
        for sum_ref in refs[3:]:
            part = slice(start, start + sum_ref.shape[0])
            start += sum_ref.shape[0]
            total = times_transposed(before[0][part, :], before[1][:, 3 * inner :])
            total += times_transposed(out_ref[part, :], w_ref[:, 3 * inner :])
            sum_ref[...] = total.astype(sum_ref.dtype)

    shapes = [
        jax.ShapeDtypeStruct((rows, 3 * inner), BF16),
        jax.ShapeDtypeStruct((rows, inner), BF16),
        jax.ShapeDtypeStruct((heads, rows), F32),
    ]
    if earlier is not None:
        shapes += sum_shapes(blocks)
    outs = pl.pallas_call(
        kernel,
        out_shape=shapes,
        compiler_params=pltpu.CompilerParams(vmem_limit_bytes=32 << 20),
        cost_estimate=pl.CostEstimate(flops=1000, bytes_accessed=1000, transcendentals=0),
        name="attend_forward",
    )(*blocks, weight, bias[None], segment[:, None], segment[None], *(earlier or ()))
    return tuple(outs[:3]), list(outs[3:])


def sum_shapes(blocks):
    kinds = (F32, BF16) if len(blocks) == 2 else (BF16,)
    return [jax.ShapeDtypeStruct(block.shape, kind) for block, kind in zip(blocks, kinds)]


def attend_backward(blocks, weight, qkv, mixture, log_total, segment, earlier=None):
    rows = sum(block.shape[0] for block in blocks)
    inner = weight.shape[1] // 4
    extra = 0 if earlier is None else 2
    heads = inner // HEAD
    step = min(512, rows)
    scale = 1.0 / math.sqrt(HEAD)

    def kernel(*refs):
        xs = refs[: len(blocks)]
        (w_ref, qkv_ref, mix_ref, log_ref, col_ref, row_ref) = refs[len(blocks) : len(blocks) + 6]
        refs = refs[len(blocks) + 6 :]
        before, refs = refs[:extra], refs[extra:]
        grad_ref, sum_ref, dout_ref = refs[0], refs[1], refs[-1]
        start = 0
        for x in xs:
            size = x.shape[0]
            dout_ref[start : start + size, :] = dot(x[...], w_ref[:, 3 * inner :]).astype(BF16)
            start += size
        ones = jnp.ones((8, HEAD), F32)
        keys = [jnp.zeros((rows, HEAD), F32)] * heads
        values = [jnp.zeros((rows, HEAD), F32)] * heads
        for first in range(0, rows, step):
            part = slice(first, first + step)
            far = jnp.where(col_ref[...] == row_ref[:, part], 0.0, -1e30)
            queries = []
            for h in range(heads):
                lanes = [slice(i * inner + h * HEAD, i * inner + (h + 1) * HEAD) for i in range(3)]
                query, key = qkv_ref[part, lanes[0]], qkv_ref[:, lanes[1]]
                dout = dout_ref[part, lanes[0]]
                scores = times_transposed(key, query) * scale + far
                weights = jnp.exp(scores - log_ref[h : h + 1, part])
                product = dout.astype(F32) * mix_ref[part, lanes[0]].astype(F32)
                centre = lax.dot_general(
                    ones,
                    product,
                    (((1,), (1,)), ((), ())),
                    precision=lax.Precision.HIGHEST,
                    preferred_element_type=F32,
                )[0:1]
                grad_weights = times_transposed(qkv_ref[:, lanes[2]], dout)
                grad_scores = (weights * (grad_weights - centre)).astype(BF16)
                queries.append(contract_rows(key, grad_scores))
                keys[h] = keys[h] + dot(grad_scores, query)
                values[h] = values[h] + dot(weights.astype(BF16), dout)
            grad_ref[part, 0:inner] = (jnp.concatenate(queries, 0).T * scale).astype(BF16)
        for h in range(heads):
            grad_ref[:, inner + h * HEAD : inner + (h + 1) * HEAD] = (keys[h] * scale).astype(BF16)
            grad_ref[:, 2 * inner + h * HEAD : 2 * inner + (h + 1) * HEAD] = values[h].astype(BF16)
        sum_ref[...] = jnp.sum(grad_ref[...].astype(F32), axis=0, keepdims=True)
        start = 0
        for out_ref in refs[2:-1]:
            part = slice(start, start + out_ref.shape[0])
            start += out_ref.shape[0]
            total = times_transposed(before[0][part, :], before[1][:, : 3 * inner])
            total += times_transposed(grad_ref[part, :], w_ref[:, : 3 * inner])
            out_ref[...] = total.astype(out_ref.dtype)

    shapes = [
        jax.ShapeDtypeStruct((rows, 3 * inner), BF16),
        jax.ShapeDtypeStruct((1, 3 * inner), F32),
    ]
    if earlier is not None:
        shapes += sum_shapes(blocks)
    outs = pl.pallas_call(
        kernel,
        out_shape=shapes,
        scratch_shapes=[pltpu.VMEM((rows, inner), BF16)],
        compiler_params=pltpu.CompilerParams(vmem_limit_bytes=32 << 20),
        cost_estimate=pl.CostEstimate(flops=1000, bytes_accessed=1000, transcendentals=0),
        name="attend_backward",
    )(*blocks, weight, qkv, mixture, log_total, segment[:, None], segment[None], *(earlier or ()))
    return outs[0], outs[1], list(outs[2:])


def normal_parts(x):
    bell = jnp.exp(-0.5 * x * x)
    t = 1.0 / (1.0 + 0.23164189 * jnp.abs(x))
    tail = 0.5307027145
    for c in (-0.7265760135, 0.7107068705, -0.142248368, 0.127414796):
        tail = tail * t + c
    tail = tail * t * bell
    return jnp.where(x >= 0.0, 1.0 - tail, tail), bell * 0.3989422804014327


def feed(blocks, weights, side, forward):
    rows = sum(block.shape[0] for block in blocks)
    hidden = weights[0].shape[1] // 2
    tile = min(512, hidden)
    tiles = hidden // tile
    into, onto = (0, hidden) if forward else (hidden, 0)

    def kernel(*refs):
        xs, refs = refs[: len(blocks)], refs[len(blocks) :]
        *halves, side_ref = refs[:3]
        outs, (kept_ref, more_ref, pre_ref) = refs[3:-3], refs[-3:]

        def project(half, index):
            start, slot = 0, lax.rem(index, 2)
            first = index * tile + into
            if not isinstance(index, int):
                first = pl.multiple_of(first, tile)
            for x in xs:
                part = pl.ds(start, x.shape[0])
                pre_ref[slot, part, :] = dot(x[...], halves[half][:, pl.ds(first, tile)])
                start += x.shape[0]

        def activate(half, index):
            first = index * tile + half * hidden
            if not isinstance(index, int):
                first = pl.multiple_of(first, tile)
            columns = pl.ds(first, tile)
            pre = pre_ref[lax.rem(index, 2)]
            if forward:
                pre = pre + side_ref[:, columns]
                cdf, bell = normal_parts(pre)
                kept_ref[:, columns] = (pre * cdf).astype(BF16)
                more_ref[:, columns] = (cdf + pre * bell).astype(BF16)
            else:
                kept = (pre * side_ref[:, columns].astype(F32)).astype(BF16)
                kept_ref[:, columns] = kept
                more_ref[:, columns] = jnp.sum(kept.astype(F32), axis=0, keepdims=True)

        for half in (0, 1):
            project(half, 0)

            def step(index, _, half=half):
                project(half, index)
                activate(half, index - 1)
                return 0

            lax.fori_loop(1, tiles, step, 0)
            activate(half, tiles - 1)
        start = 0
        for out in outs:
            part = slice(start, start + out.shape[0])
            start += out.shape[0]
            total = times_transposed(kept_ref[part, 0:hidden], halves[0][:, onto : onto + hidden])
            total += times_transposed(kept_ref[part, hidden:], halves[1][:, onto : onto + hidden])
            out[...] = total.astype(out.dtype)

    wide = jax.ShapeDtypeStruct((rows, 2 * hidden), BF16)
    outs = pl.pallas_call(
        kernel,
        out_shape=sum_shapes(blocks)
        + [wide, wide if forward else jax.ShapeDtypeStruct((1, 2 * hidden), F32)],
        scratch_shapes=[pltpu.VMEM((2, rows, tile), F32)],
        compiler_params=pltpu.CompilerParams(vmem_limit_bytes=32 << 20),
        cost_estimate=pl.CostEstimate(flops=1000, bytes_accessed=1000, transcendentals=0),
        name="feed_forward" if forward else "feed_backward",
    )(*blocks, *weights, side)
    return list(outs[:-2]), outs[-2], outs[-1]


def weight_gradients(pairs, half, came=None):
    widths = [width for _, _, width in pairs]
    tile = math.gcd(256, *widths)
    if tile % 128:
        terms = [
            contract_rows(join(blocks), _columns(right, half, width))
            for blocks, right, width in pairs
        ]
        total = jnp.concatenate(terms, 1)
        return (total if came is None else total + came.astype(F32)).astype(BF16)
    counts = [width // tile for width in widths]
    edge = counts[0]
    blocks_flat = [block for blocks, _, _ in pairs for block in blocks]
    per = len(pairs[0][0])
    rows = sum(block.shape[0] for block in pairs[0][0])

    def kernel(*refs):
        lefts, refs = refs[: 2 * per], refs[2 * per :]
        rights, refs = refs[:2], refs[2:]
        came_ref = refs[0] if came is not None else None
        out_ref, turned = refs[-2:]
        index = pl.program_id(0)

        @pl.when(index == 0)
        def _():
            for pair in (0, 1):
                start = 0
                for left in lefts[pair * per : (pair + 1) * per]:
                    turned[pair, :, start : start + left.shape[0]] = left[...].T
                    start += left.shape[0]

        def run(pair):
            total = dot(turned[pair], rights[pair][...])
            if came_ref is not None:
                total += came_ref[...].astype(F32)
            out_ref[...] = total.astype(BF16)

        @pl.when(index < edge)
        def _():
            run(0)

        @pl.when(index >= edge)
        def _():
            run(1)

    shifts = [
        half * counts[i] if pairs[i][1].shape[1] > widths[i] else 0 for i in (0, 1)
    ]
    last = counts[1] - 1
    specs = [pl.BlockSpec(block.shape, lambda i: (0, 0)) for block in blocks_flat]
    specs += [
        pl.BlockSpec((rows, tile), lambda i: (0, jnp.minimum(i, edge - 1) + shifts[0])),
        pl.BlockSpec((rows, tile), lambda i: (0, jnp.clip(i - edge, 0, last) + shifts[1])),
    ]
    over = pl.BlockSpec((D, tile), lambda i: (0, i))
    return pl.pallas_call(
        kernel,
        grid=(sum(counts),),
        out_shape=jax.ShapeDtypeStruct((D, sum(widths)), BF16),
        in_specs=specs + ([over] if came is not None else []),
        out_specs=over,
        scratch_shapes=[pltpu.VMEM((2, D, rows), BF16)],
        compiler_params=pltpu.CompilerParams(vmem_limit_bytes=24 << 20),
        cost_estimate=pl.CostEstimate(flops=1000, bytes_accessed=1000, transcendentals=0),
        name="weight_gradients",
    )(*blocks_flat, pairs[0][1], pairs[1][1], *(() if came is None else (came,)))


def _columns(right, half, width):
    return right[:, half * width : (half + 1) * width] if right.shape[1] > width else right


def add_portions(spot, places, came, sums):
    count = len(places)
    came, shape = came[:count], came[0].shape

    def kernel(spots_ref, *refs):
        ins, parts, outs = refs[:count], refs[count : 2 * count], refs[2 * count :]
        for value, part, out in zip(ins, parts, outs):
            out[...] = (value[...].astype(F32) + part[...].astype(F32)).astype(BF16)

    whole = pl.BlockSpec(shape, lambda i, spots_ref: (0, 0))
    return pl.pallas_call(
        kernel,
        grid_spec=pltpu.PrefetchScalarGridSpec(
            num_scalar_prefetch=1,
            grid=(1,),
            in_specs=[whole] * count
            + [pl.BlockSpec(shape, lambda i, s, k=k: (s[k], 0)) for k in places],
            out_specs=[whole] * count,
        ),
        out_shape=[jax.ShapeDtypeStruct(shape, BF16)] * count,
        compiler_params=pltpu.CompilerParams(vmem_limit_bytes=16 << 20),
        cost_estimate=pl.CostEstimate(flops=1000, bytes_accessed=1000, transcendentals=0),
        name="add_portions",
    )(spot, *came, *([sums] * count))


def join(blocks):
    return blocks[0] if len(blocks) == 1 else jnp.concatenate(blocks, 0)


def body(
    tokens,
    cotangent,
    deal_slot,
    back_slot,
    lengths,
    time_step,
    time_table,
    w_qkv,
    b_qv,
    w_out,
    out_bias,
    ln_gain,
    ln_shift,
    w_ff1,
    b_ff1,
    w_ff2,
):
    wires = Wires(lax.axis_size("dp"), lax.axis_size("tensor"))
    rows_dev = tokens.shape[0]
    group_rows = rows_dev * wires.tensor_size
    tensor_index = lax.axis_index("tensor")
    layer_total = w_qkv.shape[0]
    inner = w_qkv.shape[3] // 2
    hidden = w_ff1.shape[2] // 2
    both = (True, False)

    time_piece = lax.dynamic_index_in_dim(time_table, time_step[0], 0, keepdims=False)

    def rings(layer, arrays, extra):
        w_qkv, w_out, w_ff1, w_ff2 = arrays
        attn_shard, feed_shard = [], []
        for mine in both:
            qkv = wires.half(w_qkv[layer], 2, mine)
            out = wires.half(w_out[layer], 0, mine).T
            attn_shard.append(jnp.concatenate([qkv[0], qkv[1], qkv[2], out], axis=1))
            first = wires.half(w_ff1[layer], 1, mine)
            second = wires.half(w_ff2[layer], 0, mine).T
            feed_shard.append(jnp.concatenate([first, second], axis=1))
        return (
            Task(wires.gather_ring(wires.chip_piece(attn_shard), extra)),
            Task(wires.gather_ring(wires.chip_piece(feed_shard))),
        )

    arrays = (w_qkv, w_out, w_ff1, w_ff2)
    attn_rings, feed_rings = [None] * (layer_total + 1), [None] * (layer_total + 1)
    attn_rings[0], feed_rings[0] = rings(0, arrays, time_piece)
    step = 0
    while not attn_rings[0].done:
        beside = (attn_rings[0], feed_rings[0] if step % 2 else None)
        if step == 1:
            tokens, back_slot = tick((tokens, back_slot), *beside)
            own_tokens = owner_swap(jnp.take(tokens, back_slot, axis=0))
        elif step == 2:
            own_tokens = tick(own_tokens, *beside)
            token_blocks = wires.rows_in(own_tokens)
        elif step == 4:
            token_blocks[-1] = tick(token_blocks[-1], *beside)
        else:
            tick((), *beside)
        step += 1
    attn_w, time_row = attn_rings[0].result
    time_row, *arrays = tie(time_row, *arrays)
    for layer in range(1, layer_total):
        attn_rings[layer], feed_rings[layer] = rings(layer, arrays, None)
    time_row = time_row.astype(F32)

    seq_ends = jnp.cumsum(lengths[0])
    positions = jnp.arange(group_rows, dtype=jnp.int32)
    if wires.tensor_size == 2:
        positions = (positions + tensor_index * rows_dev) % group_rows
    segment = jnp.sum((positions[:, None] >= seq_ends[None, :]).astype(jnp.int32), axis=1)

    stream = own_tokens.astype(F32) + time_row
    weights, saved = [], []
    for layer in range(layer_total):
        if layer == 0:
            input_blocks = [(rows.astype(F32) + time_row).astype(BF16) for rows in token_blocks]
        else:
            now = (attn_rings[layer], feed_rings[layer])
            input_blocks = wires.rows_in(tick(stream.astype(BF16), *now))
            input_blocks[-1] = tick(input_blocks[-1], *now)
            attn_w = attn_rings[layer].finish()
        ahead = (attn_rings[layer + 1], feed_rings[layer + 1])
        biases = []
        for mine in both:
            bias_q, bias_v = [wires.half(b_qv[layer, i], 0, mine) for i in (0, 1)]
            biases.append(jnp.concatenate([bias_q, jnp.zeros_like(bias_q), bias_v]))
        (qkv, mixture, log_total), _ = attend_forward(input_blocks, attn_w[0], biases[0], segment)
        if layer == 0:
            mixture = tick(mixture, feed_rings[0])
        attention = [(qkv, mixture, log_total)]
        part, sums = attend_forward(
            input_blocks, attn_w[1], biases[1], segment, (mixture, attn_w[0])
        )
        attention.append(part)
        sums[-1] = tick(sums[-1], feed_rings[layer])
        middle = stream + wires.rows_out(sums) + out_bias[layer, 0]
        normed = layer_norm(middle, ln_gain[layer, 0], ln_shift[layer, 0])
        normed_low = tick(normed.astype(BF16), feed_rings[layer], ahead[0])
        normed_blocks = wires.rows_in(normed_low)
        normed_blocks[-1] = tick(normed_blocks[-1], ahead[0])
        feed_w = feed_rings[layer].finish()
        weights.append((attn_w, feed_w))
        bias = jnp.concatenate([wires.half(b_ff1[layer], 0, mine) for mine in both])[None]
        sums, *filled = feed(normed_blocks, feed_w, bias, True)
        sums[-1] = tick(sums[-1], *ahead)
        second_sum = normed + wires.rows_out(sums) + out_bias[layer, 1]
        saved.append((input_blocks, attention, middle, normed_blocks, filled, second_sum))
        stream = layer_norm(second_sum, ln_gain[layer, 1], ln_shift[layer, 1])
        if layer == 0:
            stream, cotangent = tie(stream, cotangent)
            upstream = owner_swap(jnp.take(cotangent, back_slot, axis=0))

    encoded_own = stream.astype(BF16)
    gradient = upstream.astype(F32)
    feed_tasks, attn_tasks = [None] * (layer_total + 1), [None] * (layer_total + 1)
    attn_sums = None
    vector_grads = [None] * layer_total
    for layer in reversed(range(layer_total)):
        attn_w, feed_w = weights[layer]
        input_blocks, attention, middle, normed_blocks, (act, slope), second_sum = saved[layer]
        _, pull_second = jax.vjp(layer_norm, second_sum, ln_gain[layer, 1], ln_shift[layer, 1])
        grad_second, gain_second, shift_second = pull_second(gradient)
        later = (feed_tasks[layer + 1], attn_tasks[layer + 1])
        branch_blocks = wires.rows_in(tick(grad_second.astype(BF16), later[0]))
        if attn_sums is not None:
            branch_blocks[-1], attn_sums = tie(branch_blocks[-1], attn_sums)
            branch_blocks[-1] = tick(branch_blocks[-1], later[0])
            attn_tasks[layer + 1] = Task(wires.reduce_ring(attn_sums))
            later = (later[0], attn_tasks[layer + 1])
        sums, grad_pre, hidden_sums = feed(branch_blocks, feed_w, slope, False)
        hidden_sums = hidden_sums[0]
        if layer == layer_total - 1:
            sums[-1], encoded_own = tie(sums[-1], encoded_own)
            returned_out = owner_swap(encoded_own)
        sums[-1] = tick(sums[-1], *later)
        pairs = [(normed_blocks, grad_pre, hidden), (branch_blocks, act, hidden)]
        came = wires.partner(weight_gradients(pairs, 1))
        grad_normed = grad_second + wires.rows_out(sums)
        grad_normed, came = tie(grad_normed, came)
        _, pull_first = jax.vjp(layer_norm, middle, ln_gain[layer, 0], ln_shift[layer, 0])
        grad_middle, gain_first, shift_first = pull_first(grad_normed)
        attend_blocks = wires.rows_in(tick(grad_middle.astype(BF16), later[1]))
        feed_sums = weight_gradients(pairs, 0, came)
        attend_blocks[-1], feed_sums = tie(attend_blocks[-1], feed_sums)
        attend_blocks[-1] = tick(attend_blocks[-1], later[1])
        feed_tasks[layer] = Task(wires.reduce_ring(feed_sums))

        def attn_pairs(half, wide):
            return [(input_blocks, wide, 3 * inner), (attend_blocks, attention[half][1], inner)]

        wide, part_sums, _ = attend_backward(attend_blocks, attn_w[1], *attention[1], segment)
        send = weight_gradients(attn_pairs(1, wide), 1)
        if layer == 0:
            wide, send = tie(wide, send)
        came = wires.partner(send)
        own_wide, own_sums, sums = attend_backward(
            attend_blocks, attn_w[0], *attention[0], segment, (wide, attn_w[1])
        )
        sums[-1] = tick(sums[-1], feed_tasks[layer], later[1])
        if layer == 0:
            attn_sums = weight_gradients(attn_pairs(0, own_wide), 0, came)
            sums[-1], attn_sums = tie(sums[-1], attn_sums)
            attn_tasks[0] = Task(wires.reduce_ring(attn_sums))
        gradient = grad_middle + wires.rows_out(sums)
        if layer:
            attn_sums = weight_gradients(attn_pairs(0, own_wide), 0, came)
        qkv_sums = [part.reshape(3, inner)[::2] for part in (own_sums, part_sums)]
        vector_grads[layer] = (
            wires.ordered(qkv_sums[0], qkv_sums[1], 1),
            wires.ordered(hidden_sums[:hidden], hidden_sums[hidden:], 0),
            jnp.stack([jnp.sum(grad_middle, axis=0), jnp.sum(grad_second, axis=0)]),
            jnp.stack([gain_first, gain_second]),
            jnp.stack([shift_first, shift_second]),
        )

    returned_grad = owner_swap(gradient.astype(BF16))
    time_grad = jnp.sum(gradient, axis=0)
    local = [jnp.stack([part[i] for part in vector_grads]) for i in range(5)]
    flat = jnp.concatenate([part.reshape(-1) for part in local[:2] + [time_grad] + local[2:]])
    border = local[0].size + local[1].size
    vector_task = Task(wires.butterfly(flat, border))
    final = (attn_tasks[0], feed_tasks[0], vector_task)
    while not all(task.done for task in final):
        tick((), *final)
    reduced = [
        (attn_tasks[layer].finish(), feed_tasks[layer].finish()) for layer in range(layer_total)
    ]
    flat, shared = vector_task.result
    grad_tokens = jnp.take(returned_grad, deal_slot, axis=0)
    encoded = jnp.take(returned_out, deal_slot, axis=0)
    matrix_grads = []
    for attn_pair, feed_pair in reduced:
        rows = attn_pair[0].shape[0]
        matrix_grads.append(
            (
                wires.ordered(
                    *(
                        part[:, : 3 * inner].reshape(rows, 3, inner).transpose(1, 0, 2)
                        for part in attn_pair
                    ),
                    2,
                ),
                wires.ordered(*(part[:, 3 * inner :].T for part in attn_pair), 0),
                wires.ordered(*(part[:, :hidden] for part in feed_pair), 1),
                wires.ordered(*(part[:, hidden:].T for part in feed_pair), 0),
            )
        )
    grad_b_qv = flat[: local[0].size].reshape(local[0].shape)
    grad_b_ff1 = flat[local[0].size : border].reshape(local[1].shape)
    time_grad = shared[:D]
    rest = shared[D:].reshape(3, layer_total, 2, D)
    return (
        encoded,
        grad_tokens,
        time_grad,
        jnp.stack([part[0] for part in matrix_grads]),
        grad_b_qv,
        jnp.stack([part[1] for part in matrix_grads]),
        rest[0],
        rest[1],
        rest[2],
        jnp.stack([part[2] for part in matrix_grads]),
        grad_b_ff1,
        jnp.stack([part[3] for part in matrix_grads]),
    )


def solution(mesh):
    return jax.shard_map(
        body,
        mesh=mesh,
        in_specs=(
            P(("dp", "tensor"), None),
            P(("dp", "tensor"), None),
            P(("dp", "tensor")),
            P(("dp", "tensor")),
            P("dp", None),
            P(),
            P(None, "dp"),
            P(None, None, "dp", "tensor"),
            P(None, None, "tensor"),
            P(None, "tensor", "dp"),
            P(),
            P(),
            P(),
            P(None, "dp", "tensor"),
            P(None, "tensor"),
            P(None, "tensor", "dp"),
        ),
        out_specs=(
            P(("dp", "tensor"), None),
            P(("dp", "tensor"), None),
            P(),
            P(None, None, "dp", "tensor"),
            P(None, None, "tensor"),
            P(None, "tensor", "dp"),
            P(),
            P(),
            P(),
            P(None, "dp", "tensor"),
            P(None, "tensor"),
            P(None, "tensor", "dp"),
        ),
        check_vma=False,
    )
```

```python
import math

import jax
import jax.numpy as jnp
import numpy as np
from jax import lax
from jax.experimental import pallas as pl
from jax.experimental.pallas import tpu as pltpu
from jax.sharding import PartitionSpec as P

D = 1024
HEADS = 16
FF = 4096
HEAD = D // HEADS
F32 = jnp.float32
BF16 = jnp.bfloat16
SMALL_COST = pl.CostEstimate(flops=1000, bytes_accessed=1000, transcendentals=0)


def layer_norm(summed, scaling, offset_vec):
    centre = jnp.mean(summed, axis=-1, keepdims=True)
    spread = summed - centre
    variance = jnp.mean(spread * spread, axis=-1, keepdims=True)
    return spread * lax.rsqrt(variance + 1e-05) * scaling + offset_vec


def dot(left, right):
    return jnp.dot(left, right, preferred_element_type=F32)


def contract_rows(left, right):
    return lax.dot_general(left, right, (((0,), (0,)), ((), ())), preferred_element_type=F32)


def times_transposed(left, right):
    return lax.dot_general(left, right, (((1,), (1,)), ((), ())), preferred_element_type=F32)


class Wires:
    def __init__(self, dp_size, tensor_size):
        self.dp_size, self.tensor_size = dp_size, tensor_size
        chips = dp_size // 2
        self.chips = chips
        order = list(range(0, chips, 2)) + list(range(chips - 1, 0, -2))
        place = {chip: spot for spot, chip in enumerate(order)}
        self.rounds = chips // 2
        ahead, spots = [], np.zeros((dp_size, chips + 1), np.int32)
        for device in range(dp_size):
            chip, core = divmod(device, 2)
            way = 1 if core == 0 else -1
            ahead.append((device, 2 * order[(place[chip] + way) % chips] + core))
            spots[device, :chips] = [order[(place[chip] + way * s) % chips] for s in range(chips)]
            spots[device, chips] = core
        self.ahead = ahead
        self.back = [(there, here) for here, there in ahead]
        self.swap = [(d, d ^ 1) for d in range(dp_size)]
        dp_index = lax.axis_index("dp")
        self.core = dp_index % 2
        self.spot = lax.dynamic_index_in_dim(jnp.asarray(spots), dp_index, 0, keepdims=False)

    def round(self, forth, back):
        if back is None:
            return [lax.ppermute(forth, "dp", self.ahead)]
        return [lax.ppermute(forth, "dp", self.ahead), lax.ppermute(back, "dp", self.back)]

    def partner(self, array):
        return lax.ppermute(array, "dp", self.swap)

    def across(self, array):
        return lax.ppermute(array, "tensor", [(0, 1), (1, 0)])

    def half(self, array, axis, mine):
        width = array.shape[axis] // 2
        index = self.core if mine else 1 - self.core
        return lax.dynamic_slice_in_dim(array, index * width, width, axis)

    def ordered(self, mine, other, axis):
        return jnp.where(
            self.core == 0,
            jnp.concatenate([mine, other], axis),
            jnp.concatenate([other, mine], axis),
        )

    def chip_piece(self, shard):
        mine, other = shard
        return self.ordered(mine, self.partner(other), 0)

    def gather_ring(self, piece, extra=None):
        chip_rows = piece.shape[0]
        if extra is not None:
            tail = jnp.zeros((8, piece.shape[1]), piece.dtype)
            pair = self.ordered(extra, self.partner(extra), 0)
            tail = lax.dynamic_update_slice(tail, pair[None, :], (0, 0))
            piece = jnp.concatenate([piece, tail], 0)
        piece = yield piece
        forth, back = [piece], [piece]
        for step in range(1, self.rounds + 1):
            both_ways = step < self.chips - self.rounds
            came = yield self.round(forth[-1], back[-1] if both_ways else None)
            forth.append(came[0])
            back += came[1:]
        blocks = [0] + [self.chips - s for s in range(1, len(forth))] + list(range(1, len(back)))
        whole, vector = place_pieces(self.spot, blocks, forth + back[1:], chip_rows)
        halves = (whole, self.partner(whole))
        return halves if extra is None else (halves, vector[:, 0, :chip_rows].reshape(-1))

    def reduce_ring(self, sums):
        forth, back = add_portions(self.spot, [self.rounds, 1 + self.rounds], [], sums)
        for step in range(1, self.rounds + 1):
            both_ways = step < self.chips - self.rounds
            came = yield self.round(forth, back if both_ways else None)
            places = [self.rounds - step] if step < self.rounds else []
            if step + 1 < self.chips - self.rounds:
                places.append(1 + self.rounds + step)
            added = add_portions(self.spot, places, came, sums) if places else []
            forth = added[0] if step < self.rounds else came[0]
            if both_ways:
                back = added[1] if len(places) == 2 else came[1]
        mine, other = last_portion(self.spot, [forth, back], sums)
        return mine, self.partner(other)

    def rows_in(self, local_rows):
        if self.tensor_size == 2:
            return [local_rows, self.across(local_rows)]
        return [lax.all_gather(local_rows, "tensor", axis=0, tiled=True)]

    def rows_out(self, sums):
        if self.tensor_size == 2:
            return sums[0] + self.across(sums[1]).astype(F32)
        return lax.psum_scatter(sums[0], "tensor", scatter_dimension=0, tiled=True).astype(F32)

    def butterfly(self, array, border):
        for axis, size in (("dp", self.dp_size), ("tensor", self.tensor_size)):
            if axis == "tensor":
                array, kept = array[border:], array
            bit = 1
            while bit < size:
                pairs = [(i, i ^ bit) for i in range(size)]
                array = array + (yield lax.ppermute(array, axis, pairs))
                bit *= 2
        return kept, array


def owner_swap(rows):
    return lax.all_to_all(rows, "dp", split_axis=0, concat_axis=0, tiled=True)


class Task:
    def __init__(self, steps):
        self.steps, self.done, self.result = steps, False, None
        self.advance(None, first=True)

    def advance(self, arrived, first=False):
        try:
            self.pending = next(self.steps) if first else self.steps.send(arrived)
        except StopIteration as stop:
            self.done, self.result = True, stop.value

    def finish(self):
        while not self.done:
            self.advance(self.pending)
        return self.result


def tick(value, *tasks):
    tasks = [task for task in tasks if task is not None and not task.done]
    if not tasks:
        return value
    value, arrived = lax.optimization_barrier((value, [task.pending for task in tasks]))
    for task, part in zip(tasks, arrived):
        task.advance(part)
    return value


def tie(*values):
    return lax.optimization_barrier(values)


def place_pieces(spot, places, pieces, chip_rows):
    count, width = len(pieces), pieces[0].shape[1]
    spare = pieces[0].shape[0] - chip_rows

    def kernel(spot_ref, *refs):
        ins, outs, sems = refs[:count], refs[count:-1], refs[-1]
        copies = []
        for i, piece in enumerate(ins):
            chip = spot_ref[places[i]]
            rows = pl.ds(pl.multiple_of(chip * chip_rows, chip_rows), chip_rows)
            copies.append(
                pltpu.make_async_copy(piece.at[0:chip_rows], outs[0].at[rows], sems.at[i, 0])
            )
            if spare:
                copies.append(
                    pltpu.make_async_copy(
                        piece.at[chip_rows : chip_rows + spare, 0:128],
                        outs[1].at[chip],
                        sems.at[i, 1],
                    )
                )
        for copy in copies:
            copy.start()
        for copy in copies:
            copy.wait()

    shapes = [jax.ShapeDtypeStruct((count * chip_rows, width), BF16)]
    if spare:
        shapes.append(jax.ShapeDtypeStruct((count, spare, 128), BF16))
    outs = pl.pallas_call(
        kernel,
        out_shape=shapes,
        in_specs=[pl.BlockSpec(memory_space=pltpu.SMEM)]
        + [pl.BlockSpec(memory_space=pltpu.HBM)] * count,
        out_specs=[pl.BlockSpec(memory_space=pltpu.VMEM)] * len(shapes),
        scratch_shapes=[pltpu.SemaphoreType.DMA((count, 2))],
        compiler_params=pltpu.CompilerParams(vmem_limit_bytes=16 << 20),
        cost_estimate=SMALL_COST,
        name="place_pieces",
    )(spot, *pieces)
    return outs[0], (outs[1] if spare else None)


def attend_forward(blocks, weight, bias, segment, earlier=None):
    rows = sum(block.shape[0] for block in blocks)
    inner = weight.shape[1] // 4
    heads = inner // HEAD
    step = min(512, rows)
    scale = 1.0 / math.sqrt(HEAD)
    extra = 0 if earlier is None else 2

    def kernel(*refs):
        xs, refs = refs[: len(blocks)], refs[len(blocks) :]
        w_ref, bias_ref, col_ref, row_ref = refs[:4]
        before, refs = refs[4 : 4 + extra], refs[4 + extra :]
        qkv_ref, out_ref, log_ref = refs[:3]
        start = 0
        for x in xs:
            size = x.shape[0]
            projected = dot(x[...], w_ref[:, : 3 * inner]) + bias_ref[...]
            qkv_ref[start : start + size, :] = projected.astype(BF16)
            start += size
        for first in range(0, rows, step):
            part = slice(first, first + step)
            far = jnp.where(col_ref[...] == row_ref[:, part], 0.0, -1e30)
            mixed = []
            for h in range(heads):
                lanes = [slice(i * inner + h * HEAD, i * inner + (h + 1) * HEAD) for i in range(3)]
                scores = times_transposed(qkv_ref[:, lanes[1]], qkv_ref[part, lanes[0]])
                scores = scores * scale + far
                highest = jnp.max(scores, axis=0, keepdims=True)
                powers = jnp.exp(scores - highest)
                summed = jnp.sum(powers, axis=0, keepdims=True)
                mixture = contract_rows(qkv_ref[:, lanes[2]], powers.astype(BF16))
                mixed.append(mixture * (1.0 / summed))
                log_ref[h : h + 1, part] = highest + jnp.log(summed)
            out_ref[part, :] = jnp.concatenate(mixed, 0).T.astype(BF16)
        start = 0
        for sum_ref in refs[3:]:
            part = slice(start, start + sum_ref.shape[0])
            start += sum_ref.shape[0]
            total = times_transposed(before[0][part, :], before[1][:, 3 * inner :])
            total += times_transposed(out_ref[part, :], w_ref[:, 3 * inner :])
            sum_ref[...] = total.astype(sum_ref.dtype)

    shapes = [
        jax.ShapeDtypeStruct((rows, 3 * inner), BF16),
        jax.ShapeDtypeStruct((rows, inner), BF16),
        jax.ShapeDtypeStruct((heads, rows), F32),
    ]
    if earlier is not None:
        shapes += sum_shapes(blocks)
    outs = pl.pallas_call(
        kernel,
        out_shape=shapes,
        compiler_params=pltpu.CompilerParams(vmem_limit_bytes=32 << 20),
        cost_estimate=SMALL_COST,
        name="attend_forward",
    )(*blocks, weight, bias[None], segment[:, None], segment[None], *(earlier or ()))
    return tuple(outs[:3]), list(outs[3:])


def sum_shapes(blocks):
    kinds = (F32, BF16) if len(blocks) == 2 else (BF16,)
    return [jax.ShapeDtypeStruct(block.shape, kind) for block, kind in zip(blocks, kinds)]


def attend_backward(blocks, weight, qkv, mixture, log_total, segment, earlier=None):
    rows = sum(block.shape[0] for block in blocks)
    inner = weight.shape[1] // 4
    extra = 0 if earlier is None else 2
    heads = inner // HEAD
    step = min(512, rows)
    scale = 1.0 / math.sqrt(HEAD)

    def kernel(*refs):
        xs = refs[: len(blocks)]
        (w_ref, qkv_ref, mix_ref, log_ref, col_ref, row_ref) = refs[len(blocks) : len(blocks) + 6]
        refs = refs[len(blocks) + 6 :]
        before, refs = refs[:extra], refs[extra:]
        grad_ref, sum_ref, dout_ref = refs[0], refs[1], refs[-1]
        start = 0
        for x in xs:
            size = x.shape[0]
            dout_ref[start : start + size, :] = dot(x[...], w_ref[:, 3 * inner :]).astype(BF16)
            start += size
        ones = jnp.ones((8, HEAD), F32)
        keys = [jnp.zeros((rows, HEAD), F32)] * heads
        values = [jnp.zeros((rows, HEAD), F32)] * heads
        for first in range(0, rows, step):
            part = slice(first, first + step)
            far = jnp.where(col_ref[...] == row_ref[:, part], 0.0, -1e30)
            queries = []
            for h in range(heads):
                lanes = [slice(i * inner + h * HEAD, i * inner + (h + 1) * HEAD) for i in range(3)]
                query, key = qkv_ref[part, lanes[0]], qkv_ref[:, lanes[1]]
                dout = dout_ref[part, lanes[0]]
                scores = times_transposed(key, query) * scale + far
                weights = jnp.exp(scores - log_ref[h : h + 1, part])
                product = dout.astype(F32) * mix_ref[part, lanes[0]].astype(F32)
                centre = lax.dot_general(
                    ones,
                    product,
                    (((1,), (1,)), ((), ())),
                    precision=lax.Precision.HIGHEST,
                    preferred_element_type=F32,
                )[0:1]
                grad_weights = times_transposed(qkv_ref[:, lanes[2]], dout)
                grad_scores = (weights * (grad_weights - centre)).astype(BF16)
                queries.append(contract_rows(key, grad_scores))
                keys[h] = keys[h] + dot(grad_scores, query)
                values[h] = values[h] + dot(weights.astype(BF16), dout)
            grad_ref[part, 0:inner] = (jnp.concatenate(queries, 0).T * scale).astype(BF16)
        for h in range(heads):
            grad_ref[:, inner + h * HEAD : inner + (h + 1) * HEAD] = (keys[h] * scale).astype(BF16)
            grad_ref[:, 2 * inner + h * HEAD : 2 * inner + (h + 1) * HEAD] = values[h].astype(BF16)
        sum_ref[...] = jnp.sum(grad_ref[...].astype(F32), axis=0, keepdims=True)
        start = 0
        for out_ref in refs[2:-1]:
            part = slice(start, start + out_ref.shape[0])
            start += out_ref.shape[0]
            total = times_transposed(before[0][part, :], before[1][:, : 3 * inner])
            total += times_transposed(grad_ref[part, :], w_ref[:, : 3 * inner])
            out_ref[...] = total.astype(out_ref.dtype)

    shapes = [
        jax.ShapeDtypeStruct((rows, 3 * inner), BF16),
        jax.ShapeDtypeStruct((1, 3 * inner), F32),
    ]
    if earlier is not None:
        shapes += sum_shapes(blocks)
    outs = pl.pallas_call(
        kernel,
        out_shape=shapes,
        scratch_shapes=[pltpu.VMEM((rows, inner), BF16)],
        compiler_params=pltpu.CompilerParams(vmem_limit_bytes=32 << 20),
        cost_estimate=SMALL_COST,
        name="attend_backward",
    )(*blocks, weight, qkv, mixture, log_total, segment[:, None], segment[None], *(earlier or ()))
    return outs[0], outs[1], list(outs[2:])


def normal_parts(x):
    bell = jnp.exp(-0.5 * x * x)
    t = 1.0 / (1.0 + 0.23164189 * jnp.abs(x))
    tail = 0.5307027145
    for c in (-0.7265760135, 0.7107068705, -0.142248368, 0.127414796):
        tail = tail * t + c
    tail = tail * t * bell
    return jnp.where(x >= 0.0, 1.0 - tail, tail), bell * 0.3989422804014327


def feed(blocks, weights, side, forward):
    rows = sum(block.shape[0] for block in blocks)
    hidden = weights[0].shape[1] // 2
    tile = min(512, hidden)
    tiles = hidden // tile
    into, onto = (0, hidden) if forward else (hidden, 0)

    def kernel(*refs):
        xs, refs = refs[: len(blocks)], refs[len(blocks) :]
        *halves, side_ref = refs[:3]
        outs, (kept_ref, more_ref, pre_ref) = refs[3:-3], refs[-3:]

        def project(half, index):
            start, slot = 0, lax.rem(index, 2)
            first = index * tile + into
            if not isinstance(index, int):
                first = pl.multiple_of(first, tile)
            for x in xs:
                part = pl.ds(start, x.shape[0])
                pre_ref[slot, part, :] = dot(x[...], halves[half][:, pl.ds(first, tile)])
                start += x.shape[0]

        def activate(half, index):
            first = index * tile + half * hidden
            if not isinstance(index, int):
                first = pl.multiple_of(first, tile)
            columns = pl.ds(first, tile)
            pre = pre_ref[lax.rem(index, 2)]
            if forward:
                pre = pre + side_ref[:, columns]
                cdf, bell = normal_parts(pre)
                kept_ref[:, columns] = (pre * cdf).astype(BF16)
                more_ref[:, columns] = (cdf + pre * bell).astype(BF16)
            else:
                kept = (pre * side_ref[:, columns].astype(F32)).astype(BF16)
                kept_ref[:, columns] = kept
                more_ref[:, columns] = jnp.sum(kept.astype(F32), axis=0, keepdims=True)

        for half in (0, 1):
            project(half, 0)

            def step(index, _, half=half):
                project(half, index)
                activate(half, index - 1)
                return 0

            lax.fori_loop(1, tiles, step, 0)
            activate(half, tiles - 1)
        start = 0
        for out in outs:
            part = slice(start, start + out.shape[0])
            start += out.shape[0]
            total = times_transposed(kept_ref[part, 0:hidden], halves[0][:, onto : onto + hidden])
            total += times_transposed(kept_ref[part, hidden:], halves[1][:, onto : onto + hidden])
            out[...] = total.astype(out.dtype)

    wide = jax.ShapeDtypeStruct((rows, 2 * hidden), BF16)
    outs = pl.pallas_call(
        kernel,
        out_shape=sum_shapes(blocks)
        + [wide, wide if forward else jax.ShapeDtypeStruct((1, 2 * hidden), F32)],
        scratch_shapes=[pltpu.VMEM((2, rows, tile), F32)],
        compiler_params=pltpu.CompilerParams(vmem_limit_bytes=32 << 20),
        cost_estimate=SMALL_COST,
        name="feed_forward" if forward else "feed_backward",
    )(*blocks, *weights, side)
    return list(outs[:-2]), outs[-2], outs[-1]


def weight_gradients(pairs, half):
    widths = [width for _, _, width in pairs]
    tile = math.gcd(256, *widths)
    if tile % 128:
        terms = [
            contract_rows(join(blocks), _columns(right, half, width))
            for blocks, right, width in pairs
        ]
        return jnp.concatenate(terms, 1).astype(BF16)
    counts = [width // tile for width in widths]
    edge = counts[0]
    blocks_flat = [block for blocks, _, _ in pairs for block in blocks]
    per = len(pairs[0][0])
    rows = sum(block.shape[0] for block in pairs[0][0])

    def kernel(*refs):
        lefts, refs = refs[: 2 * per], refs[2 * per :]
        rights, (out_ref, turned) = refs[:2], refs[2:]
        index = pl.program_id(0)

        @pl.when(index == 0)
        def _():
            for pair in (0, 1):
                start = 0
                for left in lefts[pair * per : (pair + 1) * per]:
                    turned[pair, :, start : start + left.shape[0]] = left[...].T
                    start += left.shape[0]

        def run(pair):
            out_ref[...] = dot(turned[pair], rights[pair][...]).astype(BF16)

        @pl.when(index < edge)
        def _():
            run(0)

        @pl.when(index >= edge)
        def _():
            run(1)

    shifts = [
        half * counts[i] if pairs[i][1].shape[1] > widths[i] else 0 for i in (0, 1)
    ]
    last = counts[1] - 1
    specs = [pl.BlockSpec(block.shape, lambda i: (0, 0)) for block in blocks_flat]
    specs += [
        pl.BlockSpec((rows, tile), lambda i: (0, jnp.minimum(i, edge - 1) + shifts[0])),
        pl.BlockSpec((rows, tile), lambda i: (0, jnp.clip(i - edge, 0, last) + shifts[1])),
    ]
    over = pl.BlockSpec((D, tile), lambda i: (0, i))
    return pl.pallas_call(
        kernel,
        grid=(sum(counts),),
        out_shape=jax.ShapeDtypeStruct((D, sum(widths)), BF16),
        in_specs=specs,
        out_specs=over,
        scratch_shapes=[pltpu.VMEM((2, D, rows), BF16)],
        compiler_params=pltpu.CompilerParams(vmem_limit_bytes=24 << 20),
        cost_estimate=SMALL_COST,
        name="weight_gradients",
    )(*blocks_flat, pairs[0][1], pairs[1][1])


def _columns(right, half, width):
    return right[:, half * width : (half + 1) * width] if right.shape[1] > width else right


def add_portions(spot, places, came, sums):
    count, given = len(places), min(len(came), len(places))
    shape = (sums[0].shape[0] // (spot.shape[0] - 1), sums[0].shape[1])

    def kernel(spot_ref, *refs):
        ins, parts, outs = refs[:given], refs[given:-count], refs[-count:]
        for i, out in enumerate(outs):
            total = sum(part[...].astype(F32) for part in parts[i * len(sums) : (i + 1) * len(sums)])
            if given:
                total += ins[i][...].astype(F32)
            out[...] = total.astype(BF16)

    whole = pl.BlockSpec(shape, lambda i, s: (0, 0))
    portions = [pl.BlockSpec(shape, lambda i, s, k=k: (s[k], 0)) for k in places for _ in sums]
    return pl.pallas_call(
        kernel,
        grid_spec=pltpu.PrefetchScalarGridSpec(
            num_scalar_prefetch=1,
            grid=(1,),
            in_specs=[whole] * given + portions,
            out_specs=[whole] * count,
        ),
        out_shape=[jax.ShapeDtypeStruct(shape, BF16)] * count,
        compiler_params=pltpu.CompilerParams(vmem_limit_bytes=24 << 20),
        cost_estimate=SMALL_COST,
        name="add_portions",
    )(spot, *came[:given], *(list(sums) * count))


def last_portion(spot, came, sums):
    chips = spot.shape[0] - 1
    shape = (sums[0].shape[0] // chips, sums[0].shape[1])
    rows = shape[0] // 2

    def kernel(spot_ref, *refs):
        ins, (mine, other, total) = refs[:-3], refs[-3:]
        total[...] = sum(part[...].astype(F32) for part in ins)
        first = pl.multiple_of(spot_ref[chips] * rows, rows)
        mine[...] = total[pl.ds(first, rows), :]
        other[...] = total[pl.ds(rows - first, rows), :].astype(BF16)

    whole = pl.BlockSpec(shape, lambda i, s: (0, 0))
    half = pl.BlockSpec((rows, shape[1]), lambda i, s: (0, 0))
    return pl.pallas_call(
        kernel,
        grid_spec=pltpu.PrefetchScalarGridSpec(
            num_scalar_prefetch=1,
            grid=(1,),
            in_specs=[whole] * len(came) + [pl.BlockSpec(shape, lambda i, s: (s[0], 0))] * len(sums),
            out_specs=[half] * 2,
            scratch_shapes=[pltpu.VMEM(shape, F32)],
        ),
        out_shape=[
            jax.ShapeDtypeStruct((rows, shape[1]), F32),
            jax.ShapeDtypeStruct((rows, shape[1]), BF16),
        ],
        compiler_params=pltpu.CompilerParams(vmem_limit_bytes=24 << 20),
        cost_estimate=SMALL_COST,
        name="last_portion",
    )(spot, *came, *sums)


def matrix_outputs(spot, layer, layer_total, attn_pair, feed_pair, filled):
    rows, inner, hidden = attn_pair[0].shape[0], attn_pair[0].shape[1] // 4, feed_pair[0].shape[1] // 2
    chips = spot.shape[0] - 1
    shapes = [
        (layer_total, 3, rows, 2 * inner),
        (layer_total, 2 * inner, rows),
        (layer_total, rows, 2 * hidden),
        (layer_total, 2 * hidden, rows),
    ]
    given = 0 if filled is None else 4

    def kernel(spot_ref, *refs):
        pairs, (qkv, out, first, second) = (refs[0:2], refs[2:4]), refs[4 + given :]
        for index in (0, 1):
            attn, feed = (pair[index][...].astype(F32) for pair in pairs)
            core = spot_ref[chips] if index == 0 else 1 - spot_ref[chips]
            heads = pl.ds(pl.multiple_of(core * inner, inner), inner)
            units = pl.ds(pl.multiple_of(core * hidden, hidden), hidden)
            for i in range(3):
                qkv[0, i, :, heads] = attn[:, i * inner : (i + 1) * inner]
            out[0, heads, :] = attn[:, 3 * inner :].T
            first[0, :, units] = feed[:, :hidden]
            second[0, units, :] = feed[:, hidden:].T

    def over(shape):
        return pl.BlockSpec((1,) + shape[1:], lambda i, s: (layer,) + (0,) * (len(shape) - 1))

    ins = (*attn_pair, *feed_pair)
    return pl.pallas_call(
        kernel,
        grid_spec=pltpu.PrefetchScalarGridSpec(
            num_scalar_prefetch=1,
            grid=(1,),
            in_specs=[pl.BlockSpec(part.shape, lambda i, s: (0, 0)) for part in ins]
            + [pl.BlockSpec(memory_space=pl.ANY)] * given,
            out_specs=[over(shape) for shape in shapes],
        ),
        out_shape=[jax.ShapeDtypeStruct(shape, F32) for shape in shapes],
        input_output_aliases={5 + i: i for i in range(given)},
        compiler_params=pltpu.CompilerParams(vmem_limit_bytes=24 << 20),
        cost_estimate=SMALL_COST,
        name="matrix_outputs",
    )(spot, *ins, *(filled or ()))


def join(blocks):
    return blocks[0] if len(blocks) == 1 else jnp.concatenate(blocks, 0)


def body(
    tokens,
    cotangent,
    deal_slot,
    back_slot,
    lengths,
    time_step,
    time_table,
    w_qkv,
    b_qv,
    w_out,
    out_bias,
    ln_gain,
    ln_shift,
    w_ff1,
    b_ff1,
    w_ff2,
):
    wires = Wires(lax.axis_size("dp"), lax.axis_size("tensor"))
    rows_dev = tokens.shape[0]
    group_rows = rows_dev * wires.tensor_size
    tensor_index = lax.axis_index("tensor")
    layer_total = w_qkv.shape[0]
    inner = w_qkv.shape[3] // 2
    hidden = w_ff1.shape[2] // 2
    both = (True, False)

    time_piece = lax.dynamic_index_in_dim(time_table, time_step[0], 0, keepdims=False)

    def rings(layer, arrays, extra):
        w_qkv, w_out, w_ff1, w_ff2 = arrays
        attn_shard, feed_shard = [], []
        for mine in both:
            qkv = wires.half(w_qkv[layer], 2, mine)
            out = wires.half(w_out[layer], 0, mine).T
            attn_shard.append(jnp.concatenate([qkv[0], qkv[1], qkv[2], out], axis=1))
            first = wires.half(w_ff1[layer], 1, mine)
            second = wires.half(w_ff2[layer], 0, mine).T
            feed_shard.append(jnp.concatenate([first, second], axis=1))
        return (
            Task(wires.gather_ring(wires.chip_piece(attn_shard), extra)),
            Task(wires.gather_ring(wires.chip_piece(feed_shard))),
        )

    arrays = (w_qkv, w_out, w_ff1, w_ff2)
    attn_rings, feed_rings = [None] * (layer_total + 1), [None] * (layer_total + 1)
    attn_rings[0], feed_rings[0] = rings(0, arrays, time_piece)
    step = 0
    while not attn_rings[0].done:
        beside = (attn_rings[0], feed_rings[0] if step % 2 else None)
        if step == 1:
            tokens, back_slot = tick((tokens, back_slot), *beside)
            own_tokens = owner_swap(jnp.take(tokens, back_slot, axis=0))
        elif step == 2:
            own_tokens = tick(own_tokens, *beside)
            token_blocks = wires.rows_in(own_tokens)
        elif step == 4:
            token_blocks[-1] = tick(token_blocks[-1], *beside)
        else:
            tick((), *beside)
        step += 1
    attn_w, time_row = attn_rings[0].result
    time_row, *arrays = tie(time_row, *arrays)
    for layer in range(1, layer_total):
        attn_rings[layer], feed_rings[layer] = rings(layer, arrays, None)
    time_row = time_row.astype(F32)

    seq_ends = jnp.cumsum(lengths[0])
    positions = jnp.arange(group_rows, dtype=jnp.int32)
    if wires.tensor_size == 2:
        positions = (positions + tensor_index * rows_dev) % group_rows
    segment = jnp.sum((positions[:, None] >= seq_ends[None, :]).astype(jnp.int32), axis=1)

    stream = own_tokens.astype(F32) + time_row
    weights, saved = [], []
    for layer in range(layer_total):
        if layer == 0:
            input_blocks = [(rows.astype(F32) + time_row).astype(BF16) for rows in token_blocks]
            input_blocks[-1] = tick(input_blocks[-1], feed_rings[0])
        else:
            now = (attn_rings[layer], feed_rings[layer])
            input_blocks = wires.rows_in(tick(stream.astype(BF16), *now))
            input_blocks[-1] = tick(input_blocks[-1], *now)
            attn_w = attn_rings[layer].finish()
        ahead = (attn_rings[layer + 1], feed_rings[layer + 1])
        biases = []
        for mine in both:
            bias_q, bias_v = [wires.half(b_qv[layer, i], 0, mine) for i in (0, 1)]
            biases.append(jnp.concatenate([bias_q, jnp.zeros_like(bias_q), bias_v]))
        (qkv, mixture, log_total), _ = attend_forward(input_blocks, attn_w[0], biases[0], segment)
        attention = [(qkv, mixture, log_total)]
        part, sums = attend_forward(
            input_blocks, attn_w[1], biases[1], segment, (mixture, attn_w[0])
        )
        attention.append(part)
        sums[-1] = tick(sums[-1], feed_rings[layer])
        middle = stream + wires.rows_out(sums) + out_bias[layer, 0]
        normed = layer_norm(middle, ln_gain[layer, 0], ln_shift[layer, 0])
        normed_low = tick(normed.astype(BF16), feed_rings[layer], ahead[0])
        if layer == layer_total - 1:
            normed_low, upstream = tie(normed_low, upstream)
        normed_blocks = wires.rows_in(normed_low)
        normed_blocks[-1] = tick(normed_blocks[-1], ahead[0])
        feed_w = feed_rings[layer].finish()
        weights.append((attn_w, feed_w))
        bias = jnp.concatenate([wires.half(b_ff1[layer], 0, mine) for mine in both])[None]
        sums, *filled = feed(normed_blocks, feed_w, bias, True)
        if layer == 0:
            sums[-1], cotangent = tie(sums[-1], cotangent)
            upstream = owner_swap(jnp.take(cotangent, back_slot, axis=0))
        sums[-1] = tick(sums[-1], *ahead)
        second_sum = normed + wires.rows_out(sums) + out_bias[layer, 1]
        saved.append((input_blocks, attention, middle, normed_blocks, filled, second_sum))
        stream = layer_norm(second_sum, ln_gain[layer, 1], ln_shift[layer, 1])

    encoded_own = stream.astype(BF16)
    gradient = upstream.astype(F32)
    feed_tasks, attn_tasks = [None] * (layer_total + 1), [None] * (layer_total + 1)
    attn_sums = None
    vector_grads = [None] * layer_total
    for layer in reversed(range(layer_total)):
        attn_w, feed_w = weights[layer]
        input_blocks, attention, middle, normed_blocks, (act, slope), second_sum = saved[layer]
        _, pull_second = jax.vjp(layer_norm, second_sum, ln_gain[layer, 1], ln_shift[layer, 1])
        grad_second, gain_second, shift_second = pull_second(gradient)
        later_feed, later_attn = feed_tasks[layer + 1], None
        send = tick(grad_second.astype(BF16), later_feed)
        if layer == layer_total - 1:
            send, encoded_own = tie(send, encoded_own)
            returned_out = owner_swap(encoded_own)
        if attn_sums is not None:
            send, *attn_sums = tie(send, *attn_sums)
            later_attn = attn_tasks[layer + 1] = Task(wires.reduce_ring(attn_sums))
        branch_blocks = wires.rows_in(send)
        branch_blocks[-1] = tick(branch_blocks[-1], later_feed, later_attn)
        sums, grad_pre, hidden_sums = feed(branch_blocks, feed_w, slope, False)
        hidden_sums = hidden_sums[0]
        if layer == layer_total - 1:
            sums[-1], returned_out = tie(sums[-1], returned_out)
        sums[-1] = tick(sums[-1], later_attn)
        pairs = [(normed_blocks, grad_pre, hidden), (branch_blocks, act, hidden)]
        came = wires.partner(weight_gradients(pairs, 1))
        grad_normed = grad_second + wires.rows_out(sums)
        grad_normed = tick(grad_normed, later_attn)
        _, pull_first = jax.vjp(layer_norm, middle, ln_gain[layer, 0], ln_shift[layer, 0])
        grad_middle, gain_first, shift_first = pull_first(grad_normed)
        send, *feed_sums = tie(grad_middle.astype(BF16), weight_gradients(pairs, 0), came)
        send = tick(send, later_attn)
        feed_tasks[layer] = Task(wires.reduce_ring(feed_sums))
        attend_blocks = wires.rows_in(send)
        attend_blocks[-1] = tick(attend_blocks[-1], feed_tasks[layer])

        def attn_pairs(half, wide):
            return [(input_blocks, wide, 3 * inner), (attend_blocks, attention[half][1], inner)]

        wide, part_sums, _ = attend_backward(attend_blocks, attn_w[1], *attention[1], segment)
        send = weight_gradients(attn_pairs(1, wide), 1)
        if layer == 0:
            wide, send = tie(wide, send)
        came = wires.partner(send)
        own_wide, own_sums, sums = attend_backward(
            attend_blocks, attn_w[0], *attention[0], segment, (wide, attn_w[1])
        )
        sums[-1] = tick(sums[-1], feed_tasks[layer])
        attn_sums = [weight_gradients(attn_pairs(0, own_wide), 0), came]
        if layer == 0:
            sums[-1], *attn_sums = tie(sums[-1], *attn_sums)
            attn_tasks[0] = Task(wires.reduce_ring(attn_sums))
        gradient = grad_middle + wires.rows_out(sums)
        qkv_sums = [part.reshape(3, inner)[::2] for part in (own_sums, part_sums)]
        vector_grads[layer] = (
            wires.ordered(qkv_sums[0], qkv_sums[1], 1),
            wires.ordered(hidden_sums[:hidden], hidden_sums[hidden:], 0),
            jnp.stack([jnp.sum(grad_middle, axis=0), jnp.sum(grad_second, axis=0)]),
            jnp.stack([gain_first, gain_second]),
            jnp.stack([shift_first, shift_second]),
        )

    returned_grad = owner_swap(gradient.astype(BF16))
    time_grad = jnp.sum(gradient, axis=0)
    local = [jnp.stack([part[i] for part in vector_grads]) for i in range(5)]
    flat = jnp.concatenate([part.reshape(-1) for part in local[:2] + [time_grad] + local[2:]])
    border = local[0].size + local[1].size
    vector_task = Task(wires.butterfly(flat, border))
    final = (attn_tasks[0], feed_tasks[0], vector_task)
    while not all(task.done for task in final):
        tick((), *final)
    reduced = [
        (attn_tasks[layer].finish(), feed_tasks[layer].finish()) for layer in range(layer_total)
    ]
    flat, shared = vector_task.result
    grad_tokens = jnp.take(returned_grad, deal_slot, axis=0)
    encoded = jnp.take(returned_out, deal_slot, axis=0)
    if inner % 128 == 0 and hidden % 128 == 0:
        matrices = None
        for layer in reversed(range(layer_total)):
            matrices = matrix_outputs(wires.spot, layer, layer_total, *reduced[layer], matrices)
    else:
        parts = []
        for attn_pair, feed_pair in reduced:
            rows = attn_pair[0].shape[0]
            qkv = [
                part[:, : 3 * inner].reshape(rows, 3, inner).transpose(1, 0, 2).astype(F32)
                for part in attn_pair
            ]
            parts.append(
                (
                    wires.ordered(*qkv, 2),
                    wires.ordered(*(part[:, 3 * inner :].T.astype(F32) for part in attn_pair), 0),
                    wires.ordered(*(part[:, :hidden].astype(F32) for part in feed_pair), 1),
                    wires.ordered(*(part[:, hidden:].T.astype(F32) for part in feed_pair), 0),
                )
            )
        matrices = [jnp.stack([part[i] for part in parts]) for i in range(4)]
    grad_b_qv = flat[: local[0].size].reshape(local[0].shape)
    grad_b_ff1 = flat[local[0].size : border].reshape(local[1].shape)
    time_grad = shared[:D]
    rest = shared[D:].reshape(3, layer_total, 2, D)
    return (
        encoded,
        grad_tokens,
        time_grad,
        matrices[0],
        grad_b_qv,
        matrices[1],
        rest[0],
        rest[1],
        rest[2],
        matrices[2],
        grad_b_ff1,
        matrices[3],
    )


def solution(mesh):
    return jax.shard_map(
        body,
        mesh=mesh,
        in_specs=(
            P(("dp", "tensor"), None),
            P(("dp", "tensor"), None),
            P(("dp", "tensor")),
            P(("dp", "tensor")),
            P("dp", None),
            P(),
            P(None, "dp"),
            P(None, None, "dp", "tensor"),
            P(None, None, "tensor"),
            P(None, "tensor", "dp"),
            P(),
            P(),
            P(),
            P(None, "dp", "tensor"),
            P(None, "tensor"),
            P(None, "tensor", "dp"),
        ),
        out_specs=(
            P(("dp", "tensor"), None),
            P(("dp", "tensor"), None),
            P(),
            P(None, None, "dp", "tensor"),
            P(None, None, "tensor"),
            P(None, "tensor", "dp"),
            P(),
            P(),
            P(),
            P(None, "dp", "tensor"),
            P(None, "tensor"),
            P(None, "tensor", "dp"),
        ),
        check_vma=False,
    )
```

```python
import math

import jax
import jax.numpy as jnp
import numpy as np
from jax import lax
from jax.experimental import pallas as pl
from jax.experimental.pallas import tpu as pltpu
from jax.sharding import PartitionSpec as P

D = 1024
HEADS = 16
FF = 4096
HEAD = D // HEADS
F32 = jnp.float32
BF16 = jnp.bfloat16
SMALL_COST = pl.CostEstimate(flops=1000, bytes_accessed=1000, transcendentals=0)


def layer_norm(summed, scaling, offset_vec):
    centre = jnp.mean(summed, axis=-1, keepdims=True)
    spread = summed - centre
    variance = jnp.mean(spread * spread, axis=-1, keepdims=True)
    return spread * lax.rsqrt(variance + 1e-05) * scaling + offset_vec


def dot(left, right):
    return jnp.dot(left, right, preferred_element_type=F32)


def contract_rows(left, right):
    return lax.dot_general(left, right, (((0,), (0,)), ((), ())), preferred_element_type=F32)


def times_transposed(left, right):
    return lax.dot_general(left, right, (((1,), (1,)), ((), ())), preferred_element_type=F32)


class Wires:
    def __init__(self, dp_size, tensor_size):
        self.dp_size, self.tensor_size = dp_size, tensor_size
        chips = dp_size // 2
        self.chips = chips
        order = list(range(0, chips, 2)) + list(range(chips - 1, 0, -2))
        place = {chip: spot for spot, chip in enumerate(order)}
        self.rounds = chips // 2
        ahead, spots = [], np.zeros((dp_size, chips + 1), np.int32)
        for device in range(dp_size):
            chip, core = divmod(device, 2)
            way = 1 if core == 0 else -1
            ahead.append((device, 2 * order[(place[chip] + way) % chips] + core))
            spots[device, :chips] = [order[(place[chip] + way * s) % chips] for s in range(chips)]
            spots[device, chips] = core
        self.ahead = ahead
        self.back = [(there, here) for here, there in ahead]
        self.swap = [(d, d ^ 1) for d in range(dp_size)]
        dp_index = lax.axis_index("dp")
        self.core = dp_index % 2
        self.spot = lax.dynamic_index_in_dim(jnp.asarray(spots), dp_index, 0, keepdims=False)

    def round(self, forth, back):
        if back is None:
            return [lax.ppermute(forth, "dp", self.ahead)]
        return [lax.ppermute(forth, "dp", self.ahead), lax.ppermute(back, "dp", self.back)]

    def partner(self, array):
        return lax.ppermute(array, "dp", self.swap)

    def across(self, array):
        return lax.ppermute(array, "tensor", [(0, 1), (1, 0)])

    def half(self, array, axis, mine):
        width = array.shape[axis] // 2
        index = self.core if mine else 1 - self.core
        return lax.dynamic_slice_in_dim(array, index * width, width, axis)

    def ordered(self, mine, other, axis):
        return jnp.where(
            self.core == 0,
            jnp.concatenate([mine, other], axis),
            jnp.concatenate([other, mine], axis),
        )

    def chip_piece(self, shard):
        mine, other = shard
        return self.ordered(mine, self.partner(other), 0)

    def gather_ring(self, piece, extra=None):
        chip_rows = piece.shape[0]
        if extra is not None:
            tail = jnp.zeros((8, piece.shape[1]), piece.dtype)
            pair = self.ordered(extra, self.partner(extra), 0)
            tail = lax.dynamic_update_slice(tail, pair[None, :], (0, 0))
            piece = jnp.concatenate([piece, tail], 0)
        piece = yield piece
        forth, back = [piece], [piece]
        for step in range(1, self.rounds + 1):
            both_ways = step < self.chips - self.rounds
            came = yield self.round(forth[-1], back[-1] if both_ways else None)
            forth.append(came[0])
            back += came[1:]
        blocks = [0] + [self.chips - s for s in range(1, len(forth))] + list(range(1, len(back)))
        whole, vector = place_pieces(self.spot, blocks, forth + back[1:], chip_rows)
        halves = (whole, self.partner(whole))
        return halves if extra is None else (halves, vector[:, 0, :chip_rows].reshape(-1))

    def reduce_ring(self, sums):
        forth, back = add_portions(self.spot, [self.rounds, 1 + self.rounds], [], sums)
        for step in range(1, self.rounds + 1):
            both_ways = step < self.chips - self.rounds
            came = yield self.round(forth, back if both_ways else None)
            places = [self.rounds - step] if step < self.rounds else []
            if step + 1 < self.chips - self.rounds:
                places.append(1 + self.rounds + step)
            added = add_portions(self.spot, places, came, sums) if places else []
            forth = added[0] if step < self.rounds else came[0]
            if both_ways:
                back = added[1] if len(places) == 2 else came[1]
        mine, other = last_portion(self.spot, [forth, back], sums)
        return mine, self.partner(other)

    def rows_in(self, local_rows):
        if self.tensor_size == 2:
            return [local_rows, self.across(local_rows)]
        return [lax.all_gather(local_rows, "tensor", axis=0, tiled=True)]

    def rows_out(self, sums):
        if self.tensor_size == 2:
            return sums[0] + self.across(sums[1]).astype(F32)
        return lax.psum_scatter(sums[0], "tensor", scatter_dimension=0, tiled=True).astype(F32)

    def butterfly(self, array, border):
        for axis, size in (("dp", self.dp_size), ("tensor", self.tensor_size)):
            if axis == "tensor":
                array, kept = array[border:], array
            bit = 1
            while bit < size:
                pairs = [(i, i ^ bit) for i in range(size)]
                array = array + (yield lax.ppermute(array, axis, pairs))
                bit *= 2
        return kept, array


def owner_swap(rows):
    return lax.all_to_all(rows, "dp", split_axis=0, concat_axis=0, tiled=True)


class Task:
    def __init__(self, steps):
        self.steps, self.done, self.result = steps, False, None
        self.advance(None, first=True)

    def advance(self, arrived, first=False):
        try:
            self.pending = next(self.steps) if first else self.steps.send(arrived)
        except StopIteration as stop:
            self.done, self.result = True, stop.value

    def finish(self):
        while not self.done:
            self.advance(self.pending)
        return self.result


def tick(value, *tasks):
    tasks = [task for task in tasks if task is not None and not task.done]
    if not tasks:
        return value
    value, arrived = lax.optimization_barrier((value, [task.pending for task in tasks]))
    for task, part in zip(tasks, arrived):
        task.advance(part)
    return value


def tie(*values):
    return lax.optimization_barrier(values)


def place_pieces(spot, places, pieces, chip_rows):
    count, width = len(pieces), pieces[0].shape[1]
    spare = pieces[0].shape[0] - chip_rows

    def kernel(spot_ref, *refs):
        ins, outs, sems = refs[:count], refs[count:-1], refs[-1]
        copies = []
        for i, piece in enumerate(ins):
            chip = spot_ref[places[i]]
            rows = pl.ds(pl.multiple_of(chip * chip_rows, chip_rows), chip_rows)
            copies.append(
                pltpu.make_async_copy(piece.at[0:chip_rows], outs[0].at[rows], sems.at[i, 0])
            )
            if spare:
                copies.append(
                    pltpu.make_async_copy(
                        piece.at[chip_rows : chip_rows + spare, 0:128],
                        outs[1].at[chip],
                        sems.at[i, 1],
                    )
                )
        for copy in copies:
            copy.start()
        for copy in copies:
            copy.wait()

    shapes = [jax.ShapeDtypeStruct((count * chip_rows, width), BF16)]
    if spare:
        shapes.append(jax.ShapeDtypeStruct((count, spare, 128), BF16))
    outs = pl.pallas_call(
        kernel,
        out_shape=shapes,
        in_specs=[pl.BlockSpec(memory_space=pltpu.SMEM)]
        + [pl.BlockSpec(memory_space=pltpu.HBM)] * count,
        out_specs=[pl.BlockSpec(memory_space=pltpu.VMEM)] * len(shapes),
        scratch_shapes=[pltpu.SemaphoreType.DMA((count, 2))],
        compiler_params=pltpu.CompilerParams(vmem_limit_bytes=16 << 20),
        cost_estimate=pl.CostEstimate(
            flops=0, bytes_accessed=1 << 26, transcendentals=0
        ),
        name="place_pieces",
    )(spot, *pieces)
    return outs[0], (outs[1] if spare else None)


def attend_forward(blocks, weight, bias, segment, earlier=None):
    rows = sum(block.shape[0] for block in blocks)
    inner = weight.shape[1] // 4
    heads = inner // HEAD
    step = min(512, rows)
    scale = 1.0 / math.sqrt(HEAD)
    extra = 0 if earlier is None else 2

    def kernel(*refs):
        xs, refs = refs[: len(blocks)], refs[len(blocks) :]
        w_ref, bias_ref, col_ref, row_ref = refs[:4]
        before, refs = refs[4 : 4 + extra], refs[4 + extra :]
        qkv_ref, out_ref, log_ref = refs[:3]
        start = 0
        for x in xs:
            size = x.shape[0]
            projected = dot(x[...], w_ref[:, : 3 * inner]) + bias_ref[...]
            qkv_ref[start : start + size, :] = projected.astype(BF16)
            start += size
        for first in range(0, rows, step):
            part = slice(first, first + step)
            far = jnp.where(col_ref[...] == row_ref[:, part], 0.0, -1e30)
            mixed = []
            for h in range(heads):
                lanes = [slice(i * inner + h * HEAD, i * inner + (h + 1) * HEAD) for i in range(3)]
                scores = times_transposed(qkv_ref[:, lanes[1]], qkv_ref[part, lanes[0]])
                scores = scores * scale + far
                highest = jnp.max(scores, axis=0, keepdims=True)
                powers = jnp.exp(scores - highest)
                summed = jnp.sum(powers, axis=0, keepdims=True)
                mixture = contract_rows(qkv_ref[:, lanes[2]], powers.astype(BF16))
                mixed.append(mixture * (1.0 / summed))
                log_ref[h : h + 1, part] = highest + jnp.log(summed)
            out_ref[part, :] = jnp.concatenate(mixed, 0).T.astype(BF16)
        start = 0
        for sum_ref in refs[3:]:
            part = slice(start, start + sum_ref.shape[0])
            start += sum_ref.shape[0]
            total = times_transposed(before[0][part, :], before[1][:, 3 * inner :])
            total += times_transposed(out_ref[part, :], w_ref[:, 3 * inner :])
            sum_ref[...] = total.astype(sum_ref.dtype)

    shapes = [
        jax.ShapeDtypeStruct((rows, 3 * inner), BF16),
        jax.ShapeDtypeStruct((rows, inner), BF16),
        jax.ShapeDtypeStruct((heads, rows), F32),
    ]
    if earlier is not None:
        shapes += sum_shapes(blocks)
    outs = pl.pallas_call(
        kernel,
        out_shape=shapes,
        compiler_params=pltpu.CompilerParams(vmem_limit_bytes=32 << 20),
        cost_estimate=SMALL_COST,
        name="attend_forward",
    )(*blocks, weight, bias[None], segment[:, None], segment[None], *(earlier or ()))
    return tuple(outs[:3]), list(outs[3:])


def sum_shapes(blocks):
    kinds = (F32, BF16) if len(blocks) == 2 else (BF16,)
    return [jax.ShapeDtypeStruct(block.shape, kind) for block, kind in zip(blocks, kinds)]


def attend_backward(blocks, weight, qkv, mixture, log_total, segment, earlier=None):
    rows = sum(block.shape[0] for block in blocks)
    inner = weight.shape[1] // 4
    extra = 0 if earlier is None else 2
    heads = inner // HEAD
    step = min(512, rows)
    scale = 1.0 / math.sqrt(HEAD)

    def kernel(*refs):
        xs = refs[: len(blocks)]
        (w_ref, qkv_ref, mix_ref, log_ref, col_ref, row_ref) = refs[len(blocks) : len(blocks) + 6]
        refs = refs[len(blocks) + 6 :]
        before, refs = refs[:extra], refs[extra:]
        grad_ref, sum_ref, dout_ref = refs[0], refs[1], refs[-1]
        start = 0
        for x in xs:
            size = x.shape[0]
            dout_ref[start : start + size, :] = dot(x[...], w_ref[:, 3 * inner :]).astype(BF16)
            start += size
        ones = jnp.ones((8, HEAD), F32)
        keys = [jnp.zeros((rows, HEAD), F32)] * heads
        values = [jnp.zeros((rows, HEAD), F32)] * heads
        for first in range(0, rows, step):
            part = slice(first, first + step)
            far = jnp.where(col_ref[...] == row_ref[:, part], 0.0, -1e30)
            queries = []
            for h in range(heads):
                lanes = [slice(i * inner + h * HEAD, i * inner + (h + 1) * HEAD) for i in range(3)]
                query, key = qkv_ref[part, lanes[0]], qkv_ref[:, lanes[1]]
                dout = dout_ref[part, lanes[0]]
                scores = times_transposed(key, query) * scale + far
                weights = jnp.exp(scores - log_ref[h : h + 1, part])
                product = dout.astype(F32) * mix_ref[part, lanes[0]].astype(F32)
                centre = lax.dot_general(
                    ones,
                    product,
                    (((1,), (1,)), ((), ())),
                    precision=lax.Precision.HIGHEST,
                    preferred_element_type=F32,
                )[0:1]
                grad_weights = times_transposed(qkv_ref[:, lanes[2]], dout)
                grad_scores = (weights * (grad_weights - centre)).astype(BF16)
                queries.append(contract_rows(key, grad_scores))
                keys[h] = keys[h] + dot(grad_scores, query)
                values[h] = values[h] + dot(weights.astype(BF16), dout)
            grad_ref[part, 0:inner] = (jnp.concatenate(queries, 0).T * scale).astype(BF16)
        for h in range(heads):
            grad_ref[:, inner + h * HEAD : inner + (h + 1) * HEAD] = (keys[h] * scale).astype(BF16)
            grad_ref[:, 2 * inner + h * HEAD : 2 * inner + (h + 1) * HEAD] = values[h].astype(BF16)
        sum_ref[...] = jnp.sum(grad_ref[...].astype(F32), axis=0, keepdims=True)
        start = 0
        for out_ref in refs[2:-1]:
            part = slice(start, start + out_ref.shape[0])
            start += out_ref.shape[0]
            total = times_transposed(before[0][part, :], before[1][:, : 3 * inner])
            total += times_transposed(grad_ref[part, :], w_ref[:, : 3 * inner])
            out_ref[...] = total.astype(out_ref.dtype)

    shapes = [
        jax.ShapeDtypeStruct((rows, 3 * inner), BF16),
        jax.ShapeDtypeStruct((1, 3 * inner), F32),
    ]
    if earlier is not None:
        shapes += sum_shapes(blocks)
    outs = pl.pallas_call(
        kernel,
        out_shape=shapes,
        scratch_shapes=[pltpu.VMEM((rows, inner), BF16)],
        compiler_params=pltpu.CompilerParams(vmem_limit_bytes=32 << 20),
        cost_estimate=SMALL_COST,
        name="attend_backward",
    )(*blocks, weight, qkv, mixture, log_total, segment[:, None], segment[None], *(earlier or ()))
    return outs[0], outs[1], list(outs[2:])


def normal_parts(x):
    bell = jnp.exp(-0.5 * x * x)
    t = 1.0 / (1.0 + 0.23164189 * jnp.abs(x))
    tail = 0.5307027145
    for c in (-0.7265760135, 0.7107068705, -0.142248368, 0.127414796):
        tail = tail * t + c
    tail = tail * t * bell
    return jnp.where(x >= 0.0, 1.0 - tail, tail), bell * 0.3989422804014327


def feed(blocks, weights, side, forward):
    rows = sum(block.shape[0] for block in blocks)
    hidden = weights[0].shape[1] // 2
    tile = min(512, hidden)
    tiles = hidden // tile
    into, onto = (0, hidden) if forward else (hidden, 0)

    def kernel(*refs):
        xs, refs = refs[: len(blocks)], refs[len(blocks) :]
        *halves, side_ref = refs[:3]
        outs, (kept_ref, more_ref, pre_ref) = refs[3:-3], refs[-3:]

        def project(half, index):
            start, slot = 0, lax.rem(index, 2)
            first = index * tile + into
            if not isinstance(index, int):
                first = pl.multiple_of(first, tile)
            for x in xs:
                part = pl.ds(start, x.shape[0])
                pre_ref[slot, part, :] = dot(x[...], halves[half][:, pl.ds(first, tile)])
                start += x.shape[0]

        def activate(half, index):
            first = index * tile + half * hidden
            if not isinstance(index, int):
                first = pl.multiple_of(first, tile)
            columns = pl.ds(first, tile)
            pre = pre_ref[lax.rem(index, 2)]
            if forward:
                pre = pre + side_ref[:, columns]
                cdf, bell = normal_parts(pre)
                kept_ref[:, columns] = (pre * cdf).astype(BF16)
                more_ref[:, columns] = (cdf + pre * bell).astype(BF16)
            else:
                kept = (pre * side_ref[:, columns].astype(F32)).astype(BF16)
                kept_ref[:, columns] = kept
                more_ref[:, columns] = jnp.sum(kept.astype(F32), axis=0, keepdims=True)

        for half in (0, 1):
            project(half, 0)

            def step(index, _, half=half):
                project(half, index)
                activate(half, index - 1)
                return 0

            lax.fori_loop(1, tiles, step, 0)
            activate(half, tiles - 1)
        start = 0
        for out in outs:
            part = slice(start, start + out.shape[0])
            start += out.shape[0]
            total = times_transposed(kept_ref[part, 0:hidden], halves[0][:, onto : onto + hidden])
            total += times_transposed(kept_ref[part, hidden:], halves[1][:, onto : onto + hidden])
            out[...] = total.astype(out.dtype)

    wide = jax.ShapeDtypeStruct((rows, 2 * hidden), BF16)
    outs = pl.pallas_call(
        kernel,
        out_shape=sum_shapes(blocks)
        + [wide, wide if forward else jax.ShapeDtypeStruct((1, 2 * hidden), F32)],
        scratch_shapes=[pltpu.VMEM((2, rows, tile), F32)],
        compiler_params=pltpu.CompilerParams(vmem_limit_bytes=32 << 20),
        cost_estimate=SMALL_COST,
        name="feed_forward" if forward else "feed_backward",
    )(*blocks, *weights, side)
    return list(outs[:-2]), outs[-2], outs[-1]


def weight_gradients(pairs, half):
    widths = [width for _, _, width in pairs]
    tile = math.gcd(256, *widths)
    if tile % 128:
        terms = [
            contract_rows(join(blocks), _columns(right, half, width))
            for blocks, right, width in pairs
        ]
        return jnp.concatenate(terms, 1).astype(BF16)
    counts = [width // tile for width in widths]
    edge = counts[0]
    blocks_flat = [block for blocks, _, _ in pairs for block in blocks]
    per = len(pairs[0][0])
    rows = sum(block.shape[0] for block in pairs[0][0])

    def kernel(*refs):
        lefts, refs = refs[: 2 * per], refs[2 * per :]
        rights, (out_ref, turned) = refs[:2], refs[2:]
        index = pl.program_id(0)

        @pl.when(index == 0)
        def _():
            for pair in (0, 1):
                start = 0
                for left in lefts[pair * per : (pair + 1) * per]:
                    turned[pair, :, start : start + left.shape[0]] = left[...].T
                    start += left.shape[0]

        def run(pair):
            out_ref[...] = dot(turned[pair], rights[pair][...]).astype(BF16)

        @pl.when(index < edge)
        def _():
            run(0)

        @pl.when(index >= edge)
        def _():
            run(1)

    shifts = [
        half * counts[i] if pairs[i][1].shape[1] > widths[i] else 0 for i in (0, 1)
    ]
    last = counts[1] - 1
    specs = [pl.BlockSpec(block.shape, lambda i: (0, 0)) for block in blocks_flat]
    specs += [
        pl.BlockSpec((rows, tile), lambda i: (0, jnp.minimum(i, edge - 1) + shifts[0])),
        pl.BlockSpec((rows, tile), lambda i: (0, jnp.clip(i - edge, 0, last) + shifts[1])),
    ]
    over = pl.BlockSpec((D, tile), lambda i: (0, i))
    return pl.pallas_call(
        kernel,
        grid=(sum(counts),),
        out_shape=jax.ShapeDtypeStruct((D, sum(widths)), BF16),
        in_specs=specs,
        out_specs=over,
        scratch_shapes=[pltpu.VMEM((2, D, rows), BF16)],
        compiler_params=pltpu.CompilerParams(vmem_limit_bytes=24 << 20),
        cost_estimate=SMALL_COST,
        name="weight_gradients",
    )(*blocks_flat, pairs[0][1], pairs[1][1])


def _columns(right, half, width):
    return right[:, half * width : (half + 1) * width] if right.shape[1] > width else right


def add_portions(spot, places, came, sums):
    count, given = len(places), min(len(came), len(places))
    shape = (sums[0].shape[0] // (spot.shape[0] - 1), sums[0].shape[1])

    def kernel(spot_ref, *refs):
        ins, parts, outs = refs[:given], refs[given:-count], refs[-count:]
        for i, out in enumerate(outs):
            total = sum(part[...].astype(F32) for part in parts[i * len(sums) : (i + 1) * len(sums)])
            if given:
                total += ins[i][...].astype(F32)
            out[...] = total.astype(BF16)

    whole = pl.BlockSpec(shape, lambda i, s: (0, 0))
    portions = [pl.BlockSpec(shape, lambda i, s, k=k: (s[k], 0)) for k in places for _ in sums]
    return pl.pallas_call(
        kernel,
        grid_spec=pltpu.PrefetchScalarGridSpec(
            num_scalar_prefetch=1,
            grid=(1,),
            in_specs=[whole] * given + portions,
            out_specs=[whole] * count,
        ),
        out_shape=[jax.ShapeDtypeStruct(shape, BF16)] * count,
        compiler_params=pltpu.CompilerParams(vmem_limit_bytes=24 << 20),
        cost_estimate=SMALL_COST,
        name="add_portions",
    )(spot, *came[:given], *(list(sums) * count))


def last_portion(spot, came, sums):
    chips = spot.shape[0] - 1
    shape = (sums[0].shape[0] // chips, sums[0].shape[1])
    rows = shape[0] // 2

    def kernel(spot_ref, *refs):
        ins, (mine, other, total) = refs[:-3], refs[-3:]
        total[...] = sum(part[...].astype(F32) for part in ins)
        first = pl.multiple_of(spot_ref[chips] * rows, rows)
        mine[...] = total[pl.ds(first, rows), :]
        other[...] = total[pl.ds(rows - first, rows), :].astype(BF16)

    whole = pl.BlockSpec(shape, lambda i, s: (0, 0))
    half = pl.BlockSpec((rows, shape[1]), lambda i, s: (0, 0))
    return pl.pallas_call(
        kernel,
        grid_spec=pltpu.PrefetchScalarGridSpec(
            num_scalar_prefetch=1,
            grid=(1,),
            in_specs=[whole] * len(came) + [pl.BlockSpec(shape, lambda i, s: (s[0], 0))] * len(sums),
            out_specs=[half] * 2,
            scratch_shapes=[pltpu.VMEM(shape, F32)],
        ),
        out_shape=[
            jax.ShapeDtypeStruct((rows, shape[1]), F32),
            jax.ShapeDtypeStruct((rows, shape[1]), BF16),
        ],
        compiler_params=pltpu.CompilerParams(vmem_limit_bytes=24 << 20),
        cost_estimate=SMALL_COST,
        name="last_portion",
    )(spot, *came, *sums)


def matrix_outputs(spot, layer, layer_total, attn_pair, feed_pair, filled):
    rows, inner, hidden = attn_pair[0].shape[0], attn_pair[0].shape[1] // 4, feed_pair[0].shape[1] // 2
    chips = spot.shape[0] - 1
    shapes = [
        (layer_total, 3, rows, 2 * inner),
        (layer_total, 2 * inner, rows),
        (layer_total, rows, 2 * hidden),
        (layer_total, 2 * hidden, rows),
    ]
    given = 0 if filled is None else 4

    def kernel(spot_ref, *refs):
        pairs, (qkv, out, first, second) = (refs[0:2], refs[2:4]), refs[4 + given :]
        for index in (0, 1):
            attn, feed = (pair[index][...].astype(F32) for pair in pairs)
            core = spot_ref[chips] if index == 0 else 1 - spot_ref[chips]
            heads = pl.ds(pl.multiple_of(core * inner, inner), inner)
            units = pl.ds(pl.multiple_of(core * hidden, hidden), hidden)
            for i in range(3):
                qkv[0, i, :, heads] = attn[:, i * inner : (i + 1) * inner]
            out[0, heads, :] = attn[:, 3 * inner :].T
            first[0, :, units] = feed[:, :hidden]
            second[0, units, :] = feed[:, hidden:].T

    def over(shape):
        return pl.BlockSpec((1,) + shape[1:], lambda i, s: (layer,) + (0,) * (len(shape) - 1))

    ins = (*attn_pair, *feed_pair)
    return pl.pallas_call(
        kernel,
        grid_spec=pltpu.PrefetchScalarGridSpec(
            num_scalar_prefetch=1,
            grid=(1,),
            in_specs=[pl.BlockSpec(part.shape, lambda i, s: (0, 0)) for part in ins]
            + [pl.BlockSpec(memory_space=pl.ANY)] * given,
            out_specs=[over(shape) for shape in shapes],
        ),
        out_shape=[jax.ShapeDtypeStruct(shape, F32) for shape in shapes],
        input_output_aliases={5 + i: i for i in range(given)},
        compiler_params=pltpu.CompilerParams(vmem_limit_bytes=24 << 20),
        cost_estimate=SMALL_COST,
        name="matrix_outputs",
    )(spot, *ins, *(filled or ()))


def join(blocks):
    return blocks[0] if len(blocks) == 1 else jnp.concatenate(blocks, 0)


def body(
    tokens,
    cotangent,
    deal_slot,
    back_slot,
    lengths,
    time_step,
    time_table,
    w_qkv,
    b_qv,
    w_out,
    out_bias,
    ln_gain,
    ln_shift,
    w_ff1,
    b_ff1,
    w_ff2,
):
    wires = Wires(lax.axis_size("dp"), lax.axis_size("tensor"))
    rows_dev = tokens.shape[0]
    group_rows = rows_dev * wires.tensor_size
    tensor_index = lax.axis_index("tensor")
    layer_total = w_qkv.shape[0]
    inner = w_qkv.shape[3] // 2
    hidden = w_ff1.shape[2] // 2
    both = (True, False)

    time_piece = lax.dynamic_index_in_dim(time_table, time_step[0], 0, keepdims=False)

    def rings(layer, arrays, extra):
        w_qkv, w_out, w_ff1, w_ff2 = arrays
        attn_shard, feed_shard = [], []
        for mine in both:
            qkv = wires.half(w_qkv[layer], 2, mine)
            out = wires.half(w_out[layer], 0, mine).T
            attn_shard.append(jnp.concatenate([qkv[0], qkv[1], qkv[2], out], axis=1))
            first = wires.half(w_ff1[layer], 1, mine)
            second = wires.half(w_ff2[layer], 0, mine).T
            feed_shard.append(jnp.concatenate([first, second], axis=1))
        return (
            Task(wires.gather_ring(wires.chip_piece(attn_shard), extra)),
            Task(wires.gather_ring(wires.chip_piece(feed_shard))),
        )

    arrays = (w_qkv, w_out, w_ff1, w_ff2)
    attn_rings, feed_rings = [None] * (layer_total + 1), [None] * (layer_total + 1)
    attn_rings[0], feed_rings[0] = rings(0, arrays, time_piece)
    step = 0
    while not attn_rings[0].done:
        beside = (attn_rings[0], feed_rings[0] if step % 2 else None)
        if step == 1:
            tokens, back_slot = tick((tokens, back_slot), *beside)
            own_tokens = owner_swap(jnp.take(tokens, back_slot, axis=0))
        elif step == 2:
            own_tokens = tick(own_tokens, *beside)
            token_blocks = wires.rows_in(own_tokens)
        elif step == 4:
            token_blocks[-1] = tick(token_blocks[-1], *beside)
        else:
            tick((), *beside)
        step += 1
    attn_w, time_row = attn_rings[0].result
    time_row, *arrays = tie(time_row, *arrays)
    for layer in range(1, layer_total):
        attn_rings[layer], feed_rings[layer] = rings(layer, arrays, None)
    time_row = time_row.astype(F32)

    seq_ends = jnp.cumsum(lengths[0])
    positions = jnp.arange(group_rows, dtype=jnp.int32)
    if wires.tensor_size == 2:
        positions = (positions + tensor_index * rows_dev) % group_rows
    segment = jnp.sum((positions[:, None] >= seq_ends[None, :]).astype(jnp.int32), axis=1)

    stream = own_tokens.astype(F32) + time_row
    weights, saved = [], []
    for layer in range(layer_total):
        if layer == 0:
            input_blocks = [(rows.astype(F32) + time_row).astype(BF16) for rows in token_blocks]
            input_blocks[-1] = tick(input_blocks[-1], feed_rings[0])
        else:
            now = (attn_rings[layer], feed_rings[layer])
            input_blocks = wires.rows_in(tick(stream.astype(BF16), *now))
            input_blocks[-1] = tick(input_blocks[-1], *now)
            attn_w = attn_rings[layer].finish()
        ahead = (attn_rings[layer + 1], feed_rings[layer + 1])
        biases = []
        for mine in both:
            bias_q, bias_v = [wires.half(b_qv[layer, i], 0, mine) for i in (0, 1)]
            biases.append(jnp.concatenate([bias_q, jnp.zeros_like(bias_q), bias_v]))
        (qkv, mixture, log_total), _ = attend_forward(input_blocks, attn_w[0], biases[0], segment)
        attention = [(qkv, mixture, log_total)]
        part, sums = attend_forward(
            input_blocks, attn_w[1], biases[1], segment, (mixture, attn_w[0])
        )
        attention.append(part)
        sums[-1] = tick(sums[-1], feed_rings[layer])
        middle = stream + wires.rows_out(sums) + out_bias[layer, 0]
        normed = layer_norm(middle, ln_gain[layer, 0], ln_shift[layer, 0])
        normed_low = tick(normed.astype(BF16), feed_rings[layer], ahead[0])
        normed_blocks = wires.rows_in(normed_low)
        normed_blocks[-1] = tick(normed_blocks[-1], ahead[0])
        feed_w = feed_rings[layer].finish()
        weights.append((attn_w, feed_w))
        bias = jnp.concatenate([wires.half(b_ff1[layer], 0, mine) for mine in both])[None]
        sums, *filled = feed(normed_blocks, feed_w, bias, True)
        if layer == 0:
            sums[-1], cotangent = tie(sums[-1], cotangent)
            upstream = owner_swap(jnp.take(cotangent, back_slot, axis=0))
        sums[-1] = tick(sums[-1], *ahead)
        second_sum = normed + wires.rows_out(sums) + out_bias[layer, 1]
        saved.append((input_blocks, attention, middle, normed_blocks, filled, second_sum))
        stream = layer_norm(second_sum, ln_gain[layer, 1], ln_shift[layer, 1])

    encoded_own = stream.astype(BF16)
    gradient = upstream.astype(F32)
    feed_tasks, attn_tasks = [None] * (layer_total + 1), [None] * (layer_total + 1)
    attn_sums = None
    vector_grads = [None] * layer_total
    for layer in reversed(range(layer_total)):
        attn_w, feed_w = weights[layer]
        input_blocks, attention, middle, normed_blocks, (act, slope), second_sum = saved[layer]
        _, pull_second = jax.vjp(layer_norm, second_sum, ln_gain[layer, 1], ln_shift[layer, 1])
        grad_second, gain_second, shift_second = pull_second(gradient)
        later_feed, later_attn = feed_tasks[layer + 1], None
        send = tick(grad_second.astype(BF16), later_feed)
        if layer == layer_total - 1:
            send, encoded_own = tie(send, encoded_own)
            returned_out = owner_swap(encoded_own)
        if attn_sums is not None:
            send, *attn_sums = tie(send, *attn_sums)
            later_attn = attn_tasks[layer + 1] = Task(wires.reduce_ring(attn_sums))
        branch_blocks = wires.rows_in(send)
        branch_blocks[-1] = tick(branch_blocks[-1], later_feed, later_attn)
        sums, grad_pre, hidden_sums = feed(branch_blocks, feed_w, slope, False)
        hidden_sums = hidden_sums[0]
        pairs = [(normed_blocks, grad_pre, hidden), (branch_blocks, act, hidden)]
        came = wires.partner(weight_gradients(pairs, 1))
        grad_normed = grad_second + wires.rows_out(sums)
        grad_normed = tick(grad_normed, later_attn)
        _, pull_first = jax.vjp(layer_norm, middle, ln_gain[layer, 0], ln_shift[layer, 0])
        grad_middle, gain_first, shift_first = pull_first(grad_normed)
        send, *feed_sums = tie(grad_middle.astype(BF16), weight_gradients(pairs, 0), came)
        feed_tasks[layer] = Task(wires.reduce_ring(feed_sums))
        attend_blocks = wires.rows_in(send)
        attend_blocks[-1] = tick(attend_blocks[-1], feed_tasks[layer], later_attn)

        def attn_pairs(half, wide):
            return [(input_blocks, wide, 3 * inner), (attend_blocks, attention[half][1], inner)]

        wide, part_sums, _ = attend_backward(attend_blocks, attn_w[1], *attention[1], segment)
        send = weight_gradients(attn_pairs(1, wide), 1)
        came = wires.partner(send)
        own_wide, own_sums, sums = attend_backward(
            attend_blocks, attn_w[0], *attention[0], segment, (wide, attn_w[1])
        )
        sums[-1] = tick(sums[-1], feed_tasks[layer], later_attn)
        attn_sums = [weight_gradients(attn_pairs(0, own_wide), 0), came]
        if layer == 0:
            attn_tasks[0] = Task(wires.reduce_ring(attn_sums))
        gradient = grad_middle + wires.rows_out(sums)
        qkv_sums = [part.reshape(3, inner)[::2] for part in (own_sums, part_sums)]
        vector_grads[layer] = (
            wires.ordered(qkv_sums[0], qkv_sums[1], 1),
            wires.ordered(hidden_sums[:hidden], hidden_sums[hidden:], 0),
            jnp.stack([jnp.sum(grad_middle, axis=0), jnp.sum(grad_second, axis=0)]),
            jnp.stack([gain_first, gain_second]),
            jnp.stack([shift_first, shift_second]),
        )

    returned_grad = owner_swap(gradient.astype(BF16))
    time_grad = jnp.sum(gradient, axis=0)
    local = [jnp.stack([part[i] for part in vector_grads]) for i in range(5)]
    flat = jnp.concatenate([part.reshape(-1) for part in local[:2] + [time_grad] + local[2:]])
    border = local[0].size + local[1].size
    vector_task = Task(wires.butterfly(flat, border))
    vector_task.finish()
    reduced = [
        (attn_tasks[layer].finish(), feed_tasks[layer].finish()) for layer in range(layer_total)
    ]
    flat, shared = vector_task.result
    grad_tokens = jnp.take(returned_grad, deal_slot, axis=0)
    encoded = jnp.take(returned_out, deal_slot, axis=0)
    if inner % 128 == 0 and hidden % 128 == 0:
        matrices = None
        for layer in reversed(range(layer_total)):
            matrices = matrix_outputs(wires.spot, layer, layer_total, *reduced[layer], matrices)
    else:
        parts = []
        for attn_pair, feed_pair in reduced:
            rows = attn_pair[0].shape[0]
            qkv = [
                part[:, : 3 * inner].reshape(rows, 3, inner).transpose(1, 0, 2).astype(F32)
                for part in attn_pair
            ]
            parts.append(
                (
                    wires.ordered(*qkv, 2),
                    wires.ordered(*(part[:, 3 * inner :].T.astype(F32) for part in attn_pair), 0),
                    wires.ordered(*(part[:, :hidden].astype(F32) for part in feed_pair), 1),
                    wires.ordered(*(part[:, hidden:].T.astype(F32) for part in feed_pair), 0),
                )
            )
        matrices = [jnp.stack([part[i] for part in parts]) for i in range(4)]
    grad_b_qv = flat[: local[0].size].reshape(local[0].shape)
    grad_b_ff1 = flat[local[0].size : border].reshape(local[1].shape)
    time_grad = shared[:D]
    rest = shared[D:].reshape(3, layer_total, 2, D)
    return (
        encoded,
        grad_tokens,
        time_grad,
        matrices[0],
        grad_b_qv,
        matrices[1],
        rest[0],
        rest[1],
        rest[2],
        matrices[2],
        grad_b_ff1,
        matrices[3],
    )


def solution(mesh):
    return jax.shard_map(
        body,
        mesh=mesh,
        in_specs=(
            P(("dp", "tensor"), None),
            P(("dp", "tensor"), None),
            P(("dp", "tensor")),
            P(("dp", "tensor")),
            P("dp", None),
            P(),
            P(None, "dp"),
            P(None, None, "dp", "tensor"),
            P(None, None, "tensor"),
            P(None, "tensor", "dp"),
            P(),
            P(),
            P(),
            P(None, "dp", "tensor"),
            P(None, "tensor"),
            P(None, "tensor", "dp"),
        ),
        out_specs=(
            P(("dp", "tensor"), None),
            P(("dp", "tensor"), None),
            P(),
            P(None, None, "dp", "tensor"),
            P(None, None, "tensor"),
            P(None, "tensor", "dp"),
            P(),
            P(),
            P(),
            P(None, "dp", "tensor"),
            P(None, "tensor"),
            P(None, "tensor", "dp"),
        ),
        check_vma=False,
    )
```

```python
import math

import jax
import jax.numpy as jnp
import numpy as np
from jax import lax
from jax.experimental import pallas as pl
from jax.experimental.pallas import tpu as pltpu
from jax.sharding import PartitionSpec as P

D = 1024
HEADS = 16
FF = 4096
HEAD = D // HEADS
F32 = jnp.float32
BF16 = jnp.bfloat16
SMALL_COST = pl.CostEstimate(flops=1000, bytes_accessed=1000, transcendentals=0)


def layer_norm(summed, scaling, offset_vec):
    centre = jnp.mean(summed, axis=-1, keepdims=True)
    spread = summed - centre
    variance = jnp.mean(spread * spread, axis=-1, keepdims=True)
    return spread * lax.rsqrt(variance + 1e-05) * scaling + offset_vec


def dot(left, right):
    return jnp.dot(left, right, preferred_element_type=F32)


def contract_rows(left, right):
    return lax.dot_general(left, right, (((0,), (0,)), ((), ())), preferred_element_type=F32)


def times_transposed(left, right):
    return lax.dot_general(left, right, (((1,), (1,)), ((), ())), preferred_element_type=F32)


class Wires:
    def __init__(self, dp_size, tensor_size):
        self.dp_size, self.tensor_size = dp_size, tensor_size
        chips = dp_size // 2
        self.chips = chips
        order = list(range(0, chips, 2)) + list(range(chips - 1, 0, -2))
        place = {chip: spot for spot, chip in enumerate(order)}
        self.rounds = chips // 2
        ahead, spots = [], np.zeros((dp_size, chips + 1), np.int32)
        for device in range(dp_size):
            chip, core = divmod(device, 2)
            way = 1 if core == 0 else -1
            ahead.append((device, 2 * order[(place[chip] + way) % chips] + core))
            spots[device, :chips] = [order[(place[chip] + way * s) % chips] for s in range(chips)]
            spots[device, chips] = core
        self.ahead = ahead
        self.back = [(there, here) for here, there in ahead]
        self.swap = [(d, d ^ 1) for d in range(dp_size)]
        dp_index = lax.axis_index("dp")
        self.core = dp_index % 2
        self.spot = lax.dynamic_index_in_dim(jnp.asarray(spots), dp_index, 0, keepdims=False)

    def round(self, forth, back):
        if back is None:
            return [lax.ppermute(forth, "dp", self.ahead)]
        return [lax.ppermute(forth, "dp", self.ahead), lax.ppermute(back, "dp", self.back)]

    def partner(self, array):
        return lax.ppermute(array, "dp", self.swap)

    def across(self, array):
        return lax.ppermute(array, "tensor", [(0, 1), (1, 0)])

    def half(self, array, axis, mine):
        width = array.shape[axis] // 2
        index = self.core if mine else 1 - self.core
        return lax.dynamic_slice_in_dim(array, index * width, width, axis)

    def ordered(self, mine, other, axis):
        return jnp.where(
            self.core == 0,
            jnp.concatenate([mine, other], axis),
            jnp.concatenate([other, mine], axis),
        )

    def chip_piece(self, shard):
        mine, other = shard
        return self.ordered(mine, self.partner(other), 0)

    def gather_ring(self, piece, extra=None):
        chip_rows = piece.shape[0]
        if extra is not None:
            tail = jnp.zeros((8, piece.shape[1]), piece.dtype)
            pair = self.ordered(extra, self.partner(extra), 0)
            tail = lax.dynamic_update_slice(tail, pair[None, :], (0, 0))
            piece = jnp.concatenate([piece, tail], 0)
        piece = yield piece
        forth, back = [piece], [piece]
        for step in range(1, self.rounds + 1):
            both_ways = step < self.chips - self.rounds
            came = yield self.round(forth[-1], back[-1] if both_ways else None)
            forth.append(came[0])
            back += came[1:]
            if step == self.rounds - 1:
                places = [0] + [-s % self.chips for s in range(1, len(forth))] + list(range(1, len(back)))
                outs = place_pieces(self.spot, places, forth + back[1:], chip_rows, None)
        outs = place_pieces(self.spot, [-self.rounds % self.chips], forth[-1:], chip_rows, outs)
        whole, vector = outs[0], outs[-1]
        halves = (whole, self.partner(whole))
        return halves if extra is None else (halves, vector[:, 0, :chip_rows].reshape(-1))

    def first_portions(self, sums):
        return add_portions(self.spot, [self.rounds, 1 + self.rounds], [], sums)

    def reduce_ring(self, sums, first=None):
        forth, back = first or self.first_portions(sums)
        for step in range(1, self.rounds + 1):
            both_ways = step < self.chips - self.rounds
            came = yield self.round(forth, back if both_ways else None)
            places = [self.rounds - step] if step < self.rounds else []
            if step + 1 < self.chips - self.rounds:
                places.append(1 + self.rounds + step)
            added = add_portions(self.spot, places, came, sums) if places else []
            forth = added[0] if step < self.rounds else came[0]
            if both_ways:
                back = added[1] if len(places) == 2 else came[1]
        mine, other = last_portion(self.spot, [forth, back], sums)
        return mine, self.partner(other)

    def rows_in(self, local_rows):
        if self.tensor_size == 2:
            return [local_rows, self.across(local_rows)]
        return [lax.all_gather(local_rows, "tensor", axis=0, tiled=True)]

    def rows_out(self, sums):
        if self.tensor_size == 2:
            return sums[0] + self.across(sums[1]).astype(F32)
        return lax.psum_scatter(sums[0], "tensor", scatter_dimension=0, tiled=True).astype(F32)

    def butterfly(self, array, border):
        for axis, size in (("dp", self.dp_size), ("tensor", self.tensor_size)):
            if axis == "tensor":
                array, kept = array[border:], array
            bit = 1
            while bit < size:
                pairs = [(i, i ^ bit) for i in range(size)]
                array = array + (yield lax.ppermute(array, axis, pairs))
                bit *= 2
        return kept, array


def pick(rows, index):
    return rows.at[index].get(mode="promise_in_bounds")


def owner_swap(rows):
    return lax.all_to_all(rows, "dp", split_axis=0, concat_axis=0, tiled=True)


class Task:
    def __init__(self, steps):
        self.steps, self.done, self.result = steps, False, None
        self.advance(None, first=True)

    def advance(self, arrived, first=False):
        try:
            self.pending = next(self.steps) if first else self.steps.send(arrived)
        except StopIteration as stop:
            self.done, self.result = True, stop.value

    def finish(self):
        while not self.done:
            self.advance(self.pending)
        return self.result


def tick(value, *tasks):
    tasks = [task for task in tasks if task is not None and not task.done]
    if not tasks:
        return value
    value, arrived = lax.optimization_barrier((value, [task.pending for task in tasks]))
    for task, part in zip(tasks, arrived):
        task.advance(part)
    return value


def tie(*values):
    return lax.optimization_barrier(values)


def place_pieces(spot, places, pieces, chip_rows, filled):
    count, width = len(pieces), pieces[0].shape[1]
    chips = spot.shape[0] - 1
    spare = pieces[0].shape[0] - chip_rows
    given = 0 if filled is None else len(filled)

    def kernel(spot_ref, *refs):
        ins, outs, sems = refs[:count], refs[count + given : -1], refs[-1]
        copies = []
        for i, piece in enumerate(ins):
            chip = spot_ref[places[i]]
            rows = pl.ds(pl.multiple_of(chip * chip_rows, chip_rows), chip_rows)
            copies.append(
                pltpu.make_async_copy(piece.at[0:chip_rows], outs[0].at[rows], sems.at[i, 0])
            )
            if spare:
                copies.append(
                    pltpu.make_async_copy(
                        piece.at[chip_rows : chip_rows + spare, 0:128],
                        outs[1].at[chip],
                        sems.at[i, 1],
                    )
                )
        for copy in copies:
            copy.start()
        for copy in copies:
            copy.wait()

    shapes = [jax.ShapeDtypeStruct((chips * chip_rows, width), BF16)]
    if spare:
        shapes.append(jax.ShapeDtypeStruct((chips, spare, 128), BF16))
    return pl.pallas_call(
        kernel,
        out_shape=shapes,
        in_specs=[pl.BlockSpec(memory_space=pltpu.SMEM)]
        + [pl.BlockSpec(memory_space=pl.ANY)] * (count + given),
        out_specs=[pl.BlockSpec(memory_space=pl.ANY)] * len(shapes),
        scratch_shapes=[pltpu.SemaphoreType.DMA((count, 2))],
        input_output_aliases={1 + count + i: i for i in range(given)},
        compiler_params=pltpu.CompilerParams(vmem_limit_bytes=16 << 20),
        cost_estimate=pl.CostEstimate(
            flops=0, bytes_accessed=1 << 26, transcendentals=0
        ),
        name="place_pieces",
    )(spot, *pieces, *(filled or ()))


def attend_forward(blocks, weight, bias, segment, earlier=None):
    rows = sum(block.shape[0] for block in blocks)
    inner = weight.shape[1] // 4
    heads = inner // HEAD
    step = min(512, rows)
    scale = 1.0 / math.sqrt(HEAD)
    extra = 0 if earlier is None else 2

    def kernel(*refs):
        xs, refs = refs[: len(blocks)], refs[len(blocks) :]
        w_ref, bias_ref, col_ref, row_ref = refs[:4]
        before, refs = refs[4 : 4 + extra], refs[4 + extra :]
        qkv_ref, out_ref, log_ref = refs[:3]
        start = 0
        for x in xs:
            size = x.shape[0]
            projected = dot(x[...], w_ref[:, : 3 * inner]) + bias_ref[...]
            qkv_ref[start : start + size, :] = projected.astype(BF16)
            start += size
        for first in range(0, rows, step):
            part = slice(first, first + step)
            far = jnp.where(col_ref[...] == row_ref[:, part], 0.0, -1e30)
            mixed = []
            for h in range(heads):
                lanes = [slice(i * inner + h * HEAD, i * inner + (h + 1) * HEAD) for i in range(3)]
                scores = times_transposed(qkv_ref[:, lanes[1]], qkv_ref[part, lanes[0]])
                scores = scores * scale + far
                highest = jnp.max(scores, axis=0, keepdims=True)
                powers = jnp.exp(scores - highest)
                summed = jnp.sum(powers, axis=0, keepdims=True)
                mixture = contract_rows(qkv_ref[:, lanes[2]], powers.astype(BF16))
                mixed.append(mixture * (1.0 / summed))
                log_ref[h : h + 1, part] = highest + jnp.log(summed)
            out_ref[part, :] = jnp.concatenate(mixed, 0).T.astype(BF16)
        start = 0
        for sum_ref in refs[3:]:
            part = slice(start, start + sum_ref.shape[0])
            start += sum_ref.shape[0]
            total = times_transposed(before[0][part, :], before[1][:, 3 * inner :])
            total += times_transposed(out_ref[part, :], w_ref[:, 3 * inner :])
            sum_ref[...] = total.astype(sum_ref.dtype)

    shapes = [
        jax.ShapeDtypeStruct((rows, 3 * inner), BF16),
        jax.ShapeDtypeStruct((rows, inner), BF16),
        jax.ShapeDtypeStruct((heads, rows), F32),
    ]
    if earlier is not None:
        shapes += sum_shapes(blocks)
    outs = pl.pallas_call(
        kernel,
        out_shape=shapes,
        compiler_params=pltpu.CompilerParams(vmem_limit_bytes=32 << 20),
        cost_estimate=SMALL_COST,
        name="attend_forward",
    )(*blocks, weight, bias[None], segment[:, None], segment[None], *(earlier or ()))
    return tuple(outs[:3]), list(outs[3:])


def sum_shapes(blocks):
    kinds = (F32, BF16) if len(blocks) == 2 else (BF16,)
    return [jax.ShapeDtypeStruct(block.shape, kind) for block, kind in zip(blocks, kinds)]


def attend_backward(blocks, weight, qkv, mixture, log_total, segment, earlier=None):
    rows = sum(block.shape[0] for block in blocks)
    inner = weight.shape[1] // 4
    extra = 0 if earlier is None else 2
    heads = inner // HEAD
    step = min(512, rows)
    scale = 1.0 / math.sqrt(HEAD)

    def kernel(*refs):
        xs = refs[: len(blocks)]
        (w_ref, qkv_ref, mix_ref, log_ref, col_ref, row_ref) = refs[len(blocks) : len(blocks) + 6]
        refs = refs[len(blocks) + 6 :]
        before, refs = refs[:extra], refs[extra:]
        grad_ref, sum_ref, dout_ref = refs[0], refs[1], refs[-1]
        start = 0
        for x in xs:
            size = x.shape[0]
            dout_ref[start : start + size, :] = dot(x[...], w_ref[:, 3 * inner :]).astype(BF16)
            start += size
        ones = jnp.ones((8, HEAD), F32)
        keys = [jnp.zeros((rows, HEAD), F32)] * heads
        values = [jnp.zeros((rows, HEAD), F32)] * heads
        for first in range(0, rows, step):
            part = slice(first, first + step)
            far = jnp.where(col_ref[...] == row_ref[:, part], 0.0, -1e30)
            queries = []
            for h in range(heads):
                lanes = [slice(i * inner + h * HEAD, i * inner + (h + 1) * HEAD) for i in range(3)]
                query, key = qkv_ref[part, lanes[0]], qkv_ref[:, lanes[1]]
                dout = dout_ref[part, lanes[0]]
                scores = times_transposed(key, query) * scale + far
                weights = jnp.exp(scores - log_ref[h : h + 1, part])
                product = dout.astype(F32) * mix_ref[part, lanes[0]].astype(F32)
                centre = lax.dot_general(
                    ones,
                    product,
                    (((1,), (1,)), ((), ())),
                    precision=lax.Precision.HIGHEST,
                    preferred_element_type=F32,
                )[0:1]
                grad_weights = times_transposed(qkv_ref[:, lanes[2]], dout)
                grad_scores = (weights * (grad_weights - centre)).astype(BF16)
                queries.append(contract_rows(key, grad_scores))
                keys[h] = keys[h] + dot(grad_scores, query)
                values[h] = values[h] + dot(weights.astype(BF16), dout)
            grad_ref[part, 0:inner] = (jnp.concatenate(queries, 0).T * scale).astype(BF16)
        for h in range(heads):
            grad_ref[:, inner + h * HEAD : inner + (h + 1) * HEAD] = (keys[h] * scale).astype(BF16)
            grad_ref[:, 2 * inner + h * HEAD : 2 * inner + (h + 1) * HEAD] = values[h].astype(BF16)
        sum_ref[...] = jnp.sum(grad_ref[...].astype(F32), axis=0, keepdims=True)
        start = 0
        for out_ref in refs[2:-1]:
            part = slice(start, start + out_ref.shape[0])
            start += out_ref.shape[0]
            total = times_transposed(before[0][part, :], before[1][:, : 3 * inner])
            total += times_transposed(grad_ref[part, :], w_ref[:, : 3 * inner])
            out_ref[...] = total.astype(out_ref.dtype)

    shapes = [
        jax.ShapeDtypeStruct((rows, 3 * inner), BF16),
        jax.ShapeDtypeStruct((1, 3 * inner), F32),
    ]
    if earlier is not None:
        shapes += sum_shapes(blocks)
    outs = pl.pallas_call(
        kernel,
        out_shape=shapes,
        scratch_shapes=[pltpu.VMEM((rows, inner), BF16)],
        compiler_params=pltpu.CompilerParams(vmem_limit_bytes=32 << 20),
        cost_estimate=SMALL_COST,
        name="attend_backward",
    )(*blocks, weight, qkv, mixture, log_total, segment[:, None], segment[None], *(earlier or ()))
    return outs[0], outs[1], list(outs[2:])


def normal_parts(x):
    bell = jnp.exp(-0.5 * x * x)
    t = 1.0 / (1.0 + 0.23164189 * jnp.abs(x))
    tail = 0.5307027145
    for c in (-0.7265760135, 0.7107068705, -0.142248368, 0.127414796):
        tail = tail * t + c
    tail = tail * t * bell
    return jnp.where(x >= 0.0, 1.0 - tail, tail), bell * 0.3989422804014327


def feed(blocks, weights, side, forward):
    rows = sum(block.shape[0] for block in blocks)
    hidden = weights[0].shape[1] // 2
    tile = min(512, hidden)
    tiles = hidden // tile
    into, onto = (0, hidden) if forward else (hidden, 0)

    def kernel(*refs):
        xs, refs = refs[: len(blocks)], refs[len(blocks) :]
        *halves, side_ref = refs[:3]
        outs, (kept_ref, more_ref, pre_ref) = refs[3:-3], refs[-3:]

        def project(half, index):
            start, slot = 0, lax.rem(index, 2)
            first = index * tile + into
            if not isinstance(index, int):
                first = pl.multiple_of(first, tile)
            for x in xs:
                part = pl.ds(start, x.shape[0])
                pre_ref[slot, part, :] = dot(x[...], halves[half][:, pl.ds(first, tile)])
                start += x.shape[0]

        def activate(half, index):
            first = index * tile + half * hidden
            if not isinstance(index, int):
                first = pl.multiple_of(first, tile)
            columns = pl.ds(first, tile)
            pre = pre_ref[lax.rem(index, 2)]
            if forward:
                pre = pre + side_ref[:, columns]
                cdf, bell = normal_parts(pre)
                kept_ref[:, columns] = (pre * cdf).astype(BF16)
                more_ref[:, columns] = (cdf + pre * bell).astype(BF16)
            else:
                kept = (pre * side_ref[:, columns].astype(F32)).astype(BF16)
                kept_ref[:, columns] = kept
                more_ref[:, columns] = jnp.sum(kept.astype(F32), axis=0, keepdims=True)

        for half in (0, 1):
            project(half, 0)

            def step(index, _, half=half):
                project(half, index)
                activate(half, index - 1)
                return 0

            lax.fori_loop(1, tiles, step, 0)
            activate(half, tiles - 1)
        start = 0
        for out in outs:
            part = slice(start, start + out.shape[0])
            start += out.shape[0]
            total = times_transposed(kept_ref[part, 0:hidden], halves[0][:, onto : onto + hidden])
            total += times_transposed(kept_ref[part, hidden:], halves[1][:, onto : onto + hidden])
            out[...] = total.astype(out.dtype)

    wide = jax.ShapeDtypeStruct((rows, 2 * hidden), BF16)
    outs = pl.pallas_call(
        kernel,
        out_shape=sum_shapes(blocks)
        + [wide, wide if forward else jax.ShapeDtypeStruct((1, 2 * hidden), F32)],
        scratch_shapes=[pltpu.VMEM((2, rows, tile), F32)],
        compiler_params=pltpu.CompilerParams(vmem_limit_bytes=32 << 20),
        cost_estimate=SMALL_COST,
        name="feed_forward" if forward else "feed_backward",
    )(*blocks, *weights, side)
    return list(outs[:-2]), outs[-2], outs[-1]


def weight_gradients(pairs, half):
    widths = [width for _, _, width in pairs]
    tile = math.gcd(256, *widths)
    if tile % 128:
        terms = [
            contract_rows(join(blocks), _columns(right, half, width))
            for blocks, right, width in pairs
        ]
        return jnp.concatenate(terms, 1).astype(BF16)
    counts = [width // tile for width in widths]
    edge = counts[0]
    blocks_flat = [block for blocks, _, _ in pairs for block in blocks]
    per = len(pairs[0][0])
    rows = sum(block.shape[0] for block in pairs[0][0])

    def kernel(*refs):
        lefts, refs = refs[: 2 * per], refs[2 * per :]
        rights, (out_ref, turned) = refs[:2], refs[2:]
        index = pl.program_id(0)

        @pl.when(index == 0)
        def _():
            for pair in (0, 1):
                start = 0
                for left in lefts[pair * per : (pair + 1) * per]:
                    turned[pair, :, start : start + left.shape[0]] = left[...].T
                    start += left.shape[0]

        def run(pair):
            out_ref[...] = dot(turned[pair], rights[pair][...]).astype(BF16)

        @pl.when(index < edge)
        def _():
            run(0)

        @pl.when(index >= edge)
        def _():
            run(1)

    shifts = [
        half * counts[i] if pairs[i][1].shape[1] > widths[i] else 0 for i in (0, 1)
    ]
    last = counts[1] - 1
    specs = [pl.BlockSpec(block.shape, lambda i: (0, 0)) for block in blocks_flat]
    specs += [
        pl.BlockSpec((rows, tile), lambda i: (0, jnp.minimum(i, edge - 1) + shifts[0])),
        pl.BlockSpec((rows, tile), lambda i: (0, jnp.clip(i - edge, 0, last) + shifts[1])),
    ]
    over = pl.BlockSpec((D, tile), lambda i: (0, i))
    return pl.pallas_call(
        kernel,
        grid=(sum(counts),),
        out_shape=jax.ShapeDtypeStruct((D, sum(widths)), BF16),
        in_specs=specs,
        out_specs=over,
        scratch_shapes=[pltpu.VMEM((2, D, rows), BF16)],
        compiler_params=pltpu.CompilerParams(vmem_limit_bytes=24 << 20),
        cost_estimate=SMALL_COST,
        name="weight_gradients",
    )(*blocks_flat, pairs[0][1], pairs[1][1])


def _columns(right, half, width):
    return right[:, half * width : (half + 1) * width] if right.shape[1] > width else right


def add_portions(spot, places, came, sums):
    count, given = len(places), min(len(came), len(places))
    shape = (sums[0].shape[0] // (spot.shape[0] - 1), sums[0].shape[1])

    def kernel(spot_ref, *refs):
        ins, parts, outs = refs[:given], refs[given:-count], refs[-count:]
        for i, out in enumerate(outs):
            total = sum(part[...].astype(F32) for part in parts[i * len(sums) : (i + 1) * len(sums)])
            if given:
                total += ins[i][...].astype(F32)
            out[...] = total.astype(BF16)

    whole = pl.BlockSpec(shape, lambda i, s: (0, 0))
    portions = [pl.BlockSpec(shape, lambda i, s, k=k: (s[k], 0)) for k in places for _ in sums]
    return pl.pallas_call(
        kernel,
        grid_spec=pltpu.PrefetchScalarGridSpec(
            num_scalar_prefetch=1,
            grid=(1,),
            in_specs=[whole] * given + portions,
            out_specs=[whole] * count,
        ),
        out_shape=[jax.ShapeDtypeStruct(shape, BF16)] * count,
        compiler_params=pltpu.CompilerParams(vmem_limit_bytes=24 << 20),
        cost_estimate=SMALL_COST,
        name="add_portions",
    )(spot, *came[:given], *(list(sums) * count))


def last_portion(spot, came, sums):
    chips = spot.shape[0] - 1
    shape = (sums[0].shape[0] // chips, sums[0].shape[1])
    rows = shape[0] // 2

    def kernel(spot_ref, *refs):
        ins, (mine, other, total) = refs[:-3], refs[-3:]
        total[...] = sum(part[...].astype(F32) for part in ins)
        first = pl.multiple_of(spot_ref[chips] * rows, rows)
        mine[...] = total[pl.ds(first, rows), :]
        other[...] = total[pl.ds(rows - first, rows), :].astype(BF16)

    whole = pl.BlockSpec(shape, lambda i, s: (0, 0))
    half = pl.BlockSpec((rows, shape[1]), lambda i, s: (0, 0))
    return pl.pallas_call(
        kernel,
        grid_spec=pltpu.PrefetchScalarGridSpec(
            num_scalar_prefetch=1,
            grid=(1,),
            in_specs=[whole] * len(came) + [pl.BlockSpec(shape, lambda i, s: (s[0], 0))] * len(sums),
            out_specs=[half] * 2,
            scratch_shapes=[pltpu.VMEM(shape, F32)],
        ),
        out_shape=[
            jax.ShapeDtypeStruct((rows, shape[1]), F32),
            jax.ShapeDtypeStruct((rows, shape[1]), BF16),
        ],
        compiler_params=pltpu.CompilerParams(vmem_limit_bytes=24 << 20),
        cost_estimate=SMALL_COST,
        name="last_portion",
    )(spot, *came, *sums)


def matrix_outputs(spot, layer, layer_total, attn_pair, feed_pair, filled):
    rows, inner, hidden = attn_pair[0].shape[0], attn_pair[0].shape[1] // 4, feed_pair[0].shape[1] // 2
    chips = spot.shape[0] - 1
    shapes = [
        (layer_total, 3, rows, 2 * inner),
        (layer_total, rows, 2 * inner),
        (layer_total, rows, 2 * hidden),
        (layer_total, rows, 2 * hidden),
    ]
    given = 0 if filled is None else 4

    def kernel(spot_ref, *refs):
        pairs, (qkv, out, first, second) = (refs[0:2], refs[2:4]), refs[4 + given :]
        for index in (0, 1):
            attn, feed = (pair[index][...].astype(F32) for pair in pairs)
            core = spot_ref[chips] if index == 0 else 1 - spot_ref[chips]
            heads = pl.ds(pl.multiple_of(core * inner, inner), inner)
            units = pl.ds(pl.multiple_of(core * hidden, hidden), hidden)
            for i in range(3):
                qkv[0, i, :, heads] = attn[:, i * inner : (i + 1) * inner]
            out[0, :, heads] = attn[:, 3 * inner :]
            first[0, :, units] = feed[:, :hidden]
            second[0, :, units] = feed[:, hidden:]

    def over(shape):
        return pl.BlockSpec((1,) + shape[1:], lambda i, s: (layer,) + (0,) * (len(shape) - 1))

    ins = (*attn_pair, *feed_pair)
    return pl.pallas_call(
        kernel,
        grid_spec=pltpu.PrefetchScalarGridSpec(
            num_scalar_prefetch=1,
            grid=(1,),
            in_specs=[pl.BlockSpec(part.shape, lambda i, s: (0, 0)) for part in ins]
            + [pl.BlockSpec(memory_space=pl.ANY)] * given,
            out_specs=[over(shape) for shape in shapes],
        ),
        out_shape=[jax.ShapeDtypeStruct(shape, F32) for shape in shapes],
        input_output_aliases={5 + i: i for i in range(given)},
        compiler_params=pltpu.CompilerParams(vmem_limit_bytes=24 << 20),
        cost_estimate=SMALL_COST,
        name="matrix_outputs",
    )(spot, *ins, *(filled or ()))


def join(blocks):
    return blocks[0] if len(blocks) == 1 else jnp.concatenate(blocks, 0)


def body(
    tokens,
    cotangent,
    deal_slot,
    back_slot,
    lengths,
    time_step,
    time_table,
    w_qkv,
    b_qv,
    w_out,
    out_bias,
    ln_gain,
    ln_shift,
    w_ff1,
    b_ff1,
    w_ff2,
):
    wires = Wires(lax.axis_size("dp"), lax.axis_size("tensor"))
    rows_dev = tokens.shape[0]
    group_rows = rows_dev * wires.tensor_size
    tensor_index = lax.axis_index("tensor")
    layer_total = w_qkv.shape[0]
    inner = w_qkv.shape[3] // 2
    hidden = w_ff1.shape[2] // 2
    both = (True, False)

    time_piece = lax.dynamic_index_in_dim(time_table, time_step[0], 0, keepdims=False)

    def rings(layer, arrays, extra):
        w_qkv, w_out, w_ff1, w_ff2 = arrays
        attn_shard, feed_shard = [], []
        for mine in both:
            qkv = wires.half(w_qkv[layer], 2, mine)
            out = wires.half(w_out[layer], 0, mine).T
            attn_shard.append(jnp.concatenate([qkv[0], qkv[1], qkv[2], out], axis=1))
            first = wires.half(w_ff1[layer], 1, mine)
            second = wires.half(w_ff2[layer], 0, mine).T
            feed_shard.append(jnp.concatenate([first, second], axis=1))
        return (
            Task(wires.gather_ring(wires.chip_piece(attn_shard), extra)),
            Task(wires.gather_ring(wires.chip_piece(feed_shard))),
        )

    arrays = (w_qkv, w_out, w_ff1, w_ff2)
    attn_rings, feed_rings = [None] * (layer_total + 1), [None] * (layer_total + 1)
    attn_rings[0], feed_rings[0] = rings(0, arrays, time_piece)
    for layer in range(1, layer_total):
        attn_rings[layer], feed_rings[layer] = rings(layer, arrays, None)
    later = attn_rings[1:-1] + feed_rings[1:-1]
    step = 0
    while not attn_rings[0].done:
        beside = (attn_rings[0], feed_rings[0] if step % 2 or step == 4 else None)
        if step == 1:
            tokens, back_slot = tick((tokens, back_slot), *beside)
            own_tokens = owner_swap(pick(tokens, back_slot))
        elif step == 2:
            own_tokens = tick(own_tokens, *beside)
            token_blocks = wires.rows_in(own_tokens)
        elif step == 4:
            token_blocks[-1] = tick(token_blocks[-1], *beside)
            token_blocks[-1], *pieces = tie(token_blocks[-1], *(task.pending for task in later))
            for task, piece in zip(later, pieces):
                task.pending = piece
        else:
            tick((), *beside)
        step += 1
    attn_w, time_row = attn_rings[0].result
    time_row = time_row.astype(F32)

    seq_ends = jnp.cumsum(lengths[0])
    positions = jnp.arange(group_rows, dtype=jnp.int32)
    if wires.tensor_size == 2:
        positions = (positions + tensor_index * rows_dev) % group_rows
    segment = jnp.sum((positions[:, None] >= seq_ends[None, :]).astype(jnp.int32), axis=1)

    stream = own_tokens.astype(F32) + time_row
    weights, saved = [], []
    for layer in range(layer_total):
        if layer == 0:
            input_blocks = [(rows.astype(F32) + time_row).astype(BF16) for rows in token_blocks]
        else:
            input_blocks = wires.rows_in(stream.astype(BF16))
            input_blocks[-1] = tick(input_blocks[-1], feed_rings[layer])
            attn_w = attn_rings[layer].finish()
        ahead = (attn_rings[layer + 1], feed_rings[layer + 1])
        biases = []
        for mine in both:
            bias_q, bias_v = [wires.half(b_qv[layer, i], 0, mine) for i in (0, 1)]
            biases.append(jnp.concatenate([bias_q, jnp.zeros_like(bias_q), bias_v]))
        (qkv, mixture, log_total), _ = attend_forward(input_blocks, attn_w[0], biases[0], segment)
        attention = [(qkv, mixture, log_total)]
        part, sums = attend_forward(
            input_blocks, attn_w[1], biases[1], segment, (mixture, attn_w[0])
        )
        attention.append(part)
        sums[-1] = tick(sums[-1], feed_rings[layer], ahead[0])
        attended = tick(wires.rows_out(sums), feed_rings[layer], *ahead)
        middle = stream + attended + out_bias[layer, 0]
        normed = layer_norm(middle, ln_gain[layer, 0], ln_shift[layer, 0])
        normed_low = normed.astype(BF16)
        normed_blocks = wires.rows_in(normed_low)
        normed_blocks[-1] = tick(normed_blocks[-1], *ahead)
        feed_w = feed_rings[layer].finish()
        weights.append((attn_w, feed_w))
        bias = jnp.concatenate([wires.half(b_ff1[layer], 0, mine) for mine in both])[None]
        sums, *filled = feed(normed_blocks, feed_w, bias, True)
        if layer == 0:
            sums[-1], cotangent = tie(sums[-1], cotangent)
            upstream = owner_swap(pick(cotangent, back_slot))
        sums[-1] = tick(sums[-1], ahead[0])
        arrived = tick(wires.rows_out(sums), *ahead)
        second_sum = normed + arrived + out_bias[layer, 1]
        saved.append((input_blocks, attention, middle, normed_blocks, filled, second_sum))
        stream = layer_norm(second_sum, ln_gain[layer, 1], ln_shift[layer, 1])

    encoded_own = stream.astype(BF16)
    gradient = upstream.astype(F32)
    feed_tasks, attn_tasks = [None] * (layer_total + 1), [None] * (layer_total + 1)
    attn_sums, reduced, matrices = None, [None] * layer_total, None
    direct = inner % 128 == 0 and hidden % 128 == 0
    vector_grads = [None] * layer_total
    for layer in reversed(range(layer_total)):
        attn_w, feed_w = weights[layer]
        input_blocks, attention, middle, normed_blocks, (act, slope), second_sum = saved[layer]
        _, pull_second = jax.vjp(layer_norm, second_sum, ln_gain[layer, 1], ln_shift[layer, 1])
        grad_second, gain_second, shift_second = pull_second(gradient)
        later_feed, later_attn = feed_tasks[layer + 1], None
        send = tick(grad_second.astype(BF16), later_feed)
        if layer == layer_total - 1:
            send, encoded_own = tie(send, encoded_own)
            returned_out = owner_swap(encoded_own)
        if attn_sums is not None:
            send, *attn_sums = tie(send, *attn_sums)
            later_attn = attn_tasks[layer + 1] = Task(wires.reduce_ring(attn_sums))
        branch_blocks = wires.rows_in(send)
        branch_blocks[-1] = tick(branch_blocks[-1], later_feed, later_attn)
        sums, grad_pre, hidden_sums = feed(branch_blocks, feed_w, slope, False)
        hidden_sums = hidden_sums[0]
        pairs = [(normed_blocks, grad_pre, hidden), (branch_blocks, act, hidden)]
        came = wires.partner(weight_gradients(pairs, 1))
        grad_normed = grad_second + wires.rows_out(sums)
        grad_normed = tick(grad_normed, later_attn)
        _, pull_first = jax.vjp(layer_norm, middle, ln_gain[layer, 0], ln_shift[layer, 0])
        grad_middle, gain_first, shift_first = pull_first(grad_normed)
        send, *feed_sums = tie(grad_middle.astype(BF16), weight_gradients(pairs, 0), came)
        feed_tasks[layer] = Task(wires.reduce_ring(feed_sums))
        attend_blocks = wires.rows_in(send)
        attend_blocks[-1] = tick(attend_blocks[-1], feed_tasks[layer], later_attn)

        def attn_pairs(half, wide):
            return [(input_blocks, wide, 3 * inner), (attend_blocks, attention[half][1], inner)]

        wide, part_sums, _ = attend_backward(attend_blocks, attn_w[1], *attention[1], segment)
        send = weight_gradients(attn_pairs(1, wide), 1)
        came = wires.partner(send)
        own_wide, own_sums, sums = attend_backward(
            attend_blocks, attn_w[0], *attention[0], segment, (wide, attn_w[1])
        )
        sums[-1] = tick(sums[-1], feed_tasks[layer], later_attn)
        attn_sums = [weight_gradients(attn_pairs(0, own_wide), 0), came]
        if layer == 0:
            first_portions = wires.first_portions(attn_sums)
        arrived = wires.rows_out(sums)
        if layer + 1 < layer_total:
            reduced[layer + 1] = (later_attn.finish(), later_feed.finish())
            if direct:
                matrices = matrix_outputs(
                    wires.spot, layer + 1, layer_total, *reduced[layer + 1], matrices
                )
                arrived, matrices = tie(arrived, matrices)
        if layer == 0:
            arrived, encoded = tie(arrived, pick(returned_out, deal_slot))
            attn_tasks[0] = Task(wires.reduce_ring(attn_sums, first_portions))
        gradient = grad_middle + arrived
        qkv_sums = [part.reshape(3, inner)[::2] for part in (own_sums, part_sums)]
        vector_grads[layer] = (
            wires.ordered(qkv_sums[0], qkv_sums[1], 1),
            wires.ordered(hidden_sums[:hidden], hidden_sums[hidden:], 0),
            jnp.stack([jnp.sum(grad_middle, axis=0), jnp.sum(grad_second, axis=0)]),
            jnp.stack([gain_first, gain_second]),
            jnp.stack([shift_first, shift_second]),
        )

    returned_grad = owner_swap(gradient.astype(BF16))
    time_grad = jnp.sum(gradient, axis=0)
    local = [jnp.stack([part[i] for part in vector_grads]) for i in range(5)]
    flat = jnp.concatenate([part.reshape(-1) for part in local[:2] + [time_grad] + local[2:]])
    border = local[0].size + local[1].size
    vector_task = Task(wires.butterfly(flat, border))
    vector_task.finish()
    reduced[0] = (attn_tasks[0].finish(), feed_tasks[0].finish())
    flat, shared = vector_task.result
    grad_tokens = pick(returned_grad, deal_slot)
    if direct:
        matrices = matrix_outputs(wires.spot, 0, layer_total, *reduced[0], matrices)
        matrices = [part.transpose(0, 2, 1) if i % 2 else part for i, part in enumerate(matrices)]
    else:
        parts = []
        for attn_pair, feed_pair in reduced:
            rows = attn_pair[0].shape[0]
            qkv = [
                part[:, : 3 * inner].reshape(rows, 3, inner).transpose(1, 0, 2).astype(F32)
                for part in attn_pair
            ]
            parts.append(
                (
                    wires.ordered(*qkv, 2),
                    wires.ordered(*(part[:, 3 * inner :].T.astype(F32) for part in attn_pair), 0),
                    wires.ordered(*(part[:, :hidden].astype(F32) for part in feed_pair), 1),
                    wires.ordered(*(part[:, hidden:].T.astype(F32) for part in feed_pair), 0),
                )
            )
        matrices = [jnp.stack([part[i] for part in parts]) for i in range(4)]
    grad_b_qv = flat[: local[0].size].reshape(local[0].shape)
    grad_b_ff1 = flat[local[0].size : border].reshape(local[1].shape)
    time_grad = shared[:D]
    rest = shared[D:].reshape(3, layer_total, 2, D)
    return (
        encoded,
        grad_tokens,
        time_grad,
        matrices[0],
        grad_b_qv,
        matrices[1],
        rest[0],
        rest[1],
        rest[2],
        matrices[2],
        grad_b_ff1,
        matrices[3],
    )


def solution(mesh):
    return jax.shard_map(
        body,
        mesh=mesh,
        in_specs=(
            P(("dp", "tensor"), None),
            P(("dp", "tensor"), None),
            P(("dp", "tensor")),
            P(("dp", "tensor")),
            P("dp", None),
            P(),
            P(None, "dp"),
            P(None, None, "dp", "tensor"),
            P(None, None, "tensor"),
            P(None, "tensor", "dp"),
            P(),
            P(),
            P(),
            P(None, "dp", "tensor"),
            P(None, "tensor"),
            P(None, "tensor", "dp"),
        ),
        out_specs=(
            P(("dp", "tensor"), None),
            P(("dp", "tensor"), None),
            P(),
            P(None, None, "dp", "tensor"),
            P(None, None, "tensor"),
            P(None, "tensor", "dp"),
            P(),
            P(),
            P(),
            P(None, "dp", "tensor"),
            P(None, "tensor"),
            P(None, "tensor", "dp"),
        ),
        check_vma=False,
    )
```

```python
import math

import jax
import jax.numpy as jnp
import numpy as np
from jax import lax
from jax.experimental import pallas as pl
from jax.experimental.pallas import tpu as pltpu
from jax.sharding import PartitionSpec as P

D = 1024
HEADS = 16
FF = 4096
HEAD = D // HEADS
F32 = jnp.float32
BF16 = jnp.bfloat16
SMALL_COST = pl.CostEstimate(flops=1000, bytes_accessed=1000, transcendentals=0)


def layer_norm(summed, scaling, offset_vec):
    centre = jnp.mean(summed, axis=-1, keepdims=True)
    spread = summed - centre
    variance = jnp.mean(spread * spread, axis=-1, keepdims=True)
    return spread * lax.rsqrt(variance + 1e-05) * scaling + offset_vec


def dot(left, right):
    return jnp.dot(left, right, preferred_element_type=F32)


def contract_rows(left, right):
    return lax.dot_general(left, right, (((0,), (0,)), ((), ())), preferred_element_type=F32)


def times_transposed(left, right):
    return lax.dot_general(left, right, (((1,), (1,)), ((), ())), preferred_element_type=F32)


class Wires:
    def __init__(self, dp_size, tensor_size):
        self.dp_size, self.tensor_size = dp_size, tensor_size
        chips = dp_size // 2
        self.chips = chips
        order = list(range(0, chips, 2)) + list(range(chips - 1, 0, -2))
        place = {chip: spot for spot, chip in enumerate(order)}
        self.rounds = chips // 2
        ahead, spots = [], np.zeros((dp_size, chips + 1), np.int32)
        for device in range(dp_size):
            chip, core = divmod(device, 2)
            way = 1 if core == 0 else -1
            ahead.append((device, 2 * order[(place[chip] + way) % chips] + core))
            spots[device, :chips] = [order[(place[chip] + way * s) % chips] for s in range(chips)]
            spots[device, chips] = core
        self.ahead = ahead
        self.back = [(there, here) for here, there in ahead]
        self.swap = [(d, d ^ 1) for d in range(dp_size)]
        dp_index = lax.axis_index("dp")
        self.core = dp_index % 2
        self.spot = lax.dynamic_index_in_dim(jnp.asarray(spots), dp_index, 0, keepdims=False)

    def round(self, forth, back):
        if back is None:
            return [lax.ppermute(forth, "dp", self.ahead)]
        return [lax.ppermute(forth, "dp", self.ahead), lax.ppermute(back, "dp", self.back)]

    def partner(self, array):
        return lax.ppermute(array, "dp", self.swap)

    def across(self, array):
        return lax.ppermute(array, "tensor", [(0, 1), (1, 0)])

    def half(self, array, axis, mine):
        width = array.shape[axis] // 2
        index = self.core if mine else 1 - self.core
        return lax.dynamic_slice_in_dim(array, index * width, width, axis)

    def ordered(self, mine, other, axis):
        return jnp.where(
            self.core == 0,
            jnp.concatenate([mine, other], axis),
            jnp.concatenate([other, mine], axis),
        )

    def chip_piece(self, shard):
        mine, other = shard
        return self.ordered(mine, self.partner(other), 0)

    def gather_ring(self, piece, extra=None):
        chip_rows = piece.shape[0]
        if extra is not None:
            tail = jnp.zeros((8, piece.shape[1]), piece.dtype)
            pair = self.ordered(extra, self.partner(extra), 0)
            tail = lax.dynamic_update_slice(tail, pair[None, :], (0, 0))
            piece = jnp.concatenate([piece, tail], 0)
        piece = yield piece
        forth, back = [piece], [piece]
        for step in range(1, self.rounds + 1):
            both_ways = step < self.chips - self.rounds
            came = yield self.round(forth[-1], back[-1] if both_ways else None)
            forth.append(came[0])
            back += came[1:]
            if step == self.rounds - 1:
                places = [0] + [-s % self.chips for s in range(1, len(forth))] + list(range(1, len(back)))
                outs = place_pieces(self.spot, places, forth + back[1:], chip_rows, None)
        outs = place_pieces(self.spot, [-self.rounds % self.chips], forth[-1:], chip_rows, outs)
        whole, vector = outs[0], outs[-1]
        halves = (whole, self.partner(whole))
        return halves if extra is None else (halves, vector[:, 0, :chip_rows].reshape(-1))

    def first_portions(self, sums):
        return add_portions(self.spot, [self.rounds, 1 + self.rounds], [], sums)

    def reduce_ring(self, sums, first=None):
        forth, back = first or self.first_portions(sums)
        for step in range(1, self.rounds + 1):
            both_ways = step < self.chips - self.rounds
            came = yield self.round(forth, back if both_ways else None)
            places = [self.rounds - step] if step < self.rounds else []
            if step + 1 < self.chips - self.rounds:
                places.append(1 + self.rounds + step)
            added = add_portions(self.spot, places, came, sums) if places else []
            forth = added[0] if step < self.rounds else came[0]
            if both_ways:
                back = added[1] if len(places) == 2 else came[1]
        mine, other = last_portion(self.spot, [forth, back], sums)
        return mine, self.partner(other)

    def rows_in(self, local_rows):
        if self.tensor_size == 2:
            return [local_rows, self.across(local_rows)]
        return [lax.all_gather(local_rows, "tensor", axis=0, tiled=True)]

    def rows_out(self, sums):
        if self.tensor_size == 2:
            return sums[0] + self.across(sums[1]).astype(F32)
        return lax.psum_scatter(sums[0], "tensor", scatter_dimension=0, tiled=True).astype(F32)

    def butterfly(self, array, border):
        for axis, size in (("dp", self.dp_size), ("tensor", self.tensor_size)):
            if axis == "tensor":
                array, kept = array[border:], array
            bit = 1
            while bit < size:
                pairs = [(i, i ^ bit) for i in range(size)]
                array = array + (yield lax.ppermute(array, axis, pairs))
                bit *= 2
        return kept, array


def pick(rows, index):
    return rows.at[index].get(mode="promise_in_bounds")


def owner_swap(rows):
    return lax.all_to_all(rows, "dp", split_axis=0, concat_axis=0, tiled=True)


class Task:
    def __init__(self, steps):
        self.steps, self.done, self.result = steps, False, None
        self.advance(None, first=True)

    def advance(self, arrived, first=False):
        try:
            self.pending = next(self.steps) if first else self.steps.send(arrived)
        except StopIteration as stop:
            self.done, self.result = True, stop.value

    def finish(self):
        while not self.done:
            self.advance(self.pending)
        return self.result


def tick(value, *tasks):
    tasks = [task for task in tasks if task is not None and not task.done]
    if not tasks:
        return value
    value, arrived = lax.optimization_barrier((value, [task.pending for task in tasks]))
    for task, part in zip(tasks, arrived):
        task.advance(part)
    return value


def tie(*values):
    return lax.optimization_barrier(values)


def place_pieces(spot, places, pieces, chip_rows, filled):
    count, width = len(pieces), pieces[0].shape[1]
    chips = spot.shape[0] - 1
    spare = pieces[0].shape[0] - chip_rows
    given = 0 if filled is None else len(filled)

    def kernel(spot_ref, *refs):
        ins, outs, sems = refs[:count], refs[count + given : -1], refs[-1]
        copies = []
        for i, piece in enumerate(ins):
            chip = spot_ref[places[i]]
            rows = pl.ds(pl.multiple_of(chip * chip_rows, chip_rows), chip_rows)
            copies.append(
                pltpu.make_async_copy(piece.at[0:chip_rows], outs[0].at[rows], sems.at[i, 0])
            )
            if spare:
                copies.append(
                    pltpu.make_async_copy(
                        piece.at[chip_rows : chip_rows + spare, 0:128],
                        outs[1].at[chip],
                        sems.at[i, 1],
                    )
                )
        for copy in copies:
            copy.start()
        for copy in copies:
            copy.wait()

    shapes = [jax.ShapeDtypeStruct((chips * chip_rows, width), BF16)]
    if spare:
        shapes.append(jax.ShapeDtypeStruct((chips, spare, 128), BF16))
    return pl.pallas_call(
        kernel,
        out_shape=shapes,
        in_specs=[pl.BlockSpec(memory_space=pltpu.SMEM)]
        + [pl.BlockSpec(memory_space=pl.ANY)] * (count + given),
        out_specs=[pl.BlockSpec(memory_space=pl.ANY)] * len(shapes),
        scratch_shapes=[pltpu.SemaphoreType.DMA((count, 2))],
        input_output_aliases={1 + count + i: i for i in range(given)},
        compiler_params=pltpu.CompilerParams(vmem_limit_bytes=16 << 20),
        cost_estimate=pl.CostEstimate(
            flops=0, bytes_accessed=1 << 26, transcendentals=0
        ),
        name="place_pieces",
    )(spot, *pieces, *(filled or ()))


def attend_forward(blocks, weight, bias, segment, earlier=None):
    rows = sum(block.shape[0] for block in blocks)
    inner = weight.shape[1] // 4
    heads = inner // HEAD
    step = min(512, rows)
    scale = 1.0 / math.sqrt(HEAD)
    extra = 0 if earlier is None else 2

    def kernel(*refs):
        xs, refs = refs[: len(blocks)], refs[len(blocks) :]
        w_ref, bias_ref, col_ref, row_ref = refs[:4]
        before, refs = refs[4 : 4 + extra], refs[4 + extra :]
        qkv_ref, out_ref, log_ref = refs[:3]
        start = 0
        for x in xs:
            size = x.shape[0]
            projected = dot(x[...], w_ref[:, : 3 * inner]) + bias_ref[...]
            qkv_ref[start : start + size, :] = projected.astype(BF16)
            start += size
        for first in range(0, rows, step):
            part = slice(first, first + step)
            far = jnp.where(col_ref[...] == row_ref[:, part], 0.0, -1e30)
            mixed = []
            for h in range(heads):
                lanes = [slice(i * inner + h * HEAD, i * inner + (h + 1) * HEAD) for i in range(3)]
                scores = times_transposed(qkv_ref[:, lanes[1]], qkv_ref[part, lanes[0]])
                scores = scores * scale + far
                highest = jnp.max(scores, axis=0, keepdims=True)
                powers = jnp.exp(scores - highest)
                summed = jnp.sum(powers, axis=0, keepdims=True)
                mixture = contract_rows(qkv_ref[:, lanes[2]], powers.astype(BF16))
                mixed.append(mixture * (1.0 / summed))
                log_ref[h : h + 1, part] = highest + jnp.log(summed)
            out_ref[part, :] = jnp.concatenate(mixed, 0).T.astype(BF16)
        start = 0
        for sum_ref in refs[3:]:
            part = slice(start, start + sum_ref.shape[0])
            start += sum_ref.shape[0]
            total = times_transposed(before[0][part, :], before[1][:, 3 * inner :])
            total += times_transposed(out_ref[part, :], w_ref[:, 3 * inner :])
            sum_ref[...] = total.astype(sum_ref.dtype)

    shapes = [
        jax.ShapeDtypeStruct((rows, 3 * inner), BF16),
        jax.ShapeDtypeStruct((rows, inner), BF16),
        jax.ShapeDtypeStruct((heads, rows), F32),
    ]
    if earlier is not None:
        shapes += sum_shapes(blocks)
    outs = pl.pallas_call(
        kernel,
        out_shape=shapes,
        compiler_params=pltpu.CompilerParams(vmem_limit_bytes=32 << 20),
        cost_estimate=SMALL_COST,
        name="attend_forward",
    )(*blocks, weight, bias[None], segment[:, None], segment[None], *(earlier or ()))
    return tuple(outs[:3]), list(outs[3:])


def sum_shapes(blocks):
    kinds = (F32, BF16) if len(blocks) == 2 else (BF16,)
    return [jax.ShapeDtypeStruct(block.shape, kind) for block, kind in zip(blocks, kinds)]


def attend_backward(blocks, weight, qkv, mixture, log_total, segment, earlier=None):
    rows = sum(block.shape[0] for block in blocks)
    inner = weight.shape[1] // 4
    extra = 0 if earlier is None else 2
    heads = inner // HEAD
    step = min(512, rows)
    scale = 1.0 / math.sqrt(HEAD)

    def kernel(*refs):
        xs = refs[: len(blocks)]
        (w_ref, qkv_ref, mix_ref, log_ref, col_ref, row_ref) = refs[len(blocks) : len(blocks) + 6]
        refs = refs[len(blocks) + 6 :]
        before, refs = refs[:extra], refs[extra:]
        grad_ref, sum_ref, dout_ref = refs[0], refs[1], refs[-1]
        start = 0
        for x in xs:
            size = x.shape[0]
            dout_ref[start : start + size, :] = dot(x[...], w_ref[:, 3 * inner :]).astype(BF16)
            start += size
        ones = jnp.ones((8, HEAD), F32)
        keys = [jnp.zeros((rows, HEAD), F32)] * heads
        values = [jnp.zeros((rows, HEAD), F32)] * heads
        for first in range(0, rows, step):
            part = slice(first, first + step)
            far = jnp.where(col_ref[...] == row_ref[:, part], 0.0, -1e30)
            queries = []
            for h in range(heads):
                lanes = [slice(i * inner + h * HEAD, i * inner + (h + 1) * HEAD) for i in range(3)]
                query, key = qkv_ref[part, lanes[0]], qkv_ref[:, lanes[1]]
                dout = dout_ref[part, lanes[0]]
                scores = times_transposed(key, query) * scale + far
                weights = jnp.exp(scores - log_ref[h : h + 1, part])
                product = dout.astype(F32) * mix_ref[part, lanes[0]].astype(F32)
                centre = lax.dot_general(
                    ones,
                    product,
                    (((1,), (1,)), ((), ())),
                    precision=lax.Precision.HIGHEST,
                    preferred_element_type=F32,
                )[0:1]
                grad_weights = times_transposed(qkv_ref[:, lanes[2]], dout)
                grad_scores = (weights * (grad_weights - centre)).astype(BF16)
                queries.append(contract_rows(key, grad_scores))
                keys[h] = keys[h] + dot(grad_scores, query)
                values[h] = values[h] + dot(weights.astype(BF16), dout)
            grad_ref[part, 0:inner] = (jnp.concatenate(queries, 0).T * scale).astype(BF16)
        for h in range(heads):
            grad_ref[:, inner + h * HEAD : inner + (h + 1) * HEAD] = (keys[h] * scale).astype(BF16)
            grad_ref[:, 2 * inner + h * HEAD : 2 * inner + (h + 1) * HEAD] = values[h].astype(BF16)
        sum_ref[...] = jnp.sum(grad_ref[...].astype(F32), axis=0, keepdims=True)
        start = 0
        for out_ref in refs[2:-1]:
            part = slice(start, start + out_ref.shape[0])
            start += out_ref.shape[0]
            total = times_transposed(before[0][part, :], before[1][:, : 3 * inner])
            total += times_transposed(grad_ref[part, :], w_ref[:, : 3 * inner])
            out_ref[...] = total.astype(out_ref.dtype)

    shapes = [
        jax.ShapeDtypeStruct((rows, 3 * inner), BF16),
        jax.ShapeDtypeStruct((1, 3 * inner), F32),
    ]
    if earlier is not None:
        shapes += sum_shapes(blocks)
    outs = pl.pallas_call(
        kernel,
        out_shape=shapes,
        scratch_shapes=[pltpu.VMEM((rows, inner), BF16)],
        compiler_params=pltpu.CompilerParams(vmem_limit_bytes=32 << 20),
        cost_estimate=SMALL_COST,
        name="attend_backward",
    )(*blocks, weight, qkv, mixture, log_total, segment[:, None], segment[None], *(earlier or ()))
    return outs[0], outs[1], list(outs[2:])


def normal_parts(x):
    bell = jnp.exp(-0.5 * x * x)
    t = 1.0 / (1.0 + 0.23164189 * jnp.abs(x))
    tail = 0.5307027145
    for c in (-0.7265760135, 0.7107068705, -0.142248368, 0.127414796):
        tail = tail * t + c
    tail = tail * t * bell
    return jnp.where(x >= 0.0, 1.0 - tail, tail), bell * 0.3989422804014327


def feed(blocks, weights, side, forward):
    rows = sum(block.shape[0] for block in blocks)
    hidden = weights[0].shape[1] // 2
    tile = min(512, hidden)
    tiles = hidden // tile
    into, onto = (0, hidden) if forward else (hidden, 0)

    def kernel(*refs):
        xs, refs = refs[: len(blocks)], refs[len(blocks) :]
        *halves, side_ref = refs[:3]
        outs, (kept_ref, more_ref, pre_ref) = refs[3:-3], refs[-3:]

        def project(half, index):
            start, slot = 0, lax.rem(index, 2)
            first = index * tile + into
            if not isinstance(index, int):
                first = pl.multiple_of(first, tile)
            for x in xs:
                part = pl.ds(start, x.shape[0])
                pre_ref[slot, part, :] = dot(x[...], halves[half][:, pl.ds(first, tile)])
                start += x.shape[0]

        def activate(half, index):
            first = index * tile + half * hidden
            if not isinstance(index, int):
                first = pl.multiple_of(first, tile)
            columns = pl.ds(first, tile)
            pre = pre_ref[lax.rem(index, 2)]
            if forward:
                pre = pre + side_ref[:, columns]
                cdf, bell = normal_parts(pre)
                kept_ref[:, columns] = (pre * cdf).astype(BF16)
                more_ref[:, columns] = (cdf + pre * bell).astype(BF16)
            else:
                kept = (pre * side_ref[:, columns].astype(F32)).astype(BF16)
                kept_ref[:, columns] = kept
                more_ref[:, columns] = jnp.sum(kept.astype(F32), axis=0, keepdims=True)

        for half in (0, 1):
            project(half, 0)

            def step(index, _, half=half):
                project(half, index)
                activate(half, index - 1)
                return 0

            lax.fori_loop(1, tiles, step, 0)
            activate(half, tiles - 1)
        start = 0
        for out in outs:
            part = slice(start, start + out.shape[0])
            start += out.shape[0]
            total = times_transposed(kept_ref[part, 0:hidden], halves[0][:, onto : onto + hidden])
            total += times_transposed(kept_ref[part, hidden:], halves[1][:, onto : onto + hidden])
            out[...] = total.astype(out.dtype)

    wide = jax.ShapeDtypeStruct((rows, 2 * hidden), BF16)
    outs = pl.pallas_call(
        kernel,
        out_shape=sum_shapes(blocks)
        + [wide, wide if forward else jax.ShapeDtypeStruct((1, 2 * hidden), F32)],
        scratch_shapes=[pltpu.VMEM((2, rows, tile), F32)],
        compiler_params=pltpu.CompilerParams(vmem_limit_bytes=32 << 20),
        cost_estimate=SMALL_COST,
        name="feed_forward" if forward else "feed_backward",
    )(*blocks, *weights, side)
    return list(outs[:-2]), outs[-2], outs[-1]


def weight_gradients(pairs, half):
    widths = [width for _, _, width in pairs]
    tile = math.gcd(256, *widths)
    if tile % 128:
        terms = [
            contract_rows(join(blocks), _columns(right, half, width))
            for blocks, right, width in pairs
        ]
        return jnp.concatenate(terms, 1).astype(BF16)
    counts = [width // tile for width in widths]
    edge = counts[0]
    blocks_flat = [block for blocks, _, _ in pairs for block in blocks]
    per = len(pairs[0][0])
    rows = sum(block.shape[0] for block in pairs[0][0])

    def kernel(*refs):
        lefts, refs = refs[: 2 * per], refs[2 * per :]
        rights, (out_ref, turned) = refs[:2], refs[2:]
        index = pl.program_id(0)

        @pl.when(index == 0)
        def _():
            for pair in (0, 1):
                start = 0
                for left in lefts[pair * per : (pair + 1) * per]:
                    turned[pair, :, start : start + left.shape[0]] = left[...].T
                    start += left.shape[0]

        def run(pair):
            out_ref[...] = dot(turned[pair], rights[pair][...]).astype(BF16)

        @pl.when(index < edge)
        def _():
            run(0)

        @pl.when(index >= edge)
        def _():
            run(1)

    shifts = [
        half * counts[i] if pairs[i][1].shape[1] > widths[i] else 0 for i in (0, 1)
    ]
    last = counts[1] - 1
    specs = [pl.BlockSpec(block.shape, lambda i: (0, 0)) for block in blocks_flat]
    specs += [
        pl.BlockSpec((rows, tile), lambda i: (0, jnp.minimum(i, edge - 1) + shifts[0])),
        pl.BlockSpec((rows, tile), lambda i: (0, jnp.clip(i - edge, 0, last) + shifts[1])),
    ]
    over = pl.BlockSpec((D, tile), lambda i: (0, i))
    return pl.pallas_call(
        kernel,
        grid=(sum(counts),),
        out_shape=jax.ShapeDtypeStruct((D, sum(widths)), BF16),
        in_specs=specs,
        out_specs=over,
        scratch_shapes=[pltpu.VMEM((2, D, rows), BF16)],
        compiler_params=pltpu.CompilerParams(vmem_limit_bytes=24 << 20),
        cost_estimate=SMALL_COST,
        name="weight_gradients",
    )(*blocks_flat, pairs[0][1], pairs[1][1])


def _columns(right, half, width):
    return right[:, half * width : (half + 1) * width] if right.shape[1] > width else right


def add_portions(spot, places, came, sums):
    count, given = len(places), min(len(came), len(places))
    shape = (sums[0].shape[0] // (spot.shape[0] - 1), sums[0].shape[1])

    def kernel(spot_ref, *refs):
        ins, parts, outs = refs[:given], refs[given:-count], refs[-count:]
        for i, out in enumerate(outs):
            total = sum(part[...].astype(F32) for part in parts[i * len(sums) : (i + 1) * len(sums)])
            if given:
                total += ins[i][...].astype(F32)
            out[...] = total.astype(BF16)

    whole = pl.BlockSpec(shape, lambda i, s: (0, 0))
    portions = [pl.BlockSpec(shape, lambda i, s, k=k: (s[k], 0)) for k in places for _ in sums]
    return pl.pallas_call(
        kernel,
        grid_spec=pltpu.PrefetchScalarGridSpec(
            num_scalar_prefetch=1,
            grid=(1,),
            in_specs=[whole] * given + portions,
            out_specs=[whole] * count,
        ),
        out_shape=[jax.ShapeDtypeStruct(shape, BF16)] * count,
        compiler_params=pltpu.CompilerParams(vmem_limit_bytes=24 << 20),
        cost_estimate=SMALL_COST,
        name="add_portions",
    )(spot, *came[:given], *(list(sums) * count))


def last_portion(spot, came, sums):
    chips = spot.shape[0] - 1
    shape = (sums[0].shape[0] // chips, sums[0].shape[1])
    rows = shape[0] // 2

    def kernel(spot_ref, *refs):
        ins, (mine, other, total) = refs[:-3], refs[-3:]
        total[...] = sum(part[...].astype(F32) for part in ins)
        first = pl.multiple_of(spot_ref[chips] * rows, rows)
        mine[...] = total[pl.ds(first, rows), :]
        other[...] = total[pl.ds(rows - first, rows), :].astype(BF16)

    whole = pl.BlockSpec(shape, lambda i, s: (0, 0))
    half = pl.BlockSpec((rows, shape[1]), lambda i, s: (0, 0))
    return pl.pallas_call(
        kernel,
        grid_spec=pltpu.PrefetchScalarGridSpec(
            num_scalar_prefetch=1,
            grid=(1,),
            in_specs=[whole] * len(came) + [pl.BlockSpec(shape, lambda i, s: (s[0], 0))] * len(sums),
            out_specs=[half] * 2,
            scratch_shapes=[pltpu.VMEM(shape, F32)],
        ),
        out_shape=[
            jax.ShapeDtypeStruct((rows, shape[1]), F32),
            jax.ShapeDtypeStruct((rows, shape[1]), BF16),
        ],
        compiler_params=pltpu.CompilerParams(vmem_limit_bytes=24 << 20),
        cost_estimate=SMALL_COST,
        name="last_portion",
    )(spot, *came, *sums)


def matrix_outputs(spot, layer, layer_total, attn_pair, feed_pair, filled):
    rows, inner, hidden = attn_pair[0].shape[0], attn_pair[0].shape[1] // 4, feed_pair[0].shape[1] // 2
    chips = spot.shape[0] - 1
    shapes = [
        (layer_total, 3, rows, 2 * inner),
        (layer_total, rows, 2 * inner),
        (layer_total, rows, 2 * hidden),
        (layer_total, rows, 2 * hidden),
    ]
    given = 0 if filled is None else 4

    def kernel(spot_ref, *refs):
        pairs, (qkv, out, first, second) = (refs[0:2], refs[2:4]), refs[4 + given :]
        for index in (0, 1):
            attn, feed = (pair[index][...].astype(F32) for pair in pairs)
            core = spot_ref[chips] if index == 0 else 1 - spot_ref[chips]
            heads = pl.ds(pl.multiple_of(core * inner, inner), inner)
            units = pl.ds(pl.multiple_of(core * hidden, hidden), hidden)
            for i in range(3):
                qkv[0, i, :, heads] = attn[:, i * inner : (i + 1) * inner]
            out[0, :, heads] = attn[:, 3 * inner :]
            first[0, :, units] = feed[:, :hidden]
            second[0, :, units] = feed[:, hidden:]

    def over(shape):
        return pl.BlockSpec((1,) + shape[1:], lambda i, s: (layer,) + (0,) * (len(shape) - 1))

    ins = (*attn_pair, *feed_pair)
    return pl.pallas_call(
        kernel,
        grid_spec=pltpu.PrefetchScalarGridSpec(
            num_scalar_prefetch=1,
            grid=(1,),
            in_specs=[pl.BlockSpec(part.shape, lambda i, s: (0, 0)) for part in ins]
            + [pl.BlockSpec(memory_space=pl.ANY)] * given,
            out_specs=[over(shape) for shape in shapes],
        ),
        out_shape=[jax.ShapeDtypeStruct(shape, F32) for shape in shapes],
        input_output_aliases={5 + i: i for i in range(given)},
        compiler_params=pltpu.CompilerParams(vmem_limit_bytes=24 << 20),
        cost_estimate=SMALL_COST,
        name="matrix_outputs",
    )(spot, *ins, *(filled or ()))


def join(blocks):
    return blocks[0] if len(blocks) == 1 else jnp.concatenate(blocks, 0)


def body(
    tokens,
    cotangent,
    deal_slot,
    back_slot,
    lengths,
    time_step,
    time_table,
    w_qkv,
    b_qv,
    w_out,
    out_bias,
    ln_gain,
    ln_shift,
    w_ff1,
    b_ff1,
    w_ff2,
):
    wires = Wires(lax.axis_size("dp"), lax.axis_size("tensor"))
    rows_dev = tokens.shape[0]
    group_rows = rows_dev * wires.tensor_size
    tensor_index = lax.axis_index("tensor")
    layer_total = w_qkv.shape[0]
    inner = w_qkv.shape[3] // 2
    hidden = w_ff1.shape[2] // 2
    both = (True, False)

    time_piece = lax.dynamic_index_in_dim(time_table, time_step[0], 0, keepdims=False)

    def rings(layer, arrays, extra):
        w_qkv, w_out, w_ff1, w_ff2 = arrays
        attn_shard, feed_shard = [], []
        for mine in both:
            qkv = wires.half(w_qkv[layer], 2, mine)
            out = wires.half(w_out[layer], 0, mine).T
            attn_shard.append(jnp.concatenate([qkv[0], qkv[1], qkv[2], out], axis=1))
            first = wires.half(w_ff1[layer], 1, mine)
            second = wires.half(w_ff2[layer], 0, mine).T
            feed_shard.append(jnp.concatenate([first, second], axis=1))
        return (
            Task(wires.gather_ring(wires.chip_piece(attn_shard), extra)),
            Task(wires.gather_ring(wires.chip_piece(feed_shard))),
        )

    arrays = (w_qkv, w_out, w_ff1, w_ff2)
    attn_rings, feed_rings = [None] * (layer_total + 1), [None] * (layer_total + 1)
    attn_rings[0], feed_rings[0] = rings(0, arrays, time_piece)
    for layer in range(1, layer_total):
        attn_rings[layer], feed_rings[layer] = rings(layer, arrays, None)
    later = attn_rings[1:-1] + feed_rings[1:-1]
    step = 0
    while not attn_rings[0].done:
        beside = (attn_rings[0], feed_rings[0] if step >= 3 else None)
        if step == 1:
            tokens, back_slot = tick((tokens, back_slot), *beside)
            own_tokens = owner_swap(pick(tokens, back_slot))
        elif step == 3:
            own_tokens = tick(own_tokens, *beside)
            token_blocks = wires.rows_in(own_tokens)
        elif step == 4:
            token_blocks[-1] = tick(token_blocks[-1], *beside)
            token_blocks[-1], *pieces = tie(token_blocks[-1], *(task.pending for task in later))
            for task, piece in zip(later, pieces):
                task.pending = piece
        else:
            tick((), *beside)
        step += 1
    attn_w, time_row = attn_rings[0].result
    time_row = time_row.astype(F32)

    seq_ends = jnp.cumsum(lengths[0])
    positions = jnp.arange(group_rows, dtype=jnp.int32)
    if wires.tensor_size == 2:
        positions = (positions + tensor_index * rows_dev) % group_rows
    segment = jnp.sum((positions[:, None] >= seq_ends[None, :]).astype(jnp.int32), axis=1)

    stream = own_tokens.astype(F32) + time_row
    weights, saved = [], []
    for layer in range(layer_total):
        if layer == 0:
            input_blocks = [(rows.astype(F32) + time_row).astype(BF16) for rows in token_blocks]
        else:
            input_blocks = wires.rows_in(stream.astype(BF16))
            input_blocks[-1] = tick(input_blocks[-1], attn_rings[layer], feed_rings[layer])
            attn_w = attn_rings[layer].finish()
        ahead = (attn_rings[layer + 1], feed_rings[layer + 1])
        biases = []
        for mine in both:
            bias_q, bias_v = [wires.half(b_qv[layer, i], 0, mine) for i in (0, 1)]
            biases.append(jnp.concatenate([bias_q, jnp.zeros_like(bias_q), bias_v]))
        (qkv, mixture, log_total), _ = attend_forward(input_blocks, attn_w[0], biases[0], segment)
        attention = [(qkv, mixture, log_total)]
        part, sums = attend_forward(
            input_blocks, attn_w[1], biases[1], segment, (mixture, attn_w[0])
        )
        attention.append(part)
        sums[-1] = tick(sums[-1], feed_rings[layer])
        attended = tick(wires.rows_out(sums), feed_rings[layer], ahead[0])
        middle = stream + attended + out_bias[layer, 0]
        normed = layer_norm(middle, ln_gain[layer, 0], ln_shift[layer, 0])
        normed_low = normed.astype(BF16)
        tick(normed_low, feed_rings[layer])
        normed_blocks = wires.rows_in(normed_low)
        normed_blocks[-1] = tick(normed_blocks[-1], *ahead)
        feed_w = feed_rings[layer].finish()
        weights.append((attn_w, feed_w))
        bias = jnp.concatenate([wires.half(b_ff1[layer], 0, mine) for mine in both])[None]
        sums, *filled = feed(normed_blocks, feed_w, bias, True)
        if layer == 0:
            sums[-1], cotangent = tie(sums[-1], cotangent)
            upstream = owner_swap(pick(cotangent, back_slot))
        sums[-1] = tick(sums[-1], ahead[0])
        arrived = tick(wires.rows_out(sums), *ahead)
        second_sum = normed + arrived + out_bias[layer, 1]
        saved.append((input_blocks, attention, middle, normed_blocks, filled, second_sum))
        stream = layer_norm(second_sum, ln_gain[layer, 1], ln_shift[layer, 1])

    encoded_own = stream.astype(BF16)
    gradient = upstream.astype(F32)
    feed_tasks, attn_tasks = [None] * (layer_total + 1), [None] * (layer_total + 1)
    attn_sums, reduced, matrices = None, [None] * layer_total, None
    direct = inner % 128 == 0 and hidden % 128 == 0
    vector_grads = [None] * layer_total
    for layer in reversed(range(layer_total)):
        attn_w, feed_w = weights[layer]
        input_blocks, attention, middle, normed_blocks, (act, slope), second_sum = saved[layer]
        _, pull_second = jax.vjp(layer_norm, second_sum, ln_gain[layer, 1], ln_shift[layer, 1])
        grad_second, gain_second, shift_second = pull_second(gradient)
        later_feed, later_attn = feed_tasks[layer + 1], None
        send = tick(grad_second.astype(BF16), later_feed)
        if layer == layer_total - 1:
            send, encoded_own = tie(send, encoded_own)
            returned_out = owner_swap(encoded_own)
        if attn_sums is not None:
            send, *attn_sums = tie(send, *attn_sums)
            later_attn = attn_tasks[layer + 1] = Task(wires.reduce_ring(attn_sums))
        branch_blocks = wires.rows_in(send)
        branch_blocks[-1] = tick(branch_blocks[-1], later_feed, later_attn)
        sums, grad_pre, hidden_sums = feed(branch_blocks, feed_w, slope, False)
        hidden_sums = hidden_sums[0]
        pairs = [(normed_blocks, grad_pre, hidden), (branch_blocks, act, hidden)]
        came = wires.partner(weight_gradients(pairs, 1))
        grad_normed = grad_second + wires.rows_out(sums)
        _, pull_first = jax.vjp(layer_norm, middle, ln_gain[layer, 0], ln_shift[layer, 0])
        grad_middle, gain_first, shift_first = pull_first(grad_normed)
        send, *feed_sums = tie(grad_middle.astype(BF16), weight_gradients(pairs, 0), came)
        feed_tasks[layer] = Task(wires.reduce_ring(feed_sums))
        attend_blocks = wires.rows_in(send)
        attend_blocks[-1] = tick(attend_blocks[-1], feed_tasks[layer], later_attn)

        def attn_pairs(half, wide):
            return [(input_blocks, wide, 3 * inner), (attend_blocks, attention[half][1], inner)]

        wide, part_sums, _ = attend_backward(attend_blocks, attn_w[1], *attention[1], segment)
        send = weight_gradients(attn_pairs(1, wide), 1)
        came = wires.partner(send)
        own_wide, own_sums, sums = attend_backward(
            attend_blocks, attn_w[0], *attention[0], segment, (wide, attn_w[1])
        )
        sums[-1] = tick(sums[-1], feed_tasks[layer], later_attn)
        attn_sums = [weight_gradients(attn_pairs(0, own_wide), 0), came]
        if layer == 0:
            first_portions = wires.first_portions(attn_sums)
        arrived = wires.rows_out(sums)
        if layer + 1 < layer_total:
            reduced[layer + 1] = (later_attn.finish(), later_feed.finish())
            if direct:
                matrices = matrix_outputs(
                    wires.spot, layer + 1, layer_total, *reduced[layer + 1], matrices
                )
                arrived, matrices = tie(arrived, matrices)
        if layer == 0:
            arrived, encoded = tie(arrived, pick(returned_out, deal_slot))
            attn_tasks[0] = Task(wires.reduce_ring(attn_sums, first_portions))
        gradient = grad_middle + arrived
        qkv_sums = [part.reshape(3, inner)[::2] for part in (own_sums, part_sums)]
        vector_grads[layer] = (
            wires.ordered(qkv_sums[0], qkv_sums[1], 1),
            wires.ordered(hidden_sums[:hidden], hidden_sums[hidden:], 0),
            jnp.stack([jnp.sum(grad_middle, axis=0), jnp.sum(grad_second, axis=0)]),
            jnp.stack([gain_first, gain_second]),
            jnp.stack([shift_first, shift_second]),
        )

    returned_grad = owner_swap(gradient.astype(BF16))
    time_grad = jnp.sum(gradient, axis=0)
    local = [jnp.stack([part[i] for part in vector_grads]) for i in range(5)]
    flat = jnp.concatenate([part.reshape(-1) for part in local[:2] + [time_grad] + local[2:]])
    border = local[0].size + local[1].size
    vector_task = Task(wires.butterfly(flat, border))
    vector_task.finish()
    reduced[0] = (attn_tasks[0].finish(), feed_tasks[0].finish())
    flat, shared = vector_task.result
    grad_tokens = pick(returned_grad, deal_slot)
    if direct:
        matrices = matrix_outputs(wires.spot, 0, layer_total, *reduced[0], matrices)
        matrices = [part.transpose(0, 2, 1) if i % 2 else part for i, part in enumerate(matrices)]
    else:
        parts = []
        for attn_pair, feed_pair in reduced:
            rows = attn_pair[0].shape[0]
            qkv = [
                part[:, : 3 * inner].reshape(rows, 3, inner).transpose(1, 0, 2).astype(F32)
                for part in attn_pair
            ]
            parts.append(
                (
                    wires.ordered(*qkv, 2),
                    wires.ordered(*(part[:, 3 * inner :].T.astype(F32) for part in attn_pair), 0),
                    wires.ordered(*(part[:, :hidden].astype(F32) for part in feed_pair), 1),
                    wires.ordered(*(part[:, hidden:].T.astype(F32) for part in feed_pair), 0),
                )
            )
        matrices = [jnp.stack([part[i] for part in parts]) for i in range(4)]
    grad_b_qv = flat[: local[0].size].reshape(local[0].shape)
    grad_b_ff1 = flat[local[0].size : border].reshape(local[1].shape)
    time_grad = shared[:D]
    rest = shared[D:].reshape(3, layer_total, 2, D)
    return (
        encoded,
        grad_tokens,
        time_grad,
        matrices[0],
        grad_b_qv,
        matrices[1],
        rest[0],
        rest[1],
        rest[2],
        matrices[2],
        grad_b_ff1,
        matrices[3],
    )


def solution(mesh):
    return jax.shard_map(
        body,
        mesh=mesh,
        in_specs=(
            P(("dp", "tensor"), None),
            P(("dp", "tensor"), None),
            P(("dp", "tensor")),
            P(("dp", "tensor")),
            P("dp", None),
            P(),
            P(None, "dp"),
            P(None, None, "dp", "tensor"),
            P(None, None, "tensor"),
            P(None, "tensor", "dp"),
            P(),
            P(),
            P(),
            P(None, "dp", "tensor"),
            P(None, "tensor"),
            P(None, "tensor", "dp"),
        ),
        out_specs=(
            P(("dp", "tensor"), None),
            P(("dp", "tensor"), None),
            P(),
            P(None, None, "dp", "tensor"),
            P(None, None, "tensor"),
            P(None, "tensor", "dp"),
            P(),
            P(),
            P(),
            P(None, "dp", "tensor"),
            P(None, "tensor"),
            P(None, "tensor", "dp"),
        ),
        check_vma=False,
    )
```

```python
import math

import jax
import jax.numpy as jnp
import numpy as np
from jax import lax
from jax.experimental import pallas as pl
from jax.experimental.pallas import tpu as pltpu
from jax.sharding import PartitionSpec as P

D = 1024
HEADS = 16
FF = 4096
HEAD = D // HEADS
F32 = jnp.float32
BF16 = jnp.bfloat16
SMALL_COST = pl.CostEstimate(flops=1000, bytes_accessed=1000, transcendentals=0)


def layer_norm(summed, scaling, offset_vec):
    centre = jnp.mean(summed, axis=-1, keepdims=True)
    spread = summed - centre
    variance = jnp.mean(spread * spread, axis=-1, keepdims=True)
    return spread * lax.rsqrt(variance + 1e-05) * scaling + offset_vec


def dot(left, right):
    return jnp.dot(left, right, preferred_element_type=F32)


def contract_rows(left, right):
    return lax.dot_general(left, right, (((0,), (0,)), ((), ())), preferred_element_type=F32)


def times_transposed(left, right):
    return lax.dot_general(left, right, (((1,), (1,)), ((), ())), preferred_element_type=F32)


class Wires:
    def __init__(self, dp_size, tensor_size):
        self.dp_size, self.tensor_size = dp_size, tensor_size
        chips = dp_size // 2
        self.chips = chips
        order = list(range(0, chips, 2)) + list(range(chips - 1, 0, -2))
        place = {chip: spot for spot, chip in enumerate(order)}
        self.rounds = chips // 2
        ahead, spots = [], np.zeros((dp_size, chips + 1), np.int32)
        for device in range(dp_size):
            chip, core = divmod(device, 2)
            way = 1 if core == 0 else -1
            ahead.append((device, 2 * order[(place[chip] + way) % chips] + core))
            spots[device, :chips] = [order[(place[chip] + way * s) % chips] for s in range(chips)]
            spots[device, chips] = core
        self.ahead = ahead
        self.back = [(there, here) for here, there in ahead]
        self.swap = [(d, d ^ 1) for d in range(dp_size)]
        dp_index = lax.axis_index("dp")
        self.core = dp_index % 2
        self.spot = lax.dynamic_index_in_dim(jnp.asarray(spots), dp_index, 0, keepdims=False)

    def round(self, forth, back):
        if back is None:
            return [lax.ppermute(forth, "dp", self.ahead)]
        return [lax.ppermute(forth, "dp", self.ahead), lax.ppermute(back, "dp", self.back)]

    def partner(self, array):
        return lax.ppermute(array, "dp", self.swap)

    def across(self, array):
        return lax.ppermute(array, "tensor", [(0, 1), (1, 0)])

    def half(self, array, axis, mine):
        width = array.shape[axis] // 2
        index = self.core if mine else 1 - self.core
        return lax.dynamic_slice_in_dim(array, index * width, width, axis)

    def ordered(self, mine, other, axis):
        return jnp.where(
            self.core == 0,
            jnp.concatenate([mine, other], axis),
            jnp.concatenate([other, mine], axis),
        )

    def chip_piece(self, shard):
        mine, other = shard
        return self.ordered(mine, self.partner(other), 0)

    def gather_ring(self, piece, extra=None):
        chip_rows = piece.shape[0]
        if extra is not None:
            tail = jnp.zeros((8, piece.shape[1]), piece.dtype)
            pair = self.ordered(extra, self.partner(extra), 0)
            tail = lax.dynamic_update_slice(tail, pair[None, :], (0, 0))
            piece = jnp.concatenate([piece, tail], 0)
        piece = yield piece
        forth, back = [piece], [piece]
        for step in range(1, self.rounds + 1):
            both_ways = step < self.chips - self.rounds
            came = yield self.round(forth[-1], back[-1] if both_ways else None)
            forth.append(came[0])
            back += came[1:]
            if step == self.rounds - 1:
                places = [0] + [-s % self.chips for s in range(1, len(forth))] + list(range(1, len(back)))
                outs = place_pieces(self.spot, places, forth + back[1:], chip_rows, None)
        outs = place_pieces(self.spot, [-self.rounds % self.chips], forth[-1:], chip_rows, outs)
        whole, vector = outs[0], outs[-1]
        halves = (whole, self.partner(whole))
        return halves if extra is None else (halves, vector[:, 0, :chip_rows].reshape(-1))

    def first_portions(self, sums):
        return add_portions(self.spot, [self.rounds, 1 + self.rounds], [], sums)

    def reduce_ring(self, sums, first=None):
        forth, back = first or self.first_portions(sums)
        for step in range(1, self.rounds + 1):
            both_ways = step < self.chips - self.rounds
            came = yield self.round(forth, back if both_ways else None)
            places = [self.rounds - step] if step < self.rounds else []
            if step + 1 < self.chips - self.rounds:
                places.append(1 + self.rounds + step)
            added = add_portions(self.spot, places, came, sums) if places else []
            forth = added[0] if step < self.rounds else came[0]
            if both_ways:
                back = added[1] if len(places) == 2 else came[1]
        mine, other = last_portion(self.spot, [forth, back], sums)
        return mine, self.partner(other)

    def rows_in(self, local_rows):
        if self.tensor_size == 2:
            return [local_rows, self.across(local_rows)]
        return [lax.all_gather(local_rows, "tensor", axis=0, tiled=True)]

    def rows_out(self, sums):
        if self.tensor_size == 2:
            return sums[0] + self.across(sums[1]).astype(F32)
        return lax.psum_scatter(sums[0], "tensor", scatter_dimension=0, tiled=True).astype(F32)

    def butterfly(self, array, border):
        for axis, size in (("dp", self.dp_size), ("tensor", self.tensor_size)):
            if axis == "tensor":
                array, kept = array[border:], array
            bit = 1
            while bit < size:
                pairs = [(i, i ^ bit) for i in range(size)]
                array = array + (yield lax.ppermute(array, axis, pairs))
                bit *= 2
        return kept, array


def pick(rows, index):
    return rows.at[index].get(mode="promise_in_bounds")


def owner_swap(rows):
    return lax.all_to_all(rows, "dp", split_axis=0, concat_axis=0, tiled=True)


class Task:
    def __init__(self, steps):
        self.steps, self.done, self.result = steps, False, None
        self.advance(None, first=True)

    def advance(self, arrived, first=False):
        try:
            self.pending = next(self.steps) if first else self.steps.send(arrived)
        except StopIteration as stop:
            self.done, self.result = True, stop.value

    def finish(self):
        while not self.done:
            self.advance(self.pending)
        return self.result


def tick(value, *tasks):
    tasks = [task for task in tasks if task is not None and not task.done]
    if not tasks:
        return value
    value, arrived = lax.optimization_barrier((value, [task.pending for task in tasks]))
    for task, part in zip(tasks, arrived):
        task.advance(part)
    return value


def tie(*values):
    return lax.optimization_barrier(values)


def place_pieces(spot, places, pieces, chip_rows, filled):
    count, width = len(pieces), pieces[0].shape[1]
    chips = spot.shape[0] - 1
    spare = pieces[0].shape[0] - chip_rows
    given = 0 if filled is None else len(filled)

    def kernel(spot_ref, *refs):
        ins, outs, sems = refs[:count], refs[count + given : -1], refs[-1]
        copies = []
        for i, piece in enumerate(ins):
            chip = spot_ref[places[i]]
            rows = pl.ds(pl.multiple_of(chip * chip_rows, chip_rows), chip_rows)
            copies.append(
                pltpu.make_async_copy(piece.at[0:chip_rows], outs[0].at[rows], sems.at[i, 0])
            )
            if spare:
                copies.append(
                    pltpu.make_async_copy(
                        piece.at[chip_rows : chip_rows + spare, 0:128],
                        outs[1].at[chip],
                        sems.at[i, 1],
                    )
                )
        for copy in copies:
            copy.start()
        for copy in copies:
            copy.wait()

    shapes = [jax.ShapeDtypeStruct((chips * chip_rows, width), BF16)]
    if spare:
        shapes.append(jax.ShapeDtypeStruct((chips, spare, 128), BF16))
    return pl.pallas_call(
        kernel,
        out_shape=shapes,
        in_specs=[pl.BlockSpec(memory_space=pltpu.SMEM)]
        + [pl.BlockSpec(memory_space=pl.ANY)] * (count + given),
        out_specs=[pl.BlockSpec(memory_space=pl.ANY)] * len(shapes),
        scratch_shapes=[pltpu.SemaphoreType.DMA((count, 2))],
        input_output_aliases={1 + count + i: i for i in range(given)},
        compiler_params=pltpu.CompilerParams(vmem_limit_bytes=8 << 20),
        cost_estimate=pl.CostEstimate(
            flops=0, bytes_accessed=1 << 26, transcendentals=0
        ),
        name="place_pieces",
    )(spot, *pieces, *(filled or ()))


def attend_forward(blocks, weight, bias, segment, earlier=None):
    rows = sum(block.shape[0] for block in blocks)
    inner = weight.shape[1] // 4
    heads = inner // HEAD
    step = min(512, rows)
    scale = 1.0 / math.sqrt(HEAD)
    extra = 0 if earlier is None else 2

    def kernel(*refs):
        xs, refs = refs[: len(blocks)], refs[len(blocks) :]
        w_ref, bias_ref, col_ref, row_ref = refs[:4]
        before, refs = refs[4 : 4 + extra], refs[4 + extra :]
        qkv_ref, out_ref, log_ref = refs[:3]
        start = 0
        for x in xs:
            size = x.shape[0]
            projected = dot(x[...], w_ref[:, : 3 * inner]) + bias_ref[...]
            qkv_ref[start : start + size, :] = projected.astype(BF16)
            start += size
        for first in range(0, rows, step):
            part = slice(first, first + step)
            far = jnp.where(col_ref[...] == row_ref[:, part], 0.0, -1e30)
            mixed = []
            for h in range(heads):
                lanes = [slice(i * inner + h * HEAD, i * inner + (h + 1) * HEAD) for i in range(3)]
                scores = times_transposed(qkv_ref[:, lanes[1]], qkv_ref[part, lanes[0]])
                scores = scores * scale + far
                highest = jnp.max(scores, axis=0, keepdims=True)
                powers = jnp.exp(scores - highest)
                summed = jnp.sum(powers, axis=0, keepdims=True)
                mixture = contract_rows(qkv_ref[:, lanes[2]], powers.astype(BF16))
                mixed.append(mixture * (1.0 / summed))
                log_ref[h : h + 1, part] = highest + jnp.log(summed)
            out_ref[part, :] = jnp.concatenate(mixed, 0).T.astype(BF16)
        start = 0
        for sum_ref in refs[3:]:
            part = slice(start, start + sum_ref.shape[0])
            start += sum_ref.shape[0]
            total = times_transposed(before[0][part, :], before[1][:, 3 * inner :])
            total += times_transposed(out_ref[part, :], w_ref[:, 3 * inner :])
            sum_ref[...] = total.astype(sum_ref.dtype)

    shapes = [
        jax.ShapeDtypeStruct((rows, 3 * inner), BF16),
        jax.ShapeDtypeStruct((rows, inner), BF16),
        jax.ShapeDtypeStruct((heads, rows), F32),
    ]
    if earlier is not None:
        shapes += sum_shapes(blocks)
    outs = pl.pallas_call(
        kernel,
        out_shape=shapes,
        compiler_params=pltpu.CompilerParams(vmem_limit_bytes=20 << 20),
        cost_estimate=SMALL_COST,
        name="attend_forward",
    )(*blocks, weight, bias[None], segment[:, None], segment[None], *(earlier or ()))
    return tuple(outs[:3]), list(outs[3:])


def sum_shapes(blocks):
    kinds = (F32, BF16) if len(blocks) == 2 else (BF16,)
    return [jax.ShapeDtypeStruct(block.shape, kind) for block, kind in zip(blocks, kinds)]


def attend_backward(blocks, weight, qkv, mixture, log_total, segment, earlier=None):
    rows = sum(block.shape[0] for block in blocks)
    inner = weight.shape[1] // 4
    extra = 0 if earlier is None else 2
    heads = inner // HEAD
    step = min(512, rows)
    scale = 1.0 / math.sqrt(HEAD)

    def kernel(*refs):
        xs = refs[: len(blocks)]
        (w_ref, qkv_ref, mix_ref, log_ref, col_ref, row_ref) = refs[len(blocks) : len(blocks) + 6]
        refs = refs[len(blocks) + 6 :]
        before, refs = refs[:extra], refs[extra:]
        grad_ref, sum_ref, dout_ref = refs[0], refs[1], refs[-1]
        start = 0
        for x in xs:
            size = x.shape[0]
            dout_ref[start : start + size, :] = dot(x[...], w_ref[:, 3 * inner :]).astype(BF16)
            start += size
        ones = jnp.ones((8, HEAD), F32)
        keys = [jnp.zeros((rows, HEAD), F32)] * heads
        values = [jnp.zeros((rows, HEAD), F32)] * heads
        for first in range(0, rows, step):
            part = slice(first, first + step)
            far = jnp.where(col_ref[...] == row_ref[:, part], 0.0, -1e30)
            queries = []
            for h in range(heads):
                lanes = [slice(i * inner + h * HEAD, i * inner + (h + 1) * HEAD) for i in range(3)]
                query, key = qkv_ref[part, lanes[0]], qkv_ref[:, lanes[1]]
                dout = dout_ref[part, lanes[0]]
                scores = times_transposed(key, query) * scale + far
                weights = jnp.exp(scores - log_ref[h : h + 1, part])
                product = dout.astype(F32) * mix_ref[part, lanes[0]].astype(F32)
                centre = lax.dot_general(
                    ones,
                    product,
                    (((1,), (1,)), ((), ())),
                    precision=lax.Precision.HIGHEST,
                    preferred_element_type=F32,
                )[0:1]
                grad_weights = times_transposed(qkv_ref[:, lanes[2]], dout)
                grad_scores = (weights * (grad_weights - centre)).astype(BF16)
                queries.append(contract_rows(key, grad_scores))
                keys[h] = keys[h] + dot(grad_scores, query)
                values[h] = values[h] + dot(weights.astype(BF16), dout)
            grad_ref[part, 0:inner] = (jnp.concatenate(queries, 0).T * scale).astype(BF16)
        for h in range(heads):
            grad_ref[:, inner + h * HEAD : inner + (h + 1) * HEAD] = (keys[h] * scale).astype(BF16)
            grad_ref[:, 2 * inner + h * HEAD : 2 * inner + (h + 1) * HEAD] = values[h].astype(BF16)
        sum_ref[...] = jnp.sum(grad_ref[...].astype(F32), axis=0, keepdims=True)
        start = 0
        for out_ref in refs[2:-1]:
            part = slice(start, start + out_ref.shape[0])
            start += out_ref.shape[0]
            total = times_transposed(before[0][part, :], before[1][:, : 3 * inner])
            total += times_transposed(grad_ref[part, :], w_ref[:, : 3 * inner])
            out_ref[...] = total.astype(out_ref.dtype)

    shapes = [
        jax.ShapeDtypeStruct((rows, 3 * inner), BF16),
        jax.ShapeDtypeStruct((1, 3 * inner), F32),
    ]
    if earlier is not None:
        shapes += sum_shapes(blocks)
    outs = pl.pallas_call(
        kernel,
        out_shape=shapes,
        scratch_shapes=[pltpu.VMEM((rows, inner), BF16)],
        compiler_params=pltpu.CompilerParams(vmem_limit_bytes=24 << 20),
        cost_estimate=SMALL_COST,
        name="attend_backward",
    )(*blocks, weight, qkv, mixture, log_total, segment[:, None], segment[None], *(earlier or ()))
    return outs[0], outs[1], list(outs[2:])


def normal_parts(x):
    bell = jnp.exp(-0.5 * x * x)
    t = 1.0 / (1.0 + 0.23164189 * jnp.abs(x))
    tail = 0.5307027145
    for c in (-0.7265760135, 0.7107068705, -0.142248368, 0.127414796):
        tail = tail * t + c
    tail = tail * t * bell
    return jnp.where(x >= 0.0, 1.0 - tail, tail), bell * 0.3989422804014327


def feed(blocks, weights, side, forward):
    rows = sum(block.shape[0] for block in blocks)
    hidden = weights[0].shape[1] // 2
    tile = min(512, hidden)
    tiles = hidden // tile
    into, onto = (0, hidden) if forward else (hidden, 0)

    def kernel(*refs):
        xs, refs = refs[: len(blocks)], refs[len(blocks) :]
        *halves, side_ref = refs[:3]
        outs, (kept_ref, more_ref, pre_ref) = refs[3:-3], refs[-3:]

        def project(half, index):
            start, slot = 0, lax.rem(index, 2)
            first = index * tile + into
            if not isinstance(index, int):
                first = pl.multiple_of(first, tile)
            for x in xs:
                part = pl.ds(start, x.shape[0])
                pre_ref[slot, part, :] = dot(x[...], halves[half][:, pl.ds(first, tile)])
                start += x.shape[0]

        def activate(half, index):
            first = index * tile + half * hidden
            if not isinstance(index, int):
                first = pl.multiple_of(first, tile)
            columns = pl.ds(first, tile)
            pre = pre_ref[lax.rem(index, 2)]
            if forward:
                pre = pre + side_ref[:, columns]
                cdf, bell = normal_parts(pre)
                kept_ref[:, columns] = (pre * cdf).astype(BF16)
                more_ref[:, columns] = (cdf + pre * bell).astype(BF16)
            else:
                kept = (pre * side_ref[:, columns].astype(F32)).astype(BF16)
                kept_ref[:, columns] = kept
                more_ref[:, columns] = jnp.sum(kept.astype(F32), axis=0, keepdims=True)

        for half in (0, 1):
            project(half, 0)

            def step(index, _, half=half):
                project(half, index)
                activate(half, index - 1)
                return 0

            lax.fori_loop(1, tiles, step, 0)
            activate(half, tiles - 1)
        start = 0
        for out in outs:
            part = slice(start, start + out.shape[0])
            start += out.shape[0]
            total = times_transposed(kept_ref[part, 0:hidden], halves[0][:, onto : onto + hidden])
            total += times_transposed(kept_ref[part, hidden:], halves[1][:, onto : onto + hidden])
            out[...] = total.astype(out.dtype)

    wide = jax.ShapeDtypeStruct((rows, 2 * hidden), BF16)
    outs = pl.pallas_call(
        kernel,
        out_shape=sum_shapes(blocks)
        + [wide, wide if forward else jax.ShapeDtypeStruct((1, 2 * hidden), F32)],
        scratch_shapes=[pltpu.VMEM((2, rows, tile), F32)],
        compiler_params=pltpu.CompilerParams(vmem_limit_bytes=24 << 20),
        cost_estimate=SMALL_COST,
        name="feed_forward" if forward else "feed_backward",
    )(*blocks, *weights, side)
    return list(outs[:-2]), outs[-2], outs[-1]


def weight_gradients(pairs, half):
    widths = [width for _, _, width in pairs]
    tile = math.gcd(256, *widths)
    if tile % 128:
        terms = [
            contract_rows(join(blocks), _columns(right, half, width))
            for blocks, right, width in pairs
        ]
        return jnp.concatenate(terms, 1).astype(BF16)
    counts = [width // tile for width in widths]
    edge = counts[0]
    blocks_flat = [block for blocks, _, _ in pairs for block in blocks]
    per = len(pairs[0][0])
    rows = sum(block.shape[0] for block in pairs[0][0])

    def kernel(*refs):
        lefts, refs = refs[: 2 * per], refs[2 * per :]
        rights, (out_ref, turned) = refs[:2], refs[2:]
        index = pl.program_id(0)

        @pl.when(index == 0)
        def _():
            for pair in (0, 1):
                start = 0
                for left in lefts[pair * per : (pair + 1) * per]:
                    turned[pair, :, start : start + left.shape[0]] = left[...].T
                    start += left.shape[0]

        def run(pair):
            out_ref[...] = dot(turned[pair], rights[pair][...]).astype(BF16)

        @pl.when(index < edge)
        def _():
            run(0)

        @pl.when(index >= edge)
        def _():
            run(1)

    shifts = [
        half * counts[i] if pairs[i][1].shape[1] > widths[i] else 0 for i in (0, 1)
    ]
    last = counts[1] - 1
    specs = [pl.BlockSpec(block.shape, lambda i: (0, 0)) for block in blocks_flat]
    specs += [
        pl.BlockSpec((rows, tile), lambda i: (0, jnp.minimum(i, edge - 1) + shifts[0])),
        pl.BlockSpec((rows, tile), lambda i: (0, jnp.clip(i - edge, 0, last) + shifts[1])),
    ]
    over = pl.BlockSpec((D, tile), lambda i: (0, i))
    return pl.pallas_call(
        kernel,
        grid=(sum(counts),),
        out_shape=jax.ShapeDtypeStruct((D, sum(widths)), BF16),
        in_specs=specs,
        out_specs=over,
        scratch_shapes=[pltpu.VMEM((2, D, rows), BF16)],
        compiler_params=pltpu.CompilerParams(vmem_limit_bytes=16 << 20),
        cost_estimate=SMALL_COST,
        name="weight_gradients",
    )(*blocks_flat, pairs[0][1], pairs[1][1])


def _columns(right, half, width):
    return right[:, half * width : (half + 1) * width] if right.shape[1] > width else right


def add_portions(spot, places, came, sums):
    count, given = len(places), min(len(came), len(places))
    shape = (sums[0].shape[0] // (spot.shape[0] - 1), sums[0].shape[1])

    def kernel(spot_ref, *refs):
        ins, parts, outs = refs[:given], refs[given:-count], refs[-count:]
        for i, out in enumerate(outs):
            total = sum(part[...].astype(F32) for part in parts[i * len(sums) : (i + 1) * len(sums)])
            if given:
                total += ins[i][...].astype(F32)
            out[...] = total.astype(BF16)

    whole = pl.BlockSpec(shape, lambda i, s: (0, 0))
    portions = [pl.BlockSpec(shape, lambda i, s, k=k: (s[k], 0)) for k in places for _ in sums]
    return pl.pallas_call(
        kernel,
        grid_spec=pltpu.PrefetchScalarGridSpec(
            num_scalar_prefetch=1,
            grid=(1,),
            in_specs=[whole] * given + portions,
            out_specs=[whole] * count,
        ),
        out_shape=[jax.ShapeDtypeStruct(shape, BF16)] * count,
        compiler_params=pltpu.CompilerParams(vmem_limit_bytes=8 << 20),
        cost_estimate=SMALL_COST,
        name="add_portions",
    )(spot, *came[:given], *(list(sums) * count))


def last_portion(spot, came, sums):
    chips = spot.shape[0] - 1
    shape = (sums[0].shape[0] // chips, sums[0].shape[1])
    rows = shape[0] // 2

    def kernel(spot_ref, *refs):
        ins, (mine, other, total) = refs[:-3], refs[-3:]
        total[...] = sum(part[...].astype(F32) for part in ins)
        first = pl.multiple_of(spot_ref[chips] * rows, rows)
        mine[...] = total[pl.ds(first, rows), :]
        other[...] = total[pl.ds(rows - first, rows), :].astype(BF16)

    whole = pl.BlockSpec(shape, lambda i, s: (0, 0))
    half = pl.BlockSpec((rows, shape[1]), lambda i, s: (0, 0))
    return pl.pallas_call(
        kernel,
        grid_spec=pltpu.PrefetchScalarGridSpec(
            num_scalar_prefetch=1,
            grid=(1,),
            in_specs=[whole] * len(came) + [pl.BlockSpec(shape, lambda i, s: (s[0], 0))] * len(sums),
            out_specs=[half] * 2,
            scratch_shapes=[pltpu.VMEM(shape, F32)],
        ),
        out_shape=[
            jax.ShapeDtypeStruct((rows, shape[1]), F32),
            jax.ShapeDtypeStruct((rows, shape[1]), BF16),
        ],
        compiler_params=pltpu.CompilerParams(vmem_limit_bytes=8 << 20),
        cost_estimate=SMALL_COST,
        name="last_portion",
    )(spot, *came, *sums)


def matrix_outputs(spot, layer, layer_total, attn_pair, feed_pair, filled):
    rows, inner, hidden = attn_pair[0].shape[0], attn_pair[0].shape[1] // 4, feed_pair[0].shape[1] // 2
    chips = spot.shape[0] - 1
    shapes = [
        (layer_total, 3, rows, 2 * inner),
        (layer_total, rows, 2 * inner),
        (layer_total, rows, 2 * hidden),
        (layer_total, rows, 2 * hidden),
    ]
    given = 0 if filled is None else 4

    def kernel(spot_ref, *refs):
        pairs, (qkv, out, first, second) = (refs[0:2], refs[2:4]), refs[4 + given :]
        for index in (0, 1):
            attn, feed = (pair[index][...].astype(F32) for pair in pairs)
            core = spot_ref[chips] if index == 0 else 1 - spot_ref[chips]
            heads = pl.ds(pl.multiple_of(core * inner, inner), inner)
            units = pl.ds(pl.multiple_of(core * hidden, hidden), hidden)
            for i in range(3):
                qkv[0, i, :, heads] = attn[:, i * inner : (i + 1) * inner]
            out[0, :, heads] = attn[:, 3 * inner :]
            first[0, :, units] = feed[:, :hidden]
            second[0, :, units] = feed[:, hidden:]

    def over(shape):
        return pl.BlockSpec((1,) + shape[1:], lambda i, s: (layer,) + (0,) * (len(shape) - 1))

    ins = (*attn_pair, *feed_pair)
    return pl.pallas_call(
        kernel,
        grid_spec=pltpu.PrefetchScalarGridSpec(
            num_scalar_prefetch=1,
            grid=(1,),
            in_specs=[pl.BlockSpec(part.shape, lambda i, s: (0, 0)) for part in ins]
            + [pl.BlockSpec(memory_space=pl.ANY)] * given,
            out_specs=[over(shape) for shape in shapes],
        ),
        out_shape=[jax.ShapeDtypeStruct(shape, F32) for shape in shapes],
        input_output_aliases={5 + i: i for i in range(given)},
        compiler_params=pltpu.CompilerParams(vmem_limit_bytes=12 << 20),
        cost_estimate=SMALL_COST,
        name="matrix_outputs",
    )(spot, *ins, *(filled or ()))


def join(blocks):
    return blocks[0] if len(blocks) == 1 else jnp.concatenate(blocks, 0)


def body(
    tokens,
    cotangent,
    deal_slot,
    back_slot,
    lengths,
    time_step,
    time_table,
    w_qkv,
    b_qv,
    w_out,
    out_bias,
    ln_gain,
    ln_shift,
    w_ff1,
    b_ff1,
    w_ff2,
):
    wires = Wires(lax.axis_size("dp"), lax.axis_size("tensor"))
    rows_dev = tokens.shape[0]
    group_rows = rows_dev * wires.tensor_size
    tensor_index = lax.axis_index("tensor")
    layer_total = w_qkv.shape[0]
    inner = w_qkv.shape[3] // 2
    hidden = w_ff1.shape[2] // 2
    both = (True, False)

    time_piece = lax.dynamic_index_in_dim(time_table, time_step[0], 0, keepdims=False)

    def rings(layer, arrays, extra):
        w_qkv, w_out, w_ff1, w_ff2 = arrays
        attn_shard, feed_shard = [], []
        for mine in both:
            qkv = wires.half(w_qkv[layer], 2, mine)
            out = wires.half(w_out[layer], 0, mine).T
            attn_shard.append(jnp.concatenate([qkv[0], qkv[1], qkv[2], out], axis=1))
            first = wires.half(w_ff1[layer], 1, mine)
            second = wires.half(w_ff2[layer], 0, mine).T
            feed_shard.append(jnp.concatenate([first, second], axis=1))
        return (
            Task(wires.gather_ring(wires.chip_piece(attn_shard), extra)),
            Task(wires.gather_ring(wires.chip_piece(feed_shard))),
        )

    arrays = (w_qkv, w_out, w_ff1, w_ff2)
    attn_rings, feed_rings = [None] * (layer_total + 1), [None] * (layer_total + 1)
    attn_rings[0], feed_rings[0] = rings(0, arrays, time_piece)
    for layer in range(1, layer_total):
        attn_rings[layer], feed_rings[layer] = rings(layer, arrays, None)
    later = attn_rings[1:-1] + feed_rings[1:-1]
    step = 0
    while not attn_rings[0].done:
        beside = (attn_rings[0], feed_rings[0] if step >= 3 else None)
        if step == 1:
            tokens, back_slot = tick((tokens, back_slot), *beside)
            own_tokens = owner_swap(pick(tokens, back_slot))
        elif step == 3:
            own_tokens = tick(own_tokens, *beside)
            token_blocks = wires.rows_in(own_tokens)
        elif step == 4:
            token_blocks[-1] = tick(token_blocks[-1], *beside)
            token_blocks[-1], *pieces = tie(token_blocks[-1], *(task.pending for task in later))
            for task, piece in zip(later, pieces):
                task.pending = piece
        else:
            tick((), *beside)
        step += 1
    attn_w, time_row = attn_rings[0].result
    time_row = time_row.astype(F32)

    seq_ends = jnp.cumsum(lengths[0])
    positions = jnp.arange(group_rows, dtype=jnp.int32)
    if wires.tensor_size == 2:
        positions = (positions + tensor_index * rows_dev) % group_rows
    segment = jnp.sum((positions[:, None] >= seq_ends[None, :]).astype(jnp.int32), axis=1)

    stream = own_tokens.astype(F32) + time_row
    weights, saved = [], []
    for layer in range(layer_total):
        if layer == 0:
            input_blocks = [(rows.astype(F32) + time_row).astype(BF16) for rows in token_blocks]
        else:
            input_blocks = wires.rows_in(stream.astype(BF16))
            input_blocks[-1] = tick(input_blocks[-1], attn_rings[layer], feed_rings[layer])
            attn_w = attn_rings[layer].finish()
        ahead = (attn_rings[layer + 1], feed_rings[layer + 1])
        biases = []
        for mine in both:
            bias_q, bias_v = [wires.half(b_qv[layer, i], 0, mine) for i in (0, 1)]
            biases.append(jnp.concatenate([bias_q, jnp.zeros_like(bias_q), bias_v]))
        (qkv, mixture, log_total), _ = attend_forward(input_blocks, attn_w[0], biases[0], segment)
        attention = [(qkv, mixture, log_total)]
        part, sums = attend_forward(
            input_blocks, attn_w[1], biases[1], segment, (mixture, attn_w[0])
        )
        attention.append(part)
        sums[-1] = tick(sums[-1], feed_rings[layer])
        attended = tick(wires.rows_out(sums), feed_rings[layer], ahead[0])
        middle = stream + attended + out_bias[layer, 0]
        normed = layer_norm(middle, ln_gain[layer, 0], ln_shift[layer, 0])
        normed_low = normed.astype(BF16)
        tick(normed_low, feed_rings[layer])
        normed_blocks = wires.rows_in(normed_low)
        normed_blocks[-1] = tick(normed_blocks[-1], *ahead)
        feed_w = feed_rings[layer].finish()
        weights.append((attn_w, feed_w))
        bias = jnp.concatenate([wires.half(b_ff1[layer], 0, mine) for mine in both])[None]
        sums, *filled = feed(normed_blocks, feed_w, bias, True)
        if layer == 0:
            sums[-1], cotangent = tie(sums[-1], cotangent)
            upstream = owner_swap(pick(cotangent, back_slot))
        sums[-1] = tick(sums[-1], ahead[0])
        arrived = tick(wires.rows_out(sums), *ahead)
        second_sum = normed + arrived + out_bias[layer, 1]
        saved.append((input_blocks, attention, middle, normed_blocks, filled, second_sum))
        stream = layer_norm(second_sum, ln_gain[layer, 1], ln_shift[layer, 1])

    encoded_own = stream.astype(BF16)
    gradient = upstream.astype(F32)
    feed_tasks, attn_tasks = [None] * (layer_total + 1), [None] * (layer_total + 1)
    attn_sums, reduced, matrices = None, [None] * layer_total, None
    direct = inner % 128 == 0 and hidden % 128 == 0
    vector_grads = [None] * layer_total
    for layer in reversed(range(layer_total)):
        attn_w, feed_w = weights[layer]
        input_blocks, attention, middle, normed_blocks, (act, slope), second_sum = saved[layer]
        _, pull_second = jax.vjp(layer_norm, second_sum, ln_gain[layer, 1], ln_shift[layer, 1])
        grad_second, gain_second, shift_second = pull_second(gradient)
        later_feed, later_attn = feed_tasks[layer + 1], None
        send = tick(grad_second.astype(BF16), later_feed)
        if layer == layer_total - 1:
            send, encoded_own = tie(send, encoded_own)
            returned_out = owner_swap(encoded_own)
        if attn_sums is not None:
            send, *attn_sums = tie(send, *attn_sums)
            later_attn = attn_tasks[layer + 1] = Task(wires.reduce_ring(attn_sums))
        branch_blocks = wires.rows_in(send)
        branch_blocks[-1] = tick(branch_blocks[-1], later_feed, later_attn)
        sums, grad_pre, hidden_sums = feed(branch_blocks, feed_w, slope, False)
        hidden_sums = hidden_sums[0]
        pairs = [(normed_blocks, grad_pre, hidden), (branch_blocks, act, hidden)]
        came = wires.partner(weight_gradients(pairs, 1))
        grad_normed = grad_second + wires.rows_out(sums)
        _, pull_first = jax.vjp(layer_norm, middle, ln_gain[layer, 0], ln_shift[layer, 0])
        grad_middle, gain_first, shift_first = pull_first(grad_normed)
        send, *feed_sums = tie(grad_middle.astype(BF16), weight_gradients(pairs, 0), came)
        feed_tasks[layer] = Task(wires.reduce_ring(feed_sums))
        attend_blocks = wires.rows_in(send)
        attend_blocks[-1] = tick(attend_blocks[-1], feed_tasks[layer], later_attn)

        def attn_pairs(half, wide):
            return [(input_blocks, wide, 3 * inner), (attend_blocks, attention[half][1], inner)]

        wide, part_sums, _ = attend_backward(attend_blocks, attn_w[1], *attention[1], segment)
        send = weight_gradients(attn_pairs(1, wide), 1)
        came = wires.partner(send)
        own_wide, own_sums, sums = attend_backward(
            attend_blocks, attn_w[0], *attention[0], segment, (wide, attn_w[1])
        )
        sums[-1] = tick(sums[-1], feed_tasks[layer], later_attn)
        attn_sums = [weight_gradients(attn_pairs(0, own_wide), 0), came]
        if layer == 0:
            first_portions = wires.first_portions(attn_sums)
        arrived = wires.rows_out(sums)
        if layer + 1 < layer_total:
            reduced[layer + 1] = (later_attn.finish(), later_feed.finish())
            if direct:
                matrices = matrix_outputs(
                    wires.spot, layer + 1, layer_total, *reduced[layer + 1], matrices
                )
                arrived, matrices = tie(arrived, matrices)
        if layer == 0:
            arrived, encoded = tie(arrived, pick(returned_out, deal_slot))
            attn_tasks[0] = Task(wires.reduce_ring(attn_sums, first_portions))
        gradient = grad_middle + arrived
        qkv_sums = [part.reshape(3, inner)[::2] for part in (own_sums, part_sums)]
        vector_grads[layer] = (
            wires.ordered(qkv_sums[0], qkv_sums[1], 1),
            wires.ordered(hidden_sums[:hidden], hidden_sums[hidden:], 0),
            jnp.stack([jnp.sum(grad_middle, axis=0), jnp.sum(grad_second, axis=0)]),
            jnp.stack([gain_first, gain_second]),
            jnp.stack([shift_first, shift_second]),
        )

    returned_grad = owner_swap(gradient.astype(BF16))
    time_grad = jnp.sum(gradient, axis=0)
    local = [jnp.stack([part[i] for part in vector_grads]) for i in range(5)]
    flat = jnp.concatenate([part.reshape(-1) for part in local[:2] + [time_grad] + local[2:]])
    border = local[0].size + local[1].size
    vector_task = Task(wires.butterfly(flat, border))
    vector_task.finish()
    reduced[0] = (attn_tasks[0].finish(), feed_tasks[0].finish())
    flat, shared = vector_task.result
    grad_tokens = pick(returned_grad, deal_slot)
    if direct:
        matrices = matrix_outputs(wires.spot, 0, layer_total, *reduced[0], matrices)
        matrices = [part.transpose(0, 2, 1) if i % 2 else part for i, part in enumerate(matrices)]
    else:
        parts = []
        for attn_pair, feed_pair in reduced:
            rows = attn_pair[0].shape[0]
            qkv = [
                part[:, : 3 * inner].reshape(rows, 3, inner).transpose(1, 0, 2).astype(F32)
                for part in attn_pair
            ]
            parts.append(
                (
                    wires.ordered(*qkv, 2),
                    wires.ordered(*(part[:, 3 * inner :].T.astype(F32) for part in attn_pair), 0),
                    wires.ordered(*(part[:, :hidden].astype(F32) for part in feed_pair), 1),
                    wires.ordered(*(part[:, hidden:].T.astype(F32) for part in feed_pair), 0),
                )
            )
        matrices = [jnp.stack([part[i] for part in parts]) for i in range(4)]
    grad_b_qv = flat[: local[0].size].reshape(local[0].shape)
    grad_b_ff1 = flat[local[0].size : border].reshape(local[1].shape)
    time_grad = shared[:D]
    rest = shared[D:].reshape(3, layer_total, 2, D)
    return (
        encoded,
        grad_tokens,
        time_grad,
        matrices[0],
        grad_b_qv,
        matrices[1],
        rest[0],
        rest[1],
        rest[2],
        matrices[2],
        grad_b_ff1,
        matrices[3],
    )


def solution(mesh):
    return jax.shard_map(
        body,
        mesh=mesh,
        in_specs=(
            P(("dp", "tensor"), None),
            P(("dp", "tensor"), None),
            P(("dp", "tensor")),
            P(("dp", "tensor")),
            P("dp", None),
            P(),
            P(None, "dp"),
            P(None, None, "dp", "tensor"),
            P(None, None, "tensor"),
            P(None, "tensor", "dp"),
            P(),
            P(),
            P(),
            P(None, "dp", "tensor"),
            P(None, "tensor"),
            P(None, "tensor", "dp"),
        ),
        out_specs=(
            P(("dp", "tensor"), None),
            P(("dp", "tensor"), None),
            P(),
            P(None, None, "dp", "tensor"),
            P(None, None, "tensor"),
            P(None, "tensor", "dp"),
            P(),
            P(),
            P(),
            P(None, "dp", "tensor"),
            P(None, "tensor"),
            P(None, "tensor", "dp"),
        ),
        check_vma=False,
    )
```

```python
import math

import jax
import jax.numpy as jnp
import numpy as np
from jax import lax
from jax.experimental import pallas as pl
from jax.experimental.pallas import tpu as pltpu
from jax.sharding import PartitionSpec as P

D = 1024
HEADS = 16
FF = 4096
HEAD = D // HEADS
F32 = jnp.float32
BF16 = jnp.bfloat16
SMALL_COST = pl.CostEstimate(flops=1000, bytes_accessed=1000, transcendentals=0)


def layer_norm(summed, scaling, offset_vec):
    centre = jnp.mean(summed, axis=-1, keepdims=True)
    spread = summed - centre
    variance = jnp.mean(spread * spread, axis=-1, keepdims=True)
    return spread * lax.rsqrt(variance + 1e-05) * scaling + offset_vec


def dot(left, right):
    return jnp.dot(left, right, preferred_element_type=F32)


def contract_rows(left, right):
    return lax.dot_general(left, right, (((0,), (0,)), ((), ())), preferred_element_type=F32)


def times_transposed(left, right):
    return lax.dot_general(left, right, (((1,), (1,)), ((), ())), preferred_element_type=F32)


class Wires:
    def __init__(self, dp_size, tensor_size):
        self.dp_size, self.tensor_size = dp_size, tensor_size
        chips = dp_size // 2
        self.chips = chips
        order = list(range(0, chips, 2)) + list(range(chips - 1, 0, -2))
        place = {chip: spot for spot, chip in enumerate(order)}
        self.rounds = chips // 2
        ahead, spots = [], np.zeros((dp_size, chips + 1), np.int32)
        for device in range(dp_size):
            chip, core = divmod(device, 2)
            way = 1 if core == 0 else -1
            ahead.append((device, 2 * order[(place[chip] + way) % chips] + core))
            spots[device, :chips] = [order[(place[chip] + way * s) % chips] for s in range(chips)]
            spots[device, chips] = core
        self.ahead = ahead
        self.back = [(there, here) for here, there in ahead]
        self.swap = [(d, d ^ 1) for d in range(dp_size)]
        dp_index = lax.axis_index("dp")
        self.core = dp_index % 2
        self.spot = lax.dynamic_index_in_dim(jnp.asarray(spots), dp_index, 0, keepdims=False)

    def round(self, forth, back):
        if back is None:
            return [lax.ppermute(forth, "dp", self.ahead)]
        return [lax.ppermute(forth, "dp", self.ahead), lax.ppermute(back, "dp", self.back)]

    def partner(self, array):
        return lax.ppermute(array, "dp", self.swap)

    def across(self, array):
        return lax.ppermute(array, "tensor", [(0, 1), (1, 0)])

    def half(self, array, axis, mine):
        width = array.shape[axis] // 2
        index = self.core if mine else 1 - self.core
        return lax.dynamic_slice_in_dim(array, index * width, width, axis)

    def ordered(self, mine, other, axis):
        return jnp.where(
            self.core == 0,
            jnp.concatenate([mine, other], axis),
            jnp.concatenate([other, mine], axis),
        )

    def chip_piece(self, shard):
        mine, other = shard
        return self.ordered(mine, self.partner(other), 0)

    def gather_ring(self, piece, extra=None):
        chip_rows = piece.shape[0]
        if extra is not None:
            tail = jnp.zeros((8, piece.shape[1]), piece.dtype)
            pair = self.ordered(extra, self.partner(extra), 0)
            tail = lax.dynamic_update_slice(tail, pair[None, :], (0, 0))
            piece = jnp.concatenate([piece, tail], 0)
        piece = yield piece
        forth, back = [piece], [piece]
        for step in range(1, self.rounds + 1):
            both_ways = step < self.chips - self.rounds
            came = yield self.round(forth[-1], back[-1] if both_ways else None)
            forth.append(came[0])
            back += came[1:]
            if step == self.rounds - 1:
                places = [0] + [-s % self.chips for s in range(1, len(forth))] + list(range(1, len(back)))
                outs = place_pieces(self.spot, places, forth + back[1:], chip_rows, None)
        outs = place_pieces(self.spot, [-self.rounds % self.chips], forth[-1:], chip_rows, outs)
        whole, vector = outs[0], outs[-1]
        halves = (whole, self.partner(whole))
        return halves if extra is None else (halves, vector[:, 0, :chip_rows].reshape(-1))

    def first_portions(self, sums):
        return add_portions(self.spot, [self.rounds, 1 + self.rounds], [], sums)

    def reduce_ring(self, sums, first=None):
        forth, back = first or self.first_portions(sums)
        for step in range(1, self.rounds + 1):
            both_ways = step < self.chips - self.rounds
            came = yield self.round(forth, back if both_ways else None)
            places = [self.rounds - step] if step < self.rounds else []
            if step + 1 < self.chips - self.rounds:
                places.append(1 + self.rounds + step)
            added = add_portions(self.spot, places, came, sums) if places else []
            forth = added[0] if step < self.rounds else came[0]
            if both_ways:
                back = added[1] if len(places) == 2 else came[1]
        mine, other = last_portion(self.spot, [forth, back], sums)
        return mine, self.partner(other)

    def rows_in(self, local_rows):
        if self.tensor_size == 2:
            return [local_rows, self.across(local_rows)]
        return [lax.all_gather(local_rows, "tensor", axis=0, tiled=True)]

    def rows_out(self, sums):
        if self.tensor_size == 2:
            return sums[0] + self.across(sums[1]).astype(F32)
        return lax.psum_scatter(sums[0], "tensor", scatter_dimension=0, tiled=True).astype(F32)

    def butterfly(self, array, border):
        for axis, size in (("dp", self.dp_size), ("tensor", self.tensor_size)):
            if axis == "tensor":
                array, kept = array[border:], array
            bit = 1
            while bit < size:
                pairs = [(i, i ^ bit) for i in range(size)]
                array = array + (yield lax.ppermute(array, axis, pairs))
                bit *= 2
        return kept, array


def pick(rows, index):
    return rows.at[index].get(mode="promise_in_bounds")


def owner_swap(rows):
    return lax.all_to_all(rows, "dp", split_axis=0, concat_axis=0, tiled=True)


class Task:
    def __init__(self, steps):
        self.steps, self.done, self.result = steps, False, None
        self.advance(None, first=True)

    def advance(self, arrived, first=False):
        try:
            self.pending = next(self.steps) if first else self.steps.send(arrived)
        except StopIteration as stop:
            self.done, self.result = True, stop.value

    def finish(self):
        while not self.done:
            self.advance(self.pending)
        return self.result


def tick(value, *tasks):
    tasks = [task for task in tasks if task is not None and not task.done]
    if not tasks:
        return value
    value, arrived = lax.optimization_barrier((value, [task.pending for task in tasks]))
    for task, part in zip(tasks, arrived):
        task.advance(part)
    return value


def tie(*values):
    return lax.optimization_barrier(values)


def place_pieces(spot, places, pieces, chip_rows, filled):
    count, width = len(pieces), pieces[0].shape[1]
    chips = spot.shape[0] - 1
    spare = pieces[0].shape[0] - chip_rows
    given = 0 if filled is None else len(filled)

    def kernel(spot_ref, *refs):
        ins, outs, sems = refs[:count], refs[count + given : -1], refs[-1]
        copies = []
        for i, piece in enumerate(ins):
            chip = spot_ref[places[i]]
            rows = pl.ds(pl.multiple_of(chip * chip_rows, chip_rows), chip_rows)
            copies.append(
                pltpu.make_async_copy(piece.at[0:chip_rows], outs[0].at[rows], sems.at[i, 0])
            )
            if spare:
                copies.append(
                    pltpu.make_async_copy(
                        piece.at[chip_rows : chip_rows + spare, 0:128],
                        outs[1].at[chip],
                        sems.at[i, 1],
                    )
                )
        for copy in copies:
            copy.start()
        for copy in copies:
            copy.wait()

    shapes = [jax.ShapeDtypeStruct((chips * chip_rows, width), BF16)]
    if spare:
        shapes.append(jax.ShapeDtypeStruct((chips, spare, 128), BF16))
    return pl.pallas_call(
        kernel,
        out_shape=shapes,
        in_specs=[pl.BlockSpec(memory_space=pltpu.SMEM)]
        + [pl.BlockSpec(memory_space=pl.ANY)] * (count + given),
        out_specs=[pl.BlockSpec(memory_space=pl.ANY)] * len(shapes),
        scratch_shapes=[pltpu.SemaphoreType.DMA((count, 2))],
        input_output_aliases={1 + count + i: i for i in range(given)},
        compiler_params=pltpu.CompilerParams(vmem_limit_bytes=8 << 20),
        cost_estimate=pl.CostEstimate(
            flops=0, bytes_accessed=1 << 26, transcendentals=0
        ),
        name="place_pieces",
    )(spot, *pieces, *(filled or ()))


def attend_forward(blocks, weight, bias, segment, earlier=None):
    rows = sum(block.shape[0] for block in blocks)
    inner = weight.shape[1] // 4
    heads = inner // HEAD
    step = min(512, rows)
    scale = 1.0 / math.sqrt(HEAD)
    extra = 0 if earlier is None else 2

    def kernel(*refs):
        xs, refs = refs[: len(blocks)], refs[len(blocks) :]
        w_ref, bias_ref, col_ref, row_ref = refs[:4]
        before, refs = refs[4 : 4 + extra], refs[4 + extra :]
        qkv_ref, out_ref, log_ref = refs[:3]
        start = 0
        for x in xs:
            size = x.shape[0]
            projected = dot(x[...], w_ref[:, : 3 * inner]) + bias_ref[...]
            qkv_ref[start : start + size, :] = projected.astype(BF16)
            start += size
        for first in range(0, rows, step):
            part = slice(first, first + step)
            far = jnp.where(col_ref[...] == row_ref[:, part], 0.0, -1e30)
            mixed = []
            for h in range(heads):
                lanes = [slice(i * inner + h * HEAD, i * inner + (h + 1) * HEAD) for i in range(3)]
                scores = times_transposed(qkv_ref[:, lanes[1]], qkv_ref[part, lanes[0]])
                scores = scores * scale + far
                highest = jnp.max(scores, axis=0, keepdims=True)
                powers = jnp.exp(scores - highest)
                summed = jnp.sum(powers, axis=0, keepdims=True)
                mixture = contract_rows(qkv_ref[:, lanes[2]], powers.astype(BF16))
                mixed.append(mixture * (1.0 / summed))
                log_ref[h : h + 1, part] = highest + jnp.log(summed)
            out_ref[part, :] = jnp.concatenate(mixed, 0).T.astype(BF16)
        start = 0
        for sum_ref in refs[3:]:
            part = slice(start, start + sum_ref.shape[0])
            start += sum_ref.shape[0]
            total = times_transposed(before[0][part, :], before[1][:, 3 * inner :])
            total += times_transposed(out_ref[part, :], w_ref[:, 3 * inner :])
            sum_ref[...] = total.astype(sum_ref.dtype)

    shapes = [
        jax.ShapeDtypeStruct((rows, 3 * inner), BF16),
        jax.ShapeDtypeStruct((rows, inner), BF16),
        jax.ShapeDtypeStruct((heads, rows), F32),
    ]
    if earlier is not None:
        shapes += sum_shapes(blocks)
    outs = pl.pallas_call(
        kernel,
        out_shape=shapes,
        compiler_params=pltpu.CompilerParams(vmem_limit_bytes=20 << 20),
        cost_estimate=SMALL_COST,
        name="attend_forward",
    )(*blocks, weight, bias[None], segment[:, None], segment[None], *(earlier or ()))
    return tuple(outs[:3]), list(outs[3:])


def sum_shapes(blocks):
    kinds = (F32, BF16) if len(blocks) == 2 else (BF16,)
    return [jax.ShapeDtypeStruct(block.shape, kind) for block, kind in zip(blocks, kinds)]


def attend_backward(blocks, weight, qkv, mixture, log_total, segment, earlier=None):
    rows = sum(block.shape[0] for block in blocks)
    inner = weight.shape[1] // 4
    extra = 0 if earlier is None else 2
    heads = inner // HEAD
    step = min(512, rows)
    scale = 1.0 / math.sqrt(HEAD)

    def kernel(*refs):
        xs = refs[: len(blocks)]
        (w_ref, qkv_ref, mix_ref, log_ref, col_ref, row_ref) = refs[len(blocks) : len(blocks) + 6]
        refs = refs[len(blocks) + 6 :]
        before, refs = refs[:extra], refs[extra:]
        grad_ref, sum_ref, dout_ref = refs[0], refs[1], refs[-1]
        start = 0
        for x in xs:
            size = x.shape[0]
            dout_ref[start : start + size, :] = dot(x[...], w_ref[:, 3 * inner :]).astype(BF16)
            start += size
        ones = jnp.ones((8, HEAD), F32)
        keys = [jnp.zeros((rows, HEAD), F32)] * heads
        values = [jnp.zeros((rows, HEAD), F32)] * heads
        for first in range(0, rows, step):
            part = slice(first, first + step)
            far = jnp.where(col_ref[...] == row_ref[:, part], 0.0, -1e30)
            queries = []
            for h in range(heads):
                lanes = [slice(i * inner + h * HEAD, i * inner + (h + 1) * HEAD) for i in range(3)]
                query, key = qkv_ref[part, lanes[0]], qkv_ref[:, lanes[1]]
                dout = dout_ref[part, lanes[0]]
                scores = times_transposed(key, query) * scale + far
                weights = jnp.exp(scores - log_ref[h : h + 1, part])
                product = dout.astype(F32) * mix_ref[part, lanes[0]].astype(F32)
                centre = lax.dot_general(
                    ones,
                    product,
                    (((1,), (1,)), ((), ())),
                    precision=lax.Precision.HIGHEST,
                    preferred_element_type=F32,
                )[0:1]
                grad_weights = times_transposed(qkv_ref[:, lanes[2]], dout)
                grad_scores = (weights * (grad_weights - centre)).astype(BF16)
                queries.append(contract_rows(key, grad_scores))
                keys[h] = keys[h] + dot(grad_scores, query)
                values[h] = values[h] + dot(weights.astype(BF16), dout)
            grad_ref[part, 0:inner] = (jnp.concatenate(queries, 0).T * scale).astype(BF16)
        for h in range(heads):
            grad_ref[:, inner + h * HEAD : inner + (h + 1) * HEAD] = (keys[h] * scale).astype(BF16)
            grad_ref[:, 2 * inner + h * HEAD : 2 * inner + (h + 1) * HEAD] = values[h].astype(BF16)
        sum_ref[...] = jnp.sum(grad_ref[...].astype(F32), axis=0, keepdims=True)
        start = 0
        for out_ref in refs[2:-1]:
            part = slice(start, start + out_ref.shape[0])
            start += out_ref.shape[0]
            total = times_transposed(before[0][part, :], before[1][:, : 3 * inner])
            total += times_transposed(grad_ref[part, :], w_ref[:, : 3 * inner])
            out_ref[...] = total.astype(out_ref.dtype)

    shapes = [
        jax.ShapeDtypeStruct((rows, 3 * inner), BF16),
        jax.ShapeDtypeStruct((1, 3 * inner), F32),
    ]
    if earlier is not None:
        shapes += sum_shapes(blocks)
    outs = pl.pallas_call(
        kernel,
        out_shape=shapes,
        scratch_shapes=[pltpu.VMEM((rows, inner), BF16)],
        compiler_params=pltpu.CompilerParams(vmem_limit_bytes=24 << 20),
        cost_estimate=SMALL_COST,
        name="attend_backward",
    )(*blocks, weight, qkv, mixture, log_total, segment[:, None], segment[None], *(earlier or ()))
    return outs[0], outs[1], list(outs[2:])


def normal_parts(x):
    bell = jnp.exp(-0.5 * x * x)
    t = 1.0 / (1.0 + 0.23164189 * jnp.abs(x))
    tail = 0.5307027145
    for c in (-0.7265760135, 0.7107068705, -0.142248368, 0.127414796):
        tail = tail * t + c
    tail = tail * t * bell
    return jnp.where(x >= 0.0, 1.0 - tail, tail), bell * 0.3989422804014327


def feed(blocks, weights, side, forward):
    rows = sum(block.shape[0] for block in blocks)
    hidden = weights[0].shape[1] // 2
    tile = min(512, hidden)
    tiles = hidden // tile
    into, onto = (0, hidden) if forward else (hidden, 0)

    def kernel(*refs):
        xs, refs = refs[: len(blocks)], refs[len(blocks) :]
        *halves, side_ref = refs[:3]
        outs, (kept_ref, more_ref, pre_ref) = refs[3:-3], refs[-3:]

        def project(half, index):
            start, slot = 0, lax.rem(index, 2)
            first = index * tile + into
            if not isinstance(index, int):
                first = pl.multiple_of(first, tile)
            for x in xs:
                part = pl.ds(start, x.shape[0])
                pre_ref[slot, part, :] = dot(x[...], halves[half][:, pl.ds(first, tile)])
                start += x.shape[0]

        def activate(half, index):
            first = index * tile + half * hidden
            if not isinstance(index, int):
                first = pl.multiple_of(first, tile)
            columns = pl.ds(first, tile)
            pre = pre_ref[lax.rem(index, 2)]
            if forward:
                pre = pre + side_ref[:, columns]
                cdf, bell = normal_parts(pre)
                kept_ref[:, columns] = (pre * cdf).astype(BF16)
                more_ref[:, columns] = (cdf + pre * bell).astype(BF16)
            else:
                kept = (pre * side_ref[:, columns].astype(F32)).astype(BF16)
                kept_ref[:, columns] = kept
                more_ref[:, columns] = jnp.sum(kept.astype(F32), axis=0, keepdims=True)

        for half in (0, 1):
            project(half, 0)

            def step(index, _, half=half):
                project(half, index)
                activate(half, index - 1)
                return 0

            lax.fori_loop(1, tiles, step, 0)
            activate(half, tiles - 1)
        start = 0
        for out in outs:
            part = slice(start, start + out.shape[0])
            start += out.shape[0]
            total = times_transposed(kept_ref[part, 0:hidden], halves[0][:, onto : onto + hidden])
            total += times_transposed(kept_ref[part, hidden:], halves[1][:, onto : onto + hidden])
            out[...] = total.astype(out.dtype)

    wide = jax.ShapeDtypeStruct((rows, 2 * hidden), BF16)
    outs = pl.pallas_call(
        kernel,
        out_shape=sum_shapes(blocks)
        + [wide, wide if forward else jax.ShapeDtypeStruct((1, 2 * hidden), F32)],
        scratch_shapes=[pltpu.VMEM((2, rows, tile), F32)],
        compiler_params=pltpu.CompilerParams(vmem_limit_bytes=24 << 20),
        cost_estimate=SMALL_COST,
        name="feed_forward" if forward else "feed_backward",
    )(*blocks, *weights, side)
    return list(outs[:-2]), outs[-2], outs[-1]


def weight_gradients(pairs, half):
    widths = [width for _, _, width in pairs]
    tile = math.gcd(512, *widths)
    if tile % 128:
        terms = [
            contract_rows(join(blocks), _columns(right, half, width))
            for blocks, right, width in pairs
        ]
        return jnp.concatenate(terms, 1).astype(BF16)
    counts = [width // tile for width in widths]
    edge = counts[0]
    blocks_flat = [block for blocks, _, _ in pairs for block in blocks]
    per = len(pairs[0][0])
    rows = sum(block.shape[0] for block in pairs[0][0])

    def kernel(*refs):
        lefts, refs = refs[: 2 * per], refs[2 * per :]
        rights, (out_ref, turned) = refs[:2], refs[2:]
        index = pl.program_id(0)

        @pl.when(index == 0)
        def _():
            for pair in (0, 1):
                start = 0
                for left in lefts[pair * per : (pair + 1) * per]:
                    turned[pair, :, start : start + left.shape[0]] = left[...].T
                    start += left.shape[0]

        def run(pair):
            out_ref[...] = dot(turned[pair], rights[pair][...]).astype(BF16)

        @pl.when(index < edge)
        def _():
            run(0)

        @pl.when(index >= edge)
        def _():
            run(1)

    shifts = [
        half * counts[i] if pairs[i][1].shape[1] > widths[i] else 0 for i in (0, 1)
    ]
    last = counts[1] - 1
    specs = [pl.BlockSpec(block.shape, lambda i: (0, 0)) for block in blocks_flat]
    specs += [
        pl.BlockSpec((rows, tile), lambda i: (0, jnp.minimum(i, edge - 1) + shifts[0])),
        pl.BlockSpec((rows, tile), lambda i: (0, jnp.clip(i - edge, 0, last) + shifts[1])),
    ]
    over = pl.BlockSpec((D, tile), lambda i: (0, i))
    return pl.pallas_call(
        kernel,
        grid=(sum(counts),),
        out_shape=jax.ShapeDtypeStruct((D, sum(widths)), BF16),
        in_specs=specs,
        out_specs=over,
        scratch_shapes=[pltpu.VMEM((2, D, rows), BF16)],
        compiler_params=pltpu.CompilerParams(vmem_limit_bytes=16 << 20),
        cost_estimate=SMALL_COST,
        name="weight_gradients",
    )(*blocks_flat, pairs[0][1], pairs[1][1])


def _columns(right, half, width):
    return right[:, half * width : (half + 1) * width] if right.shape[1] > width else right


def add_portions(spot, places, came, sums):
    count, given = len(places), min(len(came), len(places))
    shape = (sums[0].shape[0] // (spot.shape[0] - 1), sums[0].shape[1])

    def kernel(spot_ref, *refs):
        ins, parts, outs = refs[:given], refs[given:-count], refs[-count:]
        for i, out in enumerate(outs):
            total = sum(part[...].astype(F32) for part in parts[i * len(sums) : (i + 1) * len(sums)])
            if given:
                total += ins[i][...].astype(F32)
            out[...] = total.astype(BF16)

    whole = pl.BlockSpec(shape, lambda i, s: (0, 0))
    portions = [pl.BlockSpec(shape, lambda i, s, k=k: (s[k], 0)) for k in places for _ in sums]
    return pl.pallas_call(
        kernel,
        grid_spec=pltpu.PrefetchScalarGridSpec(
            num_scalar_prefetch=1,
            grid=(1,),
            in_specs=[whole] * given + portions,
            out_specs=[whole] * count,
        ),
        out_shape=[jax.ShapeDtypeStruct(shape, BF16)] * count,
        compiler_params=pltpu.CompilerParams(vmem_limit_bytes=8 << 20),
        cost_estimate=SMALL_COST,
        name="add_portions",
    )(spot, *came[:given], *(list(sums) * count))


def last_portion(spot, came, sums):
    chips = spot.shape[0] - 1
    shape = (sums[0].shape[0] // chips, sums[0].shape[1])
    rows = shape[0] // 2

    def kernel(spot_ref, *refs):
        ins, (mine, other, total) = refs[:-3], refs[-3:]
        total[...] = sum(part[...].astype(F32) for part in ins)
        first = pl.multiple_of(spot_ref[chips] * rows, rows)
        mine[...] = total[pl.ds(first, rows), :]
        other[...] = total[pl.ds(rows - first, rows), :].astype(BF16)

    whole = pl.BlockSpec(shape, lambda i, s: (0, 0))
    half = pl.BlockSpec((rows, shape[1]), lambda i, s: (0, 0))
    return pl.pallas_call(
        kernel,
        grid_spec=pltpu.PrefetchScalarGridSpec(
            num_scalar_prefetch=1,
            grid=(1,),
            in_specs=[whole] * len(came) + [pl.BlockSpec(shape, lambda i, s: (s[0], 0))] * len(sums),
            out_specs=[half] * 2,
            scratch_shapes=[pltpu.VMEM(shape, F32)],
        ),
        out_shape=[
            jax.ShapeDtypeStruct((rows, shape[1]), F32),
            jax.ShapeDtypeStruct((rows, shape[1]), BF16),
        ],
        compiler_params=pltpu.CompilerParams(vmem_limit_bytes=8 << 20),
        cost_estimate=SMALL_COST,
        name="last_portion",
    )(spot, *came, *sums)


def matrix_outputs(spot, layer, layer_total, attn_pair, feed_pair, filled):
    rows, inner, hidden = attn_pair[0].shape[0], attn_pair[0].shape[1] // 4, feed_pair[0].shape[1] // 2
    chips = spot.shape[0] - 1
    shapes = [
        (layer_total, 3, rows, 2 * inner),
        (layer_total, rows, 2 * inner),
        (layer_total, rows, 2 * hidden),
        (layer_total, rows, 2 * hidden),
    ]
    given = 0 if filled is None else 4

    def kernel(spot_ref, *refs):
        pairs, (qkv, out, first, second) = (refs[0:2], refs[2:4]), refs[4 + given :]
        for index in (0, 1):
            attn, feed = (pair[index][...].astype(F32) for pair in pairs)
            core = spot_ref[chips] if index == 0 else 1 - spot_ref[chips]
            heads = pl.ds(pl.multiple_of(core * inner, inner), inner)
            units = pl.ds(pl.multiple_of(core * hidden, hidden), hidden)
            for i in range(3):
                qkv[0, i, :, heads] = attn[:, i * inner : (i + 1) * inner]
            out[0, :, heads] = attn[:, 3 * inner :]
            first[0, :, units] = feed[:, :hidden]
            second[0, :, units] = feed[:, hidden:]

    def over(shape):
        return pl.BlockSpec((1,) + shape[1:], lambda i, s: (layer,) + (0,) * (len(shape) - 1))

    ins = (*attn_pair, *feed_pair)
    return pl.pallas_call(
        kernel,
        grid_spec=pltpu.PrefetchScalarGridSpec(
            num_scalar_prefetch=1,
            grid=(1,),
            in_specs=[pl.BlockSpec(part.shape, lambda i, s: (0, 0)) for part in ins]
            + [pl.BlockSpec(memory_space=pl.ANY)] * given,
            out_specs=[over(shape) for shape in shapes],
        ),
        out_shape=[jax.ShapeDtypeStruct(shape, F32) for shape in shapes],
        input_output_aliases={5 + i: i for i in range(given)},
        compiler_params=pltpu.CompilerParams(vmem_limit_bytes=12 << 20),
        cost_estimate=SMALL_COST,
        name="matrix_outputs",
    )(spot, *ins, *(filled or ()))


def join(blocks):
    return blocks[0] if len(blocks) == 1 else jnp.concatenate(blocks, 0)


def body(
    tokens,
    cotangent,
    deal_slot,
    back_slot,
    lengths,
    time_step,
    time_table,
    w_qkv,
    b_qv,
    w_out,
    out_bias,
    ln_gain,
    ln_shift,
    w_ff1,
    b_ff1,
    w_ff2,
):
    wires = Wires(lax.axis_size("dp"), lax.axis_size("tensor"))
    rows_dev = tokens.shape[0]
    group_rows = rows_dev * wires.tensor_size
    tensor_index = lax.axis_index("tensor")
    layer_total = w_qkv.shape[0]
    inner = w_qkv.shape[3] // 2
    hidden = w_ff1.shape[2] // 2
    both = (True, False)

    time_piece = lax.dynamic_index_in_dim(time_table, time_step[0], 0, keepdims=False)

    def rings(layer, arrays, extra):
        w_qkv, w_out, w_ff1, w_ff2 = arrays
        attn_shard, feed_shard = [], []
        for mine in both:
            qkv = wires.half(w_qkv[layer], 2, mine)
            out = wires.half(w_out[layer], 0, mine).T
            attn_shard.append(jnp.concatenate([qkv[0], qkv[1], qkv[2], out], axis=1))
            first = wires.half(w_ff1[layer], 1, mine)
            second = wires.half(w_ff2[layer], 0, mine).T
            feed_shard.append(jnp.concatenate([first, second], axis=1))
        return (
            Task(wires.gather_ring(wires.chip_piece(attn_shard), extra)),
            Task(wires.gather_ring(wires.chip_piece(feed_shard))),
        )

    arrays = (w_qkv, w_out, w_ff1, w_ff2)
    attn_rings, feed_rings = [None] * (layer_total + 1), [None] * (layer_total + 1)
    attn_rings[0], feed_rings[0] = rings(0, arrays, time_piece)
    for layer in range(1, layer_total):
        attn_rings[layer], feed_rings[layer] = rings(layer, arrays, None)
    later = attn_rings[1:-1] + feed_rings[1:-1]
    step = 0
    while not attn_rings[0].done:
        beside = (attn_rings[0], feed_rings[0] if step >= 3 else None)
        if step == 1:
            tokens, back_slot = tick((tokens, back_slot), *beside)
            own_tokens = owner_swap(pick(tokens, back_slot))
        elif step == 3:
            own_tokens = tick(own_tokens, *beside)
            token_blocks = wires.rows_in(own_tokens)
        elif step == 4:
            token_blocks[-1] = tick(token_blocks[-1], *beside)
            token_blocks[-1], *pieces = tie(token_blocks[-1], *(task.pending for task in later))
            for task, piece in zip(later, pieces):
                task.pending = piece
        else:
            tick((), *beside)
        step += 1
    attn_w, time_row = attn_rings[0].result
    time_row = time_row.astype(F32)

    seq_ends = jnp.cumsum(lengths[0])
    positions = jnp.arange(group_rows, dtype=jnp.int32)
    if wires.tensor_size == 2:
        positions = (positions + tensor_index * rows_dev) % group_rows
    segment = jnp.sum((positions[:, None] >= seq_ends[None, :]).astype(jnp.int32), axis=1)

    stream = own_tokens.astype(F32) + time_row
    weights, saved = [], []
    for layer in range(layer_total):
        if layer == 0:
            input_blocks = [(rows.astype(F32) + time_row).astype(BF16) for rows in token_blocks]
        else:
            input_blocks = wires.rows_in(stream.astype(BF16))
            input_blocks[-1] = tick(input_blocks[-1], attn_rings[layer], feed_rings[layer])
            attn_w = attn_rings[layer].finish()
        ahead = (attn_rings[layer + 1], feed_rings[layer + 1])
        biases = []
        for mine in both:
            bias_q, bias_v = [wires.half(b_qv[layer, i], 0, mine) for i in (0, 1)]
            biases.append(jnp.concatenate([bias_q, jnp.zeros_like(bias_q), bias_v]))
        (qkv, mixture, log_total), _ = attend_forward(input_blocks, attn_w[0], biases[0], segment)
        attention = [(qkv, mixture, log_total)]
        part, sums = attend_forward(
            input_blocks, attn_w[1], biases[1], segment, (mixture, attn_w[0])
        )
        attention.append(part)
        sums[-1] = tick(sums[-1], feed_rings[layer])
        attended = tick(wires.rows_out(sums), feed_rings[layer], ahead[0])
        middle = stream + attended + out_bias[layer, 0]
        normed = layer_norm(middle, ln_gain[layer, 0], ln_shift[layer, 0])
        normed_low = normed.astype(BF16)
        tick(normed_low, feed_rings[layer])
        normed_blocks = wires.rows_in(normed_low)
        normed_blocks[-1] = tick(normed_blocks[-1], *ahead)
        feed_w = feed_rings[layer].finish()
        weights.append((attn_w, feed_w))
        bias = jnp.concatenate([wires.half(b_ff1[layer], 0, mine) for mine in both])[None]
        sums, *filled = feed(normed_blocks, feed_w, bias, True)
        if layer == 0:
            sums[-1], cotangent = tie(sums[-1], cotangent)
            upstream = owner_swap(pick(cotangent, back_slot))
        sums[-1] = tick(sums[-1], ahead[0])
        arrived = tick(wires.rows_out(sums), *ahead)
        second_sum = normed + arrived + out_bias[layer, 1]
        saved.append((input_blocks, attention, middle, normed_blocks, filled, second_sum))
        stream = layer_norm(second_sum, ln_gain[layer, 1], ln_shift[layer, 1])

    encoded_own = stream.astype(BF16)
    gradient = upstream.astype(F32)
    feed_tasks, attn_tasks = [None] * (layer_total + 1), [None] * (layer_total + 1)
    attn_sums, reduced, matrices = None, [None] * layer_total, None
    direct = inner % 128 == 0 and hidden % 128 == 0
    vector_grads = [None] * layer_total
    for layer in reversed(range(layer_total)):
        attn_w, feed_w = weights[layer]
        input_blocks, attention, middle, normed_blocks, (act, slope), second_sum = saved[layer]
        _, pull_second = jax.vjp(layer_norm, second_sum, ln_gain[layer, 1], ln_shift[layer, 1])
        grad_second, gain_second, shift_second = pull_second(gradient)
        later_feed, later_attn = feed_tasks[layer + 1], None
        send = tick(grad_second.astype(BF16), later_feed)
        if layer == layer_total - 1:
            send, encoded_own = tie(send, encoded_own)
            returned_out = owner_swap(encoded_own)
        if attn_sums is not None:
            send, *attn_sums = tie(send, *attn_sums)
            later_attn = attn_tasks[layer + 1] = Task(wires.reduce_ring(attn_sums))
        branch_blocks = wires.rows_in(send)
        branch_blocks[-1] = tick(branch_blocks[-1], later_feed, later_attn)
        sums, grad_pre, hidden_sums = feed(branch_blocks, feed_w, slope, False)
        hidden_sums = hidden_sums[0]
        pairs = [(normed_blocks, grad_pre, hidden), (branch_blocks, act, hidden)]
        came = wires.partner(weight_gradients(pairs, 1))
        grad_normed = grad_second + wires.rows_out(sums)
        _, pull_first = jax.vjp(layer_norm, middle, ln_gain[layer, 0], ln_shift[layer, 0])
        grad_middle, gain_first, shift_first = pull_first(grad_normed)
        send, *feed_sums = tie(grad_middle.astype(BF16), weight_gradients(pairs, 0), came)
        feed_tasks[layer] = Task(wires.reduce_ring(feed_sums))
        attend_blocks = wires.rows_in(send)
        attend_blocks[-1] = tick(attend_blocks[-1], feed_tasks[layer], later_attn)

        def attn_pairs(half, wide):
            return [(input_blocks, wide, 3 * inner), (attend_blocks, attention[half][1], inner)]

        wide, part_sums, _ = attend_backward(attend_blocks, attn_w[1], *attention[1], segment)
        send = weight_gradients(attn_pairs(1, wide), 1)
        came = wires.partner(send)
        own_wide, own_sums, sums = attend_backward(
            attend_blocks, attn_w[0], *attention[0], segment, (wide, attn_w[1])
        )
        sums[-1] = tick(sums[-1], feed_tasks[layer], later_attn)
        attn_sums = [weight_gradients(attn_pairs(0, own_wide), 0), came]
        if layer == 0:
            first_portions = wires.first_portions(attn_sums)
        arrived = wires.rows_out(sums)
        if layer + 1 < layer_total:
            reduced[layer + 1] = (later_attn.finish(), later_feed.finish())
            if direct:
                matrices = matrix_outputs(
                    wires.spot, layer + 1, layer_total, *reduced[layer + 1], matrices
                )
                arrived, matrices = tie(arrived, matrices)
        if layer == 0:
            arrived, encoded = tie(arrived, pick(returned_out, deal_slot))
            attn_tasks[0] = Task(wires.reduce_ring(attn_sums, first_portions))
        gradient = grad_middle + arrived
        qkv_sums = [part.reshape(3, inner)[::2] for part in (own_sums, part_sums)]
        vector_grads[layer] = (
            wires.ordered(qkv_sums[0], qkv_sums[1], 1),
            wires.ordered(hidden_sums[:hidden], hidden_sums[hidden:], 0),
            jnp.stack([jnp.sum(grad_middle, axis=0), jnp.sum(grad_second, axis=0)]),
            jnp.stack([gain_first, gain_second]),
            jnp.stack([shift_first, shift_second]),
        )

    returned_grad = owner_swap(gradient.astype(BF16))
    time_grad = jnp.sum(gradient, axis=0)
    local = [jnp.stack([part[i] for part in vector_grads]) for i in range(5)]
    flat = jnp.concatenate([part.reshape(-1) for part in local[:2] + [time_grad] + local[2:]])
    border = local[0].size + local[1].size
    vector_task = Task(wires.butterfly(flat, border))
    vector_task.finish()
    reduced[0] = (attn_tasks[0].finish(), feed_tasks[0].finish())
    flat, shared = vector_task.result
    grad_tokens = pick(returned_grad, deal_slot)
    if direct:
        matrices = matrix_outputs(wires.spot, 0, layer_total, *reduced[0], matrices)
        matrices = [part.transpose(0, 2, 1) if i % 2 else part for i, part in enumerate(matrices)]
    else:
        parts = []
        for attn_pair, feed_pair in reduced:
            rows = attn_pair[0].shape[0]
            qkv = [
                part[:, : 3 * inner].reshape(rows, 3, inner).transpose(1, 0, 2).astype(F32)
                for part in attn_pair
            ]
            parts.append(
                (
                    wires.ordered(*qkv, 2),
                    wires.ordered(*(part[:, 3 * inner :].T.astype(F32) for part in attn_pair), 0),
                    wires.ordered(*(part[:, :hidden].astype(F32) for part in feed_pair), 1),
                    wires.ordered(*(part[:, hidden:].T.astype(F32) for part in feed_pair), 0),
                )
            )
        matrices = [jnp.stack([part[i] for part in parts]) for i in range(4)]
    grad_b_qv = flat[: local[0].size].reshape(local[0].shape)
    grad_b_ff1 = flat[local[0].size : border].reshape(local[1].shape)
    time_grad = shared[:D]
    rest = shared[D:].reshape(3, layer_total, 2, D)
    return (
        encoded,
        grad_tokens,
        time_grad,
        matrices[0],
        grad_b_qv,
        matrices[1],
        rest[0],
        rest[1],
        rest[2],
        matrices[2],
        grad_b_ff1,
        matrices[3],
    )


def solution(mesh):
    return jax.shard_map(
        body,
        mesh=mesh,
        in_specs=(
            P(("dp", "tensor"), None),
            P(("dp", "tensor"), None),
            P(("dp", "tensor")),
            P(("dp", "tensor")),
            P("dp", None),
            P(),
            P(None, "dp"),
            P(None, None, "dp", "tensor"),
            P(None, None, "tensor"),
            P(None, "tensor", "dp"),
            P(),
            P(),
            P(),
            P(None, "dp", "tensor"),
            P(None, "tensor"),
            P(None, "tensor", "dp"),
        ),
        out_specs=(
            P(("dp", "tensor"), None),
            P(("dp", "tensor"), None),
            P(),
            P(None, None, "dp", "tensor"),
            P(None, None, "tensor"),
            P(None, "tensor", "dp"),
            P(),
            P(),
            P(),
            P(None, "dp", "tensor"),
            P(None, "tensor"),
            P(None, "tensor", "dp"),
        ),
        check_vma=False,
    )
```
